128 devices in a mesh: dp: 16 (over z, x), tensor: 8 (over y, core).
Axes of the slice: x: 4, y: 4, z: 4, core: 2. Of those that a mesh axis runs over, the one named last changes fastest.
Arguments:
- activations: bfloat16 [8192, 5120], P('dp', 'tensor'), may hold values from -6 to 6
- out_grad: bfloat16 [8192, 5120], P('dp', 'tensor'), may hold values from -6 to 6
- gate_pre: bfloat16 [8192, 14336], P('dp', 'tensor'), may hold values from -6 to 6
- up_pre: bfloat16 [8192, 14336], P('dp', 'tensor'), may hold values from -6 to 6
- down_weight: bfloat16 [14336, 5120], P(('tensor', 'dp')), may hold values from -0.046875 to 0.046875
- proj_model: bfloat16 [5120, 64], replicated, may hold values from -0.078125 to 0.078125
- proj_hidden: bfloat16 [14336, 64], P('tensor'), may hold values from -0.046875 to 0.046875
- lengths: int32 [64], P('dp'), may hold values from 1 to 128, as said below
Outputs:
- grad_gate: bfloat16 [8192, 14336], P('dp', 'tensor')
- grad_up: bfloat16 [8192, 14336], P('dp', 'tensor')
- features: float32 [64, 3, 4096], P('dp')
The draws below stay inside these ranges and needn't reach their ends.
Inputs may be any that keep to these rules, and one draw needn't show every extreme that they name: In every block of 4 slots of one index of dp the lengths sum to at most 512. In every draw one slot among all 64 has exactly 128 tokens and another exactly 1.
All inputs are finite; a program needn't handle non-finite values.
Results may differ from the reference program's by a relative error of at most 0.003.
Values may be sent and summed in bfloat16 or wider, within the bound.
No kernel may reach another device: no remote copies, remote signals or barrier semaphores. Data moves between devices by JAX's collectives and lax.ppermute only.
A program may use at most 128 MiB of HBM per device.

```python
import jax
import jax.numpy as jnp
from jax import lax

D = 5120
FFW = 14336
RANK = 64
TOK_DEV = 512
E_DEV = 4
TOKENS = 8192
EXAMPLES = 64
N_DP = 16


def draw_lengths(key, part):
    longest = TOK_DEV // E_DEV
    values = jax.random.randint(key, (EXAMPLES,), 1, longest + 1).astype(jnp.int32)
    top_slot = jax.random.randint(jax.random.fold_in(key, 7), (), 0, EXAMPLES).astype(jnp.int32)
    low_slot = (top_slot + 1) % EXAMPLES
    places = jnp.arange(EXAMPLES, dtype=jnp.int32)
    values = jnp.where(places == low_slot, 1, values)
    values = jnp.where(places == top_slot, longest, values)
    return values.astype(jnp.int32)


def block_scale(own_key, shape, shards, smallest, top_value):
    factor_of, own = 1.0, jax.random.fold_in(own_key, 6)
    for dim, blocks in shards:
        draws = jnp.exp(jax.random.uniform(jax.random.fold_in(own, dim), (blocks,), jnp.float32, smallest / len(shards), top_value / len(shards)))
        factor_of = factor_of * jnp.repeat(draws, shape[dim] // blocks).reshape([-1 if axis == dim else 1 for axis in range(len(shape))])
    return factor_of


def bell_draw(own_key, extent, scale, most, cuts=(), kind=jnp.bfloat16):
    array = scale * jax.random.normal(own_key, extent, jnp.float32)
    if cuts:
        array = array * block_scale(own_key, extent, cuts, -0.22, 0.18)
    return jnp.clip(array, -most, most).astype(kind)


def setup_inputs(seed: int = 0) -> dict:
    splits = jax.random.split(jax.random.key(seed), 9)
    activations = bell_draw(splits[0], (TOKENS, D), 1.0, 6.0, ((0, 16), (1, 8)))
    out_grad = bell_draw(splits[1], (TOKENS, D), 1.0, 6.0, ((0, 16), (1, 8)))
    gate_pre = bell_draw(splits[2], (TOKENS, FFW), 1.5, 6.0, ((0, 16), (1, 8)))
    up_pre = bell_draw(splits[3], (TOKENS, FFW), 1.0, 6.0, ((0, 16), (1, 8)))
    down_weight = bell_draw(splits[4], (FFW, D), FFW ** -0.5, 0.046875, ((0, 128),))
    proj_model = bell_draw(splits[5], (D, RANK), D ** -0.5, 0.078125)
    proj_hidden = bell_draw(splits[6], (FFW, RANK), FFW ** -0.5, 0.046875, ((0, 8),))
    lengths = draw_lengths(jax.random.fold_in(splits[8], 71), 0)
    return {"activations": activations, "out_grad": out_grad, "gate_pre": gate_pre, "up_pre": up_pre, "down_weight": down_weight, "proj_model": proj_model, "proj_hidden": proj_hidden, "lengths": lengths}


def block_features(args, down_weight, proj_model, proj_hidden):
    activations, out_grad, gate_pre, up_pre, lengths = args
    offsets = jnp.cumsum(lengths).astype(jnp.int32) - lengths
    rows = jnp.arange(activations.shape[0], dtype=jnp.int32)[:, None]
    member = jnp.logical_and(rows >= offsets[None, :], rows < (offsets + lengths)[None, :]).astype(jnp.float32)
    live = lax.optimization_barrier(jnp.sum(member, axis=1))
    masked = out_grad * live[:, None].astype(jnp.bfloat16)
    hidden_grad = jnp.dot(masked, down_weight.T, preferred_element_type=jnp.float32)
    gate32 = gate_pre.astype(jnp.float32)
    up32 = up_pre.astype(jnp.float32)
    sig = jax.nn.sigmoid(gate32)
    silu = gate32 * sig
    grad_up = (hidden_grad * silu).astype(jnp.bfloat16)
    grad_gate = (hidden_grad * up32 * sig * (1.0 + gate32 * (1.0 - sig))).astype(jnp.bfloat16)
    hidden = (silu * up32).astype(jnp.bfloat16)
    in_proj = jnp.dot(activations, proj_model, preferred_element_type=jnp.float32)
    hidden_proj = jnp.dot(hidden, proj_hidden, preferred_element_type=jnp.float32)
    gate_proj = jnp.dot(grad_gate, proj_hidden, preferred_element_type=jnp.float32)
    up_proj = jnp.dot(grad_up, proj_hidden, preferred_element_type=jnp.float32)
    out_proj = jnp.dot(masked, proj_model, preferred_element_type=jnp.float32)
    weight = member / jnp.sqrt(lengths.astype(jnp.float32))[None, :]

    def pair(left, right):
        mats = jnp.einsum('te,ti,tj->eij', weight, left, right, precision=lax.Precision.HIGHEST)
        return mats.reshape(mats.shape[0], RANK * RANK)
    feats = jnp.stack([pair(in_proj, gate_proj), pair(in_proj, up_proj), pair(hidden_proj, out_proj)], axis=1)
    return (grad_gate, grad_up, feats)

def reference(activations, out_grad, gate_pre, up_pre, down_weight, proj_model, proj_hidden, lengths):
    blocks = (activations.reshape(N_DP, TOK_DEV, D), out_grad.reshape(N_DP, TOK_DEV, D), gate_pre.reshape(N_DP, TOK_DEV, FFW), up_pre.reshape(N_DP, TOK_DEV, FFW), lengths.reshape(N_DP, E_DEV))
    grad_gate, grad_up, feats = lax.map(lambda a: block_features(a, down_weight, proj_model, proj_hidden), blocks)
    return (grad_gate.reshape(TOKENS, FFW), grad_up.reshape(TOKENS, FFW), feats.reshape(EXAMPLES, 3, RANK * RANK))
```

```python
import functools

import jax
import jax.numpy as jnp
from jax import lax
from jax.experimental import pallas as pl
from jax.experimental.pallas import tpu as pltpu
from jax.sharding import Mesh
from jax.sharding import PartitionSpec as P

AXES = ("z", "x", "y", "c")
F32, BF16 = jnp.float32, jnp.bfloat16
ROWS, FEAT, HID, HALF, RANK, DEPTH = 512, 640, 1792, 896, 64, 5120
SHARD, TOP = 112, 64
STEP = 2 * FEAT
NT = (((1,), (1,)), ((), ()))
ANY = pl.BlockSpec(memory_space=pl.ANY)


def send(value, target):
    def line(z, x, y, c):
        return ((z % 4 * 4 + x % 4) * 4 + y % 4) * 2 + c

    pairs = [
        (line(z, x, y, c), line(*target(z, x, y, c)))
        for z in range(4)
        for x in range(4)
        for y in range(4)
        for c in range(2)
    ]
    return lax.ppermute(value, AXES, pairs)


def up_y(v):
    return send(v, lambda z, x, y, c: (z, x, y + 1, c))


def down_y(v):
    return send(v, lambda z, x, y, c: (z, x, y - 1, c))


def swap(v):
    return send(v, lambda z, x, y, c: (z, x, y, 1 - c))


def mate(v):
    return send(v, lambda z, x, y, c: (3 - z, x, y, c))


def gather_weights(own, c):
    def route(v, zero, one):
        hop = {
            "p": lambda z, x, y, c: (z ^ 1, x, y, c),
            "+": lambda z, x, y, c: (z, x + 1, y, c),
            "-": lambda z, x, y, c: (z, x - 1, y, c),
        }
        return send(v, lambda z, x, y, c: hop[zero if c == 0 else one](z, x, y, c))

    def pick(a, b):
        return jnp.where(c == 0, a, b)

    r1 = route(own, "p", "+")
    r2 = route(own, "+", "-")
    r3 = route(own, "-", "p")
    r4 = route(r1, "+", "p")
    r5 = route(pick(r1, r2), "-", "p")
    r6 = route(pick(r2[:TOP], r1[:TOP]), "+", "+")
    r7 = route(pick(r3[TOP:], r2[TOP:]), "-", "-")
    r8 = route(pick(r4[:TOP], r6), "+", "p")
    r9 = route(pick(r5[TOP:], r7), "-", "p")
    return [own, r1, r2, r3, r4, r5, r6, r7, r8, r9]


def weight_rows(z, x, c):
    zl, first = z % 2, c == 0

    def at(dz, dx):
        return ((zl + dz) % 2 * 4 + (x + dx) % 4) * SHARD

    return jnp.stack(
        [
            at(0, 0),
            jnp.where(first, at(1, 0), at(0, 3)),
            jnp.where(first, at(0, 3), at(0, 1)),
            jnp.where(first, at(0, 1), at(1, 0)),
            at(1, 3),
            at(1, 1),
            at(0, 2),
            at(0, 2) + TOP,
            at(1, 2),
            at(1, 2) + TOP,
        ]
    )


def gather_features(own):
    left, right = up_y(own), down_y(own)
    return [own, left, right, up_y(left[:256]), down_y(right[256:])]


WIDTHS = (SHARD,) * 6 + (TOP, SHARD - TOP, TOP, SHARD - TOP)


def product_kernel(first, rows, where_ref, *refs):
    mine, other, weights = refs[:5], refs[5:10], refs[10:20]
    out_ref, a_buf, w_buf, acc, a_sem, w_sem = refs[20:]
    y, c = where_ref[10], where_ref[11]
    a_copies = []
    for group, (pieces, core) in enumerate(((mine, c), (other, 1 - c))):
        lane = pl.multiple_of(core * FEAT, 128)
        for k, piece in enumerate(pieces):
            slot, lo, hi = (k, 0, 512) if k < 3 else (3, (k - 3) * 256, (k - 2) * 256)
            start, stop = max(lo, first), min(hi, first + rows)
            if start >= stop:
                continue
            a_copies.append(
                pltpu.make_async_copy(
                    piece.at[pl.ds(start - lo, stop - start), :],
                    a_buf.at[slot, pl.ds(start - first, stop - start), pl.ds(lane, FEAT)],
                    a_sem.at[group, k],
                )
            )

    def w_copies(step):
        shift = (0, 3, 1, 2)[step]
        lane = pl.multiple_of(lax.rem(y + shift, 4) * STEP, 128)
        return [
            pltpu.make_async_copy(
                w.at[:, pl.ds(lane, STEP)],
                w_buf.at[step % 2, pl.ds(pl.multiple_of(where_ref[k], 16), WIDTHS[k]), :],
                w_sem.at[step % 2, k],
            )
            for k, w in enumerate(weights)
        ]

    for copy in w_copies(0):
        copy.start()
    for copy in a_copies:
        copy.start()
    for copy in a_copies:
        copy.wait()
    for step in range(4):
        if step < 3:
            for copy in w_copies(step + 1):
                copy.start()
        for copy in w_copies(step):
            copy.wait()
        part = lax.dot_general(a_buf[step], w_buf[step % 2], NT, preferred_element_type=F32)
        if step == 0:
            acc[...] = part
        elif step < 3:
            acc[...] += part
        else:
            out_ref[...] = (acc[...] + part).astype(out_ref.dtype)


def product(first, rows, dtype, where, mine, other, weights):
    return pl.pallas_call(
        functools.partial(product_kernel, first, rows),
        out_shape=jax.ShapeDtypeStruct((rows, HALF), dtype),
        grid_spec=pltpu.PrefetchScalarGridSpec(
            num_scalar_prefetch=1,
            grid=(1,),
            in_specs=[ANY] * 20,
            out_specs=pl.BlockSpec((rows, HALF), lambda i, w: (0, 0)),
            scratch_shapes=[
                pltpu.VMEM((4, rows, STEP), BF16),
                pltpu.VMEM((2, HALF, STEP), BF16),
                pltpu.VMEM((rows, HALF), F32),
                pltpu.SemaphoreType.DMA((2, 5)),
                pltpu.SemaphoreType.DMA((2, 10)),
            ],
        ),
        compiler_params=pltpu.CompilerParams(vmem_limit_bytes=32 << 20),
        cost_estimate=pl.CostEstimate(
            flops=2 * rows * HALF * DEPTH,
            bytes_accessed=2 * DEPTH * (rows + HALF) + 4 * rows * HALF,
            transcendentals=0,
        ),
        name="product",
    )(where, *mine, *other, *weights)


def mask_kernel(live_ref, grad_ref, out_ref):
    rows = lax.broadcasted_iota(jnp.int32, (ROWS, FEAT), 0)
    total = live_ref[0] + live_ref[1] + live_ref[2] + live_ref[3]
    grad = grad_ref[...]
    out_ref[...] = jnp.where(rows < total, grad.astype(F32), 0.0).astype(BF16)


def mask_rows(lengths, out_grad):
    return pl.pallas_call(
        mask_kernel,
        out_shape=jax.ShapeDtypeStruct((ROWS, FEAT), BF16),
        grid_spec=pltpu.PrefetchScalarGridSpec(
            num_scalar_prefetch=1,
            grid=(1,),
            in_specs=[pl.BlockSpec((ROWS, FEAT), lambda i, n: (0, 0))],
            out_specs=pl.BlockSpec((ROWS, FEAT), lambda i, n: (0, 0)),
        ),
        name="mask",
    )(lengths, out_grad)


def early_kernel(where_ref, act_ref, masked_ref, pm_ref, gate_ref, up_ref, ph_ref, out_ref):
    j = pl.program_id(0)
    gate, up = gate_ref[...].astype(F32), up_ref[...].astype(F32)
    hidden = (gate * jax.nn.sigmoid(gate) * up).astype(BF16)
    part = lax.dot_general(hidden, ph_ref[...], NT, preferred_element_type=F32)

    @pl.when(j == 0)
    def _():
        pm = pm_ref[...]
        out_ref[:, 0:64] = lax.dot_general(act_ref[...], pm, NT, preferred_element_type=F32)
        out_ref[:, 64:128] = part
        out_ref[:, 128:192] = lax.dot_general(masked_ref[...], pm, NT, preferred_element_type=F32)

    @pl.when(j > 0)
    def _():
        out_ref[:, 64:128] += part


def early(where, activations, masked, pm_t, gate, up, ph_t):
    whole = pl.BlockSpec((ROWS, FEAT), lambda j, w: (0, 0))
    tile = pl.BlockSpec((ROWS, 256), lambda j, w: (0, j))
    return pl.pallas_call(
        early_kernel,
        out_shape=jax.ShapeDtypeStruct((ROWS, 3 * RANK), F32),
        grid_spec=pltpu.PrefetchScalarGridSpec(
            num_scalar_prefetch=1,
            grid=(7,),
            in_specs=[
                whole,
                whole,
                pl.BlockSpec((RANK, FEAT), lambda j, w: (0, 2 * w[10] + w[11])),
                tile,
                tile,
                pl.BlockSpec((RANK, 256), lambda j, w: (0, j)),
            ],
            out_specs=pl.BlockSpec((ROWS, 3 * RANK), lambda j, w: (0, 0)),
        ),
        cost_estimate=pl.CostEstimate(
            flops=ROWS * HID * 160, bytes_accessed=5 << 20, transcendentals=ROWS * HID
        ),
        name="early",
    )(where, activations, masked, pm_t, gate, up, ph_t)


def grads(gate_ref, up_ref, hidden_grad):
    gate, up = gate_ref[...].astype(F32), up_ref[...].astype(F32)
    sig = jax.nn.sigmoid(gate)
    grad_up = (hidden_grad * (gate * sig)).astype(BF16)
    grad_gate = (hidden_grad * up * sig * (1.0 + gate * (1.0 - sig))).astype(BF16)
    return grad_gate, grad_up


def own_kernel(where_ref, gate_ref, up_ref, h_ref, ph_ref, gg_ref, gu_ref, part_ref):
    grad_gate, grad_up = grads(gate_ref, up_ref, h_ref[...])
    gg_ref[...] = grad_gate
    gu_ref[...] = grad_up
    ph = ph_ref[...]
    part = jnp.concatenate(
        [
            lax.dot_general(g, ph, NT, preferred_element_type=F32)
            for g in (grad_gate, grad_up)
        ],
        axis=1,
    )
    j = pl.program_id(0)

    @pl.when(j == 0)
    def _():
        part_ref[...] = part

    @pl.when(j > 0)
    def _():
        part_ref[...] += part


def own_half(where, gate, up, h, ph_t):
    tile = pl.BlockSpec((ROWS, 128), lambda j, w: (0, 7 * w[12] + j))
    big = jax.ShapeDtypeStruct((ROWS, HID), BF16)
    return pl.pallas_call(
        own_kernel,
        out_shape=(big, big, jax.ShapeDtypeStruct((ROWS, 2 * RANK), F32)),
        grid_spec=pltpu.PrefetchScalarGridSpec(
            num_scalar_prefetch=1,
            grid=(7,),
            in_specs=[
                tile,
                tile,
                pl.BlockSpec((ROWS, 128), lambda j, w: (0, j)),
                pl.BlockSpec((RANK, 128), lambda j, w: (0, 7 * w[12] + j)),
            ],
            out_specs=(tile, tile, pl.BlockSpec((ROWS, 2 * RANK), lambda j, w: (0, 0))),
        ),
        cost_estimate=pl.CostEstimate(
            flops=ROWS * HALF * 280, bytes_accessed=6 << 20, transcendentals=ROWS * HALF
        ),
        name="own_half",
    )(where, gate, up, h, ph_t)


def other_kernel(where_ref, gate_ref, up_ref, h_ref, ph_ref, part_ref, w_ref, in_ref,
                 gg_in, gu_in, before_ref, gg_ref, gu_ref, feat_ref, acc):
    grad_gate, grad_up = grads(gate_ref, up_ref, h_ref[...].astype(F32))
    gg_ref[...] = grad_gate
    gu_ref[...] = grad_up
    ph = ph_ref[...]
    part = jnp.concatenate(
        [
            lax.dot_general(g, ph, NT, preferred_element_type=F32)
            for g in (grad_gate, grad_up)
        ],
        axis=1,
    )
    j = pl.program_id(0)

    @pl.when(j == 0)
    def _():
        acc[...] = part_ref[...] + part

    @pl.when(j > 0)
    def _():
        acc[...] += part

    @pl.when(j == 6)
    def _():
        weight = w_ref[...]
        left = in_ref[...]
        spread = jnp.concatenate([left * weight[:, s : s + 1] for s in range(4)], axis=1)
        feat_ref[...] = before_ref[...] + lax.dot_general(
            spread,
            acc[...],
            (((0,), (0,)), ((), ())),
            precision=lax.Precision.HIGHEST,
            preferred_element_type=F32,
        )


def other_half(k, rows, where, gate, up, h, ph_t, part, weight, in_proj, gg, gu, before):
    tile = pl.BlockSpec((rows, 128), lambda j, w: (k, 7 * (1 - w[12]) + j))
    big = jax.ShapeDtypeStruct((ROWS, HID), BF16)
    feat = pl.BlockSpec((4 * RANK, 2 * RANK), lambda j, w: (0, 0))
    return pl.pallas_call(
        other_kernel,
        out_shape=(big, big, jax.ShapeDtypeStruct((4 * RANK, 2 * RANK), F32)),
        grid_spec=pltpu.PrefetchScalarGridSpec(
            num_scalar_prefetch=1,
            grid=(7,),
            in_specs=[
                tile,
                tile,
                pl.BlockSpec((rows, 128), lambda j, w: (0, j)),
                pl.BlockSpec((RANK, 128), lambda j, w: (0, 7 * (1 - w[12]) + j)),
                pl.BlockSpec((rows, 2 * RANK), lambda j, w: (k, 0)),
                pl.BlockSpec((rows, 4), lambda j, w: (k, 0)),
                pl.BlockSpec((rows, RANK), lambda j, w: (k, 0)),
                ANY,
                ANY,
                feat,
            ],
            out_specs=(tile, tile, feat),
            scratch_shapes=[pltpu.VMEM((rows, 2 * RANK), F32)],
        ),
        input_output_aliases={8: 0, 9: 1},
        cost_estimate=pl.CostEstimate(
            flops=rows * HALF * 280, bytes_accessed=3 << 20, transcendentals=rows * HALF
        ),
        name="other_half",
    )(where, gate, up, h, ph_t, part, weight, in_proj, gg, gu, before)


def sum_tensor(value, c):
    half = value.shape[0] // 2
    top, low = value[:half], value[half:]
    mine = jnp.where(c == 0, top, low) + swap(jnp.where(c == 0, low, top))
    across = send(mine, lambda z, x, y, c: (z, x, y + 2, c))
    mine = (mine + across) + (up_y(mine) + down_y(mine))
    theirs = swap(mine)
    return jnp.concatenate(
        [jnp.where(c == 0, mine, theirs), jnp.where(c == 0, theirs, mine)], axis=0
    )


def on_device(
    activations, out_grad, gate_pre, up_pre, down_weight, proj_model, proj_hidden, lengths
):
    z, x, y, c = (lax.axis_index(a) for a in AXES)
    where = jnp.concatenate(
        [weight_rows(z, x, c), jnp.stack([y, c, z // 2])]
    ).astype(jnp.int32)
    weights = gather_weights(down_weight, c)
    masked = mask_rows(lengths, out_grad)
    theirs = mate(masked)
    a_mine = gather_features(masked)
    b_mine = gather_features(theirs)
    a_other = [swap(v) for v in a_mine]
    b_other = [swap(v) for v in b_mine]

    pm_t, ph_t = proj_model.T, proj_hidden.T
    parts = early(where, activations, masked, pm_t, gate_pre, up_pre, ph_t)
    mixed = lax.all_to_all(parts.reshape(8, 64, 3 * RANK), ("y", "c"), 0, 0)
    slice_proj = jnp.sum(mixed, axis=0)
    in_proj = lax.all_gather(slice_proj[:, :RANK], ("y", "c"), axis=0, tiled=True)

    offsets = jnp.cumsum(lengths) - lengths
    rows = jnp.arange(ROWS, dtype=jnp.int32)[:, None]
    member = jnp.logical_and(rows >= offsets[None, :], rows < (offsets + lengths)[None, :])
    weight = member.astype(F32) / jnp.sqrt(lengths.astype(F32))[None, :]
    slice_weight = lax.dynamic_slice(weight, ((2 * y + c) * 64, 0), (64, 4))
    spread = slice_weight[:, :, None] * slice_proj[:, None, RANK : 2 * RANK]
    down_feat = lax.dot_general(
        spread.reshape(64, 4 * RANK),
        slice_proj[:, 2 * RANK :],
        (((0,), (0,)), ((), ())),
        precision=lax.Precision.HIGHEST,
        preferred_element_type=F32,
    )

    h_out = [product(k * 256, 256, BF16, where, b_mine, b_other, weights) for k in range(2)]
    h_in = [mate(h) for h in h_out]
    h_own = product(0, 512, F32, where, a_mine, a_other, weights)
    grad_gate, grad_up, part = own_half(where, gate_pre, up_pre, h_own, ph_t)
    feat = jnp.zeros((4 * RANK, 2 * RANK), F32)
    for k in range(2):
        grad_gate, grad_up, feat = other_half(
            k, 256, where, gate_pre, up_pre, h_in[k], ph_t, part, weight, in_proj,
            grad_gate, grad_up, feat,
        )
    total = sum_tensor(jnp.concatenate([feat, down_feat], axis=1), c)
    features = total.reshape(4, RANK, 3, RANK).transpose(0, 2, 1, 3).reshape(4, 3, RANK * RANK)
    return grad_gate, grad_up, features


def solution(mesh):
    split = Mesh(mesh.devices.reshape(4, 4, 4, 2), AXES)
    dp, tensor = ("z", "x"), ("y", "c")
    return jax.shard_map(
        on_device,
        mesh=split,
        in_specs=(
            P(dp, tensor),
            P(dp, tensor),
            P(dp, tensor),
            P(dp, tensor),
            P((*tensor, *dp), None),
            P(),
            P(tensor, None),
            P(dp),
        ),
        out_specs=(P(dp, tensor), P(dp, tensor), P(dp, None, None)),
        check_vma=False,
    )
```

```python
import functools

import jax
import jax.numpy as jnp
from jax import lax
from jax.experimental import pallas as pl
from jax.experimental.pallas import tpu as pltpu
from jax.sharding import Mesh
from jax.sharding import PartitionSpec as P

AXES = ("z", "x", "y", "c")
F32, BF16 = jnp.float32, jnp.bfloat16
ROWS, FEAT, HID, HALF, RANK, DEPTH = 512, 640, 1792, 896, 64, 5120
SHARD, TOP = 112, 64
STEP = 2 * FEAT
NT = (((1,), (1,)), ((), ()))
ANY = pl.BlockSpec(memory_space=pl.ANY)


def send(value, target, name="send"):
    def line(z, x, y, c):
        return ((z % 4 * 4 + x % 4) * 4 + y % 4) * 2 + c

    pairs = [
        (line(z, x, y, c), line(*target(z, x, y, c)))
        for z in range(4)
        for x in range(4)
        for y in range(4)
        for c in range(2)
    ]
    with jax.named_scope(name):
        return lax.ppermute(value, AXES, pairs)


def up_y(v, name="up"):
    return send(v, lambda z, x, y, c: (z, x, y + 1, c), name)


def down_y(v, name="down"):
    return send(v, lambda z, x, y, c: (z, x, y - 1, c), name)


def swap(v, name="swap"):
    return send(v, lambda z, x, y, c: (z, x, y, 1 - c), name)


def mate(v, name="mate"):
    return send(v, lambda z, x, y, c: (3 - z, x, y, c), name)


def after(value, *others):
    return lax.optimization_barrier((value, *others))[0]


def pick(c, a, b):
    return jnp.where(c == 0, a, b)


def route(v, zero, one, name):
    hop = {
        "p": lambda z, x, y, c: (z ^ 1, x, y, c),
        "+": lambda z, x, y, c: (z, x + 1, y, c),
        "-": lambda z, x, y, c: (z, x - 1, y, c),
    }
    return send(v, lambda z, x, y, c: hop[zero if c == 0 else one](z, x, y, c), name)


def weight_rows(z, x, c):
    zl, first = z % 2, c == 0

    def at(dz, dx):
        return ((zl + dz) % 2 * 4 + (x + dx) % 4) * SHARD

    return jnp.stack(
        [
            at(0, 0),
            jnp.where(first, at(1, 0), at(0, 3)),
            jnp.where(first, at(0, 3), at(0, 1)),
            jnp.where(first, at(0, 1), at(1, 0)),
            at(1, 3),
            at(1, 1),
            at(0, 2),
            at(0, 2) + TOP,
            at(1, 2),
            at(1, 2) + TOP,
        ]
    )


WIDTHS = (SHARD,) * 6 + (TOP, SHARD - TOP, TOP, SHARD - TOP)


def product_kernel(first, rows, others, where_ref, *refs):
    mine, weights, other = refs[:5], refs[5:15], refs[15 : 15 + others]
    out_ref, a_buf, w_buf, a_sem, w_sem, *acc = refs[15 + others :]
    acc = acc[0] if acc else out_ref
    y, c = where_ref[10], where_ref[11]
    a_copies = []
    lane, swapped = (pl.multiple_of(core * FEAT, 128) for core in (c, 1 - c))
    for k, piece in enumerate(mine):
        slot, lo, hi = (k, 0, 512) if k < 3 else (3, (k - 3) * 256, (k - 2) * 256)
        start, stop = max(lo, first), min(hi, first + rows)
        if start < stop:
            a_copies.append(
                pltpu.make_async_copy(
                    piece.at[pl.ds(start - lo, stop - start), :],
                    a_buf.at[slot, pl.ds(start - first, stop - start), pl.ds(lane, FEAT)],
                    a_sem.at[0, k],
                )
            )
    for slot in range(4):
        ref, at = (other[0], slot * 512) if others == 1 or slot < 3 else (other[1], 0)
        a_copies.append(
            pltpu.make_async_copy(
                ref.at[pl.ds(at + first, rows), :],
                a_buf.at[slot, :, pl.ds(swapped, FEAT)],
                a_sem.at[1, slot],
            )
        )

    def w_copies(step):
        shift = (0, 3, 1, 2)[step]
        lane = pl.multiple_of(lax.rem(y + shift, 4) * STEP, 128)
        return [
            pltpu.make_async_copy(
                w.at[:, pl.ds(lane, STEP)],
                w_buf.at[step % 2, pl.ds(pl.multiple_of(where_ref[k], 16), WIDTHS[k]), :],
                w_sem.at[step % 2, k],
            )
            for k, w in enumerate(weights)
        ]

    for copy in w_copies(0):
        copy.start()
    for copy in a_copies:
        copy.start()
    for copy in a_copies:
        copy.wait()
    for step in range(4):
        if step < 3:
            for copy in w_copies(step + 1):
                copy.start()
        for copy in w_copies(step):
            copy.wait()
        part = lax.dot_general(a_buf[step], w_buf[step % 2], NT, preferred_element_type=F32)
        if step == 0:
            acc[...] = part
        elif step < 3:
            acc[...] += part
        else:
            out_ref[...] = (acc[...] + part).astype(out_ref.dtype)


def product(first, rows, dtype, where, mine, other, weights):
    return pl.pallas_call(
        functools.partial(product_kernel, first, rows, len(other)),
        out_shape=jax.ShapeDtypeStruct((rows, HALF), dtype),
        grid_spec=pltpu.PrefetchScalarGridSpec(
            num_scalar_prefetch=1,
            grid=(1,),
            in_specs=[ANY] * (15 + len(other)),
            out_specs=pl.BlockSpec((rows, HALF), lambda i, w: (0, 0)),
            scratch_shapes=[
                pltpu.VMEM((4, rows, STEP), BF16),
                pltpu.VMEM((2, HALF, STEP), BF16),
                pltpu.SemaphoreType.DMA((2, 5)),
                pltpu.SemaphoreType.DMA((2, 10)),
            ]
            + ([] if dtype == F32 else [pltpu.VMEM((rows, HALF), F32)]),
        ),
        compiler_params=pltpu.CompilerParams(vmem_limit_bytes=(11 if rows == 256 else 18) << 20),
        cost_estimate=pl.CostEstimate(
            flops=2 * rows * HALF * DEPTH,
            bytes_accessed=2 * DEPTH * (rows + HALF) + 4 * rows * HALF,
            transcendentals=0,
        ),
        name="product",
    )(where, *mine, *weights, *other)


def early_kernel(where_ref, act_ref, grad_ref, pm_ref, gate_ref, up_ref, ph_ref, out_ref):
    gate, up = gate_ref[...].astype(F32), up_ref[...].astype(F32)
    hidden = (gate * jax.nn.sigmoid(gate) * up).astype(BF16)
    pm = pm_ref[...]
    out_ref[:, 0:64] = lax.dot_general(act_ref[...], pm, NT, preferred_element_type=F32)
    out_ref[:, 64:128] = lax.dot_general(hidden, ph_ref[...], NT, preferred_element_type=F32)
    out_ref[:, 128:192] = lax.dot_general(grad_ref[...], pm, NT, preferred_element_type=F32)


def early(where, activations, out_grad, pm_t, gate, up, ph_t):
    narrow = pl.BlockSpec((128, FEAT), lambda i, w: (i, 0))
    wide = pl.BlockSpec((128, HID), lambda i, w: (i, 0))
    return pl.pallas_call(
        early_kernel,
        out_shape=jax.ShapeDtypeStruct((ROWS, 3 * RANK), F32),
        grid_spec=pltpu.PrefetchScalarGridSpec(
            num_scalar_prefetch=1,
            grid=(4,),
            in_specs=[
                narrow,
                narrow,
                pl.BlockSpec((RANK, FEAT), lambda i, w: (0, 2 * w[10] + w[11])),
                wide,
                wide,
                pl.BlockSpec((RANK, HID), lambda i, w: (0, 0)),
            ],
            out_specs=pl.BlockSpec((128, 3 * RANK), lambda i, w: (i, 0)),
        ),
        compiler_params=pltpu.CompilerParams(vmem_limit_bytes=12 << 20),
        cost_estimate=pl.CostEstimate(
            flops=ROWS * HID * 160, bytes_accessed=5 << 20, transcendentals=ROWS * HID
        ),
        name="early",
    )(where, activations, out_grad, pm_t, gate, up, ph_t)


def grads(gate_ref, up_ref, hidden_grad, ph_ref, first, total, gg_ref, gu_ref):
    row = first + lax.broadcasted_iota(jnp.int32, hidden_grad.shape, 0)
    hidden_grad = jnp.where(row < total, hidden_grad, 0.0)
    gate, up = gate_ref[...].astype(F32), up_ref[...].astype(F32)
    sig = jax.nn.sigmoid(gate)
    grad_up = (hidden_grad * (gate * sig)).astype(BF16)
    grad_gate = (hidden_grad * up * sig * (1.0 + gate * (1.0 - sig))).astype(BF16)
    gg_ref[...] = grad_gate
    gu_ref[...] = grad_up
    ph = ph_ref[...]
    return jnp.concatenate(
        [
            lax.dot_general(g, ph, NT, preferred_element_type=F32)
            for g in (grad_gate, grad_up)
        ],
        axis=1,
    )


def own_kernel(where_ref, gate_ref, up_ref, h_ref, ph_ref, gg_ref, gu_ref, part_ref):
    part_ref[...] = grads(
        gate_ref, up_ref, h_ref[...], ph_ref, pl.program_id(0) * 64, where_ref[13], gg_ref, gu_ref
    )


def own_half(where, gate, up, h, ph_t):
    tile = pl.BlockSpec((64, HALF), lambda i, w: (i, w[12]))
    big = jax.ShapeDtypeStruct((ROWS, HID), BF16)
    return pl.pallas_call(
        own_kernel,
        out_shape=(big, big, jax.ShapeDtypeStruct((ROWS, 2 * RANK), F32)),
        grid_spec=pltpu.PrefetchScalarGridSpec(
            num_scalar_prefetch=1,
            grid=(8,),
            in_specs=[
                tile,
                tile,
                pl.BlockSpec((64, HALF), lambda i, w: (i, 0)),
                pl.BlockSpec((RANK, HALF), lambda i, w: (0, w[12])),
            ],
            out_specs=(tile, tile, pl.BlockSpec((64, 2 * RANK), lambda i, w: (i, 0))),
        ),
        compiler_params=pltpu.CompilerParams(vmem_limit_bytes=8 << 20),
        cost_estimate=pl.CostEstimate(
            flops=ROWS * HALF * 280, bytes_accessed=6 << 20, transcendentals=ROWS * HALF
        ),
        name="own_half",
    )(where, gate, up, h, ph_t)


def other_kernel(k, where_ref, gate_ref, up_ref, h_ref, ph_ref, part_ref, hi_ref, lo_ref,
                 gg_in, gu_in, *refs):
    gg_ref, gu_ref, feat_ref, acc = refs[-4:]
    i = pl.program_id(0)
    part = grads(
        gate_ref, up_ref, h_ref[...].astype(F32), ph_ref, k * 256 + i * 64, where_ref[13],
        gg_ref, gu_ref,
    )
    acc[pl.ds(pl.multiple_of(i * 64, 64), 64), :] = part_ref[...] + part

    @pl.when(i == 3)
    def _():
        whole = acc[...]
        hi = whole.astype(BF16)
        lo = (whole - hi.astype(F32)).astype(BF16)
        feat = jnp.dot(lo_ref[...], hi, preferred_element_type=F32)
        feat += jnp.dot(hi_ref[...], lo, preferred_element_type=F32)
        feat += jnp.dot(hi_ref[...], hi, preferred_element_type=F32)
        feat_ref[...] = feat if k == 0 else refs[0][...] + feat


def other_half(k, where, gate, up, h, ph_t, part, spread, gg, gu, before):
    tile = pl.BlockSpec((64, HALF), lambda i, w: (4 * k + i, 1 - w[12]))
    big = jax.ShapeDtypeStruct((ROWS, HID), BF16)
    feat = pl.BlockSpec((4 * RANK, 2 * RANK), lambda i, w: (0, 0))
    columns = pl.BlockSpec((4 * RANK, 256), lambda i, w: (0, k))
    return pl.pallas_call(
        functools.partial(other_kernel, k),
        out_shape=(big, big, jax.ShapeDtypeStruct((4 * RANK, 2 * RANK), F32)),
        grid_spec=pltpu.PrefetchScalarGridSpec(
            num_scalar_prefetch=1,
            grid=(4,),
            in_specs=[
                tile,
                tile,
                pl.BlockSpec((64, HALF), lambda i, w: (i, 0)),
                pl.BlockSpec((RANK, HALF), lambda i, w: (0, 1 - w[12])),
                pl.BlockSpec((64, 2 * RANK), lambda i, w: (4 * k + i, 0)),
                columns,
                columns,
                ANY,
                ANY,
            ]
            + [feat] * len(before),
            out_specs=(tile, tile, feat),
            scratch_shapes=[pltpu.VMEM((256, 2 * RANK), F32)],
        ),
        input_output_aliases={8: 0, 9: 1},
        compiler_params=pltpu.CompilerParams(vmem_limit_bytes=8 << 20),
        cost_estimate=pl.CostEstimate(
            flops=256 * HALF * 280, bytes_accessed=3 << 20, transcendentals=256 * HALF
        ),
        name="other_half",
    )(where, gate, up, h, ph_t, part, *spread, gg, gu, *before)


def sum_tensor(value, c):
    half = value.shape[0] // 2
    top, low = value[:half], value[half:]
    mine = jnp.where(c == 0, top, low) + swap(jnp.where(c == 0, low, top))
    across = send(mine, lambda z, x, y, c: (z, x, y + 2, c))
    mine = (mine + across) + (up_y(mine) + down_y(mine))
    theirs = swap(mine)
    return jnp.concatenate(
        [jnp.where(c == 0, mine, theirs), jnp.where(c == 0, theirs, mine)], axis=0
    )


def on_device(
    activations, out_grad, gate_pre, up_pre, down_weight, proj_model, proj_hidden, lengths
):
    z, x, y, c = (lax.axis_index(a) for a in AXES)
    where = jnp.concatenate(
        [weight_rows(z, x, c), jnp.stack([y, c, z // 2, jnp.sum(lengths)])]
    ).astype(jnp.int32)
    own_w = down_weight
    r1 = route(own_w, "p", "+", "r1")
    r2 = route(own_w, "+", "-", "r2")
    theirs = mate(out_grad, "mate_rows")
    a_up, a_down = up_y(out_grad, "a_up"), down_y(out_grad, "a_down")
    r3 = route(after(own_w, theirs, a_up, a_down), "-", "p", "r3")
    a_far1, a_far2 = up_y(a_up[:256], "a_far1"), down_y(a_down[256:], "a_far2")
    r1, r2, r3, theirs, a_far1, a_far2 = lax.optimization_barrier(
        (r1, r2, r3, theirs, a_far1, a_far2)
    )
    r4 = route(r1, "+", "p", "r4")
    r5 = route(pick(c, r1, r2), "-", "p", "r5")
    r6 = route(pick(c, r2[:TOP], r1[:TOP]), "+", "+", "r6")
    b_up, b_down = up_y(theirs, "b_up"), down_y(theirs, "b_down")
    r7 = route(after(pick(c, r3[TOP:], r2[TOP:]), b_up), "-", "-", "r7")
    a_other = [swap(jnp.concatenate([out_grad, a_up, a_down, a_far1, a_far2]), "a_swap")]
    near1, near2, r5, a_other = lax.optimization_barrier(
        (b_up[:256], b_down[256:], r5, a_other)
    )
    b_near = swap(jnp.concatenate([theirs, b_up, b_down]), "b_near_swap")
    b_far1, b_far2 = up_y(near1, "b_far1"), down_y(near2, "b_far2")
    r8 = route(pick(c, r4[:TOP], r6), "+", "p", "r8")
    r9 = route(pick(c, r5[TOP:], r7), "-", "p", "r9")
    weights = [own_w, r1, r2, r3, r4, r5, r6, r7, r8, r9]
    a_mine = [out_grad, a_up, a_down, a_far1, a_far2]
    b_mine = [theirs, b_up, b_down, b_far1, b_far2]
    b_other = [b_near, swap(jnp.concatenate([b_far1, b_far2]), "b_far_swap")]

    pm_t, ph_t = proj_model.T, proj_hidden.T
    parts = early(after(where, b_up), activations, out_grad, pm_t, gate_pre, up_pre, ph_t)
    sums = sum_tensor(after(parts, b_far1, b_far2, r7), c)
    in_proj, hidden_proj, out_proj = (sums[:, i * RANK : (i + 1) * RANK] for i in range(3))

    offsets = jnp.cumsum(lengths) - lengths
    rows = jnp.arange(ROWS, dtype=jnp.int32)[:, None]
    member = jnp.logical_and(rows >= offsets[None, :], rows < (offsets + lengths)[None, :])
    weight = member.astype(F32) / jnp.sqrt(lengths.astype(F32))[None, :]

    def weighted(left):
        return (weight[:, :, None] * left[:, None, :]).reshape(ROWS, 4 * RANK)

    spread = weighted(in_proj).T
    spread_hi = spread.astype(BF16)
    spread_lo = (spread - spread_hi.astype(F32)).astype(BF16)
    down_feat = lax.dot_general(
        weighted(hidden_proj),
        out_proj,
        (((0,), (0,)), ((), ())),
        precision=lax.Precision.HIGHEST,
        preferred_element_type=F32,
    )

    h_out = [product(k * 256, 256, BF16, where, b_mine, b_other, weights) for k in range(2)]
    h_in = [mate(h, "mate_grad") for h in h_out]
    h_own = product(0, 512, F32, after(where, *h_out), a_mine, a_other, weights)
    grad_gate, grad_up, part = own_half(where, gate_pre, up_pre, h_own, ph_t)
    feat = ()
    for k in range(2):
        grad_gate, grad_up, *feat = other_half(
            k, where, gate_pre, up_pre, h_in[k], ph_t, part, (spread_hi, spread_lo),
            grad_gate, grad_up, feat,
        )
    total = jnp.concatenate([sum_tensor(feat[0], c), down_feat], axis=1)
    features = total.reshape(4, RANK, 3, RANK).transpose(0, 2, 1, 3).reshape(4, 3, RANK * RANK)
    return grad_gate, grad_up, features


def solution(mesh):
    split = Mesh(mesh.devices.reshape(4, 4, 4, 2), AXES)
    dp, tensor = ("z", "x"), ("y", "c")
    return jax.shard_map(
        on_device,
        mesh=split,
        in_specs=(
            P(dp, tensor),
            P(dp, tensor),
            P(dp, tensor),
            P(dp, tensor),
            P((*tensor, *dp), None),
            P(),
            P(tensor, None),
            P(dp),
        ),
        out_specs=(P(dp, tensor), P(dp, tensor), P(dp, None, None)),
        check_vma=False,
    )
```

```python
import functools

import jax
import jax.numpy as jnp
from jax import lax
from jax.experimental import pallas as pl
from jax.experimental.pallas import tpu as pltpu
from jax.sharding import Mesh
from jax.sharding import PartitionSpec as P

AXES = ("z", "x", "y", "c")
F32, BF16 = jnp.float32, jnp.bfloat16
ROWS, FEAT, HID, HALF, RANK, DEPTH = 512, 640, 1792, 896, 64, 5120
SHARD = 112
STEP = 2 * FEAT
NT = (((1,), (1,)), ((), ()))
ANY = pl.BlockSpec(memory_space=pl.ANY)


def send(value, target, name="send"):
    def line(z, x, y, c):
        return ((z % 4 * 4 + x % 4) * 4 + y % 4) * 2 + c

    pairs = [
        (line(z, x, y, c), line(*target(z, x, y, c)))
        for z in range(4)
        for x in range(4)
        for y in range(4)
        for c in range(2)
    ]
    with jax.named_scope(name):
        return lax.ppermute(value, AXES, pairs)


def up_y(v, name="up"):
    return send(v, lambda z, x, y, c: (z, x, y + 1, c), name)


def down_y(v, name="down"):
    return send(v, lambda z, x, y, c: (z, x, y - 1, c), name)


def along_y(v, way, name):
    return send(v, lambda z, x, y, c: (z, x, y + way * (1 - 2 * c), c), name)


def swap(v, name="swap"):
    return send(v, lambda z, x, y, c: (z, x, y, 1 - c), name)


def mate(v, name="mate"):
    return send(v, lambda z, x, y, c: (3 - z, x, y, c), name)


def after(value, *others):
    return lax.optimization_barrier((value, *others))[0]


def pick(c, a, b):
    return jnp.where(c == 0, a, b)


def route(v, zero, one, name):
    hop = {
        "p": lambda z, x, y, c: (z ^ 1, x, y, c),
        "+": lambda z, x, y, c: (z, x + 1, y, c),
        "-": lambda z, x, y, c: (z, x - 1, y, c),
    }
    return send(v, lambda z, x, y, c: hop[zero if c == 0 else one](z, x, y, c), name)


def slots(z, x, c):
    zl, first = z % 2, c == 0

    def at(dz, dx):
        return (zl + dz) % 2 * 4 + (x + dx) % 4

    held = jnp.stack(
        [
            at(0, 0),
            jnp.where(first, at(1, 0), at(0, 3)),
            jnp.where(first, at(0, 3), at(0, 1)),
            jnp.where(first, at(0, 1), at(1, 0)),
            at(1, 3),
            at(1, 1),
            at(0, 2),
            at(1, 2),
        ]
    )
    shard = jnp.arange(8)
    return jnp.sum(jnp.where(held[None, :] == shard[:, None], shard[None, :], 0), axis=1)


def product_kernel(shards, where_ref, *refs):
    mine, other, weights = refs[:4], refs[4:8], refs[8 : 8 + shards]
    out_ref, a_buf, w_buf, a_sem, w_sem, *acc = refs[8 + shards :]
    acc = acc[0] if acc else out_ref
    y, c = where_ref[16], where_ref[17]
    a_copies = []
    for group, (pieces, core) in enumerate(((mine, c), (other, 1 - c))):
        lane = pl.multiple_of(core * FEAT, 128)
        for k in range(4):
            a_copies.append(
                pltpu.make_async_copy(
                    pieces[k], a_buf.at[k, :, pl.ds(lane, FEAT)], a_sem.at[group, k]
                )
            )

    def w_copies(step):
        shift = (0, 3 - 2 * c, 1 + 2 * c, 2)[step]
        lane = pl.multiple_of(lax.rem(y + shift, 4) * STEP, 128)
        return [
            pltpu.make_async_copy(
                w.at[:, pl.ds(lane, STEP)],
                w_buf.at[step % 2, pl.ds(k * 128, SHARD), :],
                w_sem.at[step % 2, k],
            )
            for k, w in enumerate(weights)
        ]

    for copy in w_copies(0):
        copy.start()
    for copy in a_copies:
        copy.start()
    for half in range(2):
        for k in range(shards):
            w_buf[half, k * 128 + SHARD : k * 128 + 128, :] = jnp.zeros((128 - SHARD, STEP), BF16)
    for step in range(4):
        if step < 3:
            for copy in w_copies(step + 1):
                copy.start()
        a_copies[step].wait()
        a_copies[4 + step].wait()
        for copy in w_copies(step):
            copy.wait()
        part = lax.dot_general(a_buf[step], w_buf[step % 2], NT, preferred_element_type=F32)
        if step == 0:
            acc[...] = part
        elif step < 3:
            acc[...] += part
        else:
            out_ref[...] = (acc[...] + part).astype(out_ref.dtype)


def product(dtype, where, mine, other, weights):
    shards = len(weights)
    width = shards * 128
    vmem = pl.BlockSpec(memory_space=pltpu.VMEM)
    return pl.pallas_call(
        functools.partial(product_kernel, shards),
        out_shape=jax.ShapeDtypeStruct((ROWS, width), dtype),
        in_specs=[pl.BlockSpec(memory_space=pltpu.SMEM)] + [vmem] * (8 + shards),
        out_specs=vmem,
        scratch_shapes=[
            pltpu.VMEM((4, ROWS, STEP), BF16),
            pltpu.VMEM((2, width, STEP), BF16),
            pltpu.SemaphoreType.DMA((2, 4)),
            pltpu.SemaphoreType.DMA((2, shards)),
        ]
        + ([] if dtype == F32 else [pltpu.VMEM((ROWS, width), F32)]),
        compiler_params=pltpu.CompilerParams(
            vmem_limit_bytes=(8 << 20) + width * (4 * STEP + 14 * ROWS)
        ),
        cost_estimate=pl.CostEstimate(
            flops=2 * ROWS * width * DEPTH,
            bytes_accessed=2 * DEPTH * (ROWS + width) + 4 * ROWS * width,
            transcendentals=0,
        ),
        name="product",
    )(where, *mine, *other, *weights)


def early_kernel(where_ref, act_ref, grad_ref, pm_ref, gate_ref, up_ref, ph_ref, out_ref):
    gate, up = gate_ref[...].astype(F32), up_ref[...].astype(F32)
    hidden = (gate * jax.nn.sigmoid(gate) * up).astype(BF16)
    pm = pm_ref[...]
    out_ref[:, 0:64] = lax.dot_general(act_ref[...], pm, NT, preferred_element_type=F32)
    out_ref[:, 64:128] = lax.dot_general(hidden, ph_ref[...], NT, preferred_element_type=F32)
    out_ref[:, 128:192] = lax.dot_general(grad_ref[...], pm, NT, preferred_element_type=F32)


def early(where, activations, out_grad, pm_t, gate, up, ph_t):
    narrow = pl.BlockSpec((128, FEAT), lambda i, w: (i, 0))
    wide = pl.BlockSpec((128, HID), lambda i, w: (i, 0))
    return pl.pallas_call(
        early_kernel,
        out_shape=jax.ShapeDtypeStruct((ROWS, 3 * RANK), F32),
        grid_spec=pltpu.PrefetchScalarGridSpec(
            num_scalar_prefetch=1,
            grid=(4,),
            in_specs=[
                narrow,
                narrow,
                pl.BlockSpec((RANK, FEAT), lambda i, w: (0, 2 * w[16] + w[17])),
                wide,
                wide,
                pl.BlockSpec((RANK, HID), lambda i, w: (0, 0)),
            ],
            out_specs=pl.BlockSpec((128, 3 * RANK), lambda i, w: (i, 0)),
        ),
        compiler_params=pltpu.CompilerParams(vmem_limit_bytes=12 << 20),
        cost_estimate=pl.CostEstimate(
            flops=ROWS * HID * 160, bytes_accessed=5 << 20, transcendentals=ROWS * HID
        ),
        name="early",
    )(where, activations, out_grad, pm_t, gate, up, ph_t)


def grads(where_ref, base, h_refs, held, gate_ref, up_ref, ph_ref, gg_ref, gu_ref):
    at = 0
    for h_ref in h_refs:
        width = h_ref.shape[1]
        held[:, at : at + width] = h_ref[...].astype(F32)
        at += width
    hidden_grad = jnp.concatenate(
        [
            held[:, pl.ds(pl.multiple_of(where_ref[base + i] * 128, 128), 128)][:, :SHARD]
            for i in range(8)
        ],
        axis=1,
    )
    row = pl.program_id(0) * 64 + lax.broadcasted_iota(jnp.int32, hidden_grad.shape, 0)
    hidden_grad = jnp.where(row < where_ref[19], hidden_grad, 0.0)
    gate, up = gate_ref[...].astype(F32), up_ref[...].astype(F32)
    sig = jax.nn.sigmoid(gate)
    grad_up = (hidden_grad * (gate * sig)).astype(BF16)
    grad_gate = (hidden_grad * up * sig * (1.0 + gate * (1.0 - sig))).astype(BF16)
    gg_ref[...] = grad_gate
    gu_ref[...] = grad_up
    ph = ph_ref[...]
    return jnp.concatenate(
        [
            lax.dot_general(g, ph, NT, preferred_element_type=F32)
            for g in (grad_gate, grad_up)
        ],
        axis=1,
    )


def own_kernel(n, where_ref, gate_ref, up_ref, ph_ref, *refs):
    gg_ref, gu_ref, part_ref, held = refs[n:]
    part_ref[...] = grads(
        where_ref, 0, refs[:n], held, gate_ref, up_ref, ph_ref, gg_ref, gu_ref
    )


def row_tiles(half):
    tile = pl.BlockSpec((64, HALF), lambda i, w: (i, half(w)))
    return tile, pl.BlockSpec((RANK, HALF), lambda i, w: (0, half(w)))


def pieces_of(h):
    return [pl.BlockSpec((64, p.shape[1]), lambda i, w: (i, 0)) for p in h]


BIG = jax.ShapeDtypeStruct((ROWS, HID), BF16)


def own_half(where, gate, up, h, ph_t):
    tile, ranks = row_tiles(lambda w: w[18])
    return pl.pallas_call(
        functools.partial(own_kernel, len(h)),
        out_shape=(BIG, BIG, jax.ShapeDtypeStruct((ROWS, 2 * RANK), F32)),
        grid_spec=pltpu.PrefetchScalarGridSpec(
            num_scalar_prefetch=1,
            grid=(8,),
            in_specs=[tile, tile, ranks] + pieces_of(h),
            out_specs=(tile, tile, pl.BlockSpec((64, 2 * RANK), lambda i, w: (i, 0))),
            scratch_shapes=[pltpu.VMEM((64, 1024), F32)],
        ),
        compiler_params=pltpu.CompilerParams(vmem_limit_bytes=8 << 20),
        cost_estimate=pl.CostEstimate(
            flops=ROWS * HALF * 280, bytes_accessed=6 << 20, transcendentals=ROWS * HALF
        ),
        name="own_half",
    )(where, gate, up, ph_t, *h)


def other_kernel(n, where_ref, gate_ref, up_ref, ph_ref, part_ref, hi_ref, lo_ref,
                 gg_in, gu_in, *refs):
    gg_ref, gu_ref, feat_ref, held, acc = refs[n:]
    i = pl.program_id(0)
    part = grads(where_ref, 8, refs[:n], held, gate_ref, up_ref, ph_ref, gg_ref, gu_ref)
    acc[pl.ds(pl.multiple_of(i * 64, 64), 64), :] = part_ref[...] + part

    @pl.when(i == 7)
    def _():
        feat_ref[...] = twice(hi_ref[...], lo_ref[...], acc[...])


def parted(value):
    hi = value.astype(BF16)
    return hi, (value - hi.astype(F32)).astype(BF16)


def twice(hi, lo, right):
    right_hi, right_lo = parted(right)
    total = jnp.dot(lo, right_hi, preferred_element_type=F32)
    total += jnp.dot(hi, right_lo, preferred_element_type=F32)
    return total + jnp.dot(hi, right_hi, preferred_element_type=F32)


def other_half(where, gate, up, h, ph_t, part, spread, gg, gu):
    tile, ranks = row_tiles(lambda w: 1 - w[18])
    feat = pl.BlockSpec((4 * RANK, 2 * RANK), lambda i, w: (0, 0))
    spreads = pl.BlockSpec((4 * RANK, ROWS), lambda i, w: (0, 0))
    return pl.pallas_call(
        functools.partial(other_kernel, len(h)),
        out_shape=(BIG, BIG, jax.ShapeDtypeStruct((4 * RANK, 2 * RANK), F32)),
        grid_spec=pltpu.PrefetchScalarGridSpec(
            num_scalar_prefetch=1,
            grid=(8,),
            in_specs=[
                tile,
                tile,
                ranks,
                pl.BlockSpec((64, 2 * RANK), lambda i, w: (i, 0)),
                spreads,
                spreads,
                ANY,
                ANY,
            ]
            + pieces_of(h),
            out_specs=(tile, tile, feat),
            scratch_shapes=[pltpu.VMEM((64, 1024), F32), pltpu.VMEM((ROWS, 2 * RANK), F32)],
        ),
        input_output_aliases={7: 0, 8: 1},
        compiler_params=pltpu.CompilerParams(vmem_limit_bytes=8 << 20),
        cost_estimate=pl.CostEstimate(
            flops=ROWS * HALF * 280, bytes_accessed=6 << 20, transcendentals=ROWS * HALF
        ),
        name="other_half",
    )(where, gate, up, ph_t, part, *spread, gg, gu, *h)


def spread_kernel(where_ref, sums_ref, hi_ref, lo_ref, feat_ref):
    sums = sums_ref[...]
    left = sums[:, : 2 * RANK].T
    right = sums[:, 2 * RANK :]
    row = lax.broadcasted_iota(jnp.int32, (1, ROWS), 1)
    start = jnp.int32(0)
    for s in range(4):
        length = where_ref[20 + s]
        member = jnp.logical_and(row >= start, row < start + length).astype(F32)
        weight = member / jnp.sqrt(jnp.broadcast_to(length, (1, ROWS)).astype(F32))
        hi, lo = parted(left[:RANK] * weight)
        at = pl.ds(s * RANK, RANK)
        hi_ref[at, :] = hi
        lo_ref[at, :] = lo
        feat_ref[at, :] = twice(*parted(left[RANK:] * weight), right)
        start += length


def spread_features(where, sums):
    vmem = pl.BlockSpec(memory_space=pltpu.VMEM)
    side = jax.ShapeDtypeStruct((4 * RANK, ROWS), BF16)
    return pl.pallas_call(
        spread_kernel,
        out_shape=(side, side, jax.ShapeDtypeStruct((4 * RANK, RANK), F32)),
        in_specs=[pl.BlockSpec(memory_space=pltpu.SMEM), vmem],
        out_specs=(vmem, vmem, vmem),
        compiler_params=pltpu.CompilerParams(vmem_limit_bytes=8 << 20),
        name="spread",
    )(where, sums)


def sum_tensor(value, c):
    half = value.shape[0] // 2
    top, low = value[:half], value[half:]
    mine = jnp.where(c == 0, top, low) + swap(jnp.where(c == 0, low, top))
    across = send(mine, lambda z, x, y, c: (z, x, y + 2, c))
    mine = (mine + across) + (up_y(mine) + down_y(mine))
    theirs = swap(mine)
    return jnp.concatenate(
        [jnp.where(c == 0, mine, theirs), jnp.where(c == 0, theirs, mine)], axis=0
    )


def on_device(
    activations, out_grad, gate_pre, up_pre, down_weight, proj_model, proj_hidden, lengths
):
    z, x, y, c = (lax.axis_index(a) for a in AXES)
    where = jnp.concatenate(
        [
            slots(z, x, c),
            slots(3 - z, x, c),
            jnp.stack([y, c, z // 2, jnp.sum(lengths)]),
            lengths,
        ]
    ).astype(jnp.int32)
    own_w = down_weight
    r1 = route(own_w, "p", "+", "r1")
    r2 = route(own_w, "+", "-", "r2")
    r3 = route(own_w, "-", "p", "r3")
    theirs = mate(out_grad, "mate_rows")
    a1 = along_y(out_grad, 1, "a1")
    a2 = along_y(after(out_grad, a1), -1, "a2")
    a_far = along_y(a1, 1, "a_far")
    r1, r2, r3 = lax.optimization_barrier((r1, r2, r3))
    r4 = route(r1, "+", "p", "r4")
    r5 = route(pick(c, r1, r2), "-", "p", "r5")
    r6 = route(r2, "+", "-", "r6")
    theirs, a2, a_far = lax.optimization_barrier((theirs, a2, a_far))
    b1 = along_y(theirs, 1, "b1")
    b2 = along_y(theirs, -1, "b2")
    a_other = [swap(v, "a_swap") for v in (out_grad, a2, a1, a_far)]
    b1, *a_other = lax.optimization_barrier((b1, *a_other))
    b_far = along_y(b1, 1, "b_far")
    r7 = route(after(pick(c, r4, r6), r5), "+", "p", "r7")
    a_mine, b_mine = [out_grad, a1, a2, a_far], [theirs, b1, b2, b_far]
    b_other = [swap(v, "b_swap") for v in (theirs, b2, b1, b_far)]

    pm_t, ph_t = proj_model.T, proj_hidden.T
    parts = early(after(where, b1), activations, out_grad, pm_t, gate_pre, up_pre, ph_t)
    sums = sum_tensor(after(parts, r7), c)
    *spread, down_feat = spread_features(where, sums)

    h1 = product(BF16, where, b_mine, b_other, [own_w, r1, r2, r3])
    h2 = product(BF16, after(where, h1), b_mine, b_other, [r4, r5, r6])
    h3 = product(BF16, after(where, h2), b_mine, b_other, [r7])
    h_in = [mate(h, "mate_grad") for h in (h1, h2, h3)]
    o1 = product(F32, after(where, h2), a_mine, a_other, [own_w, r1, r2, r3, r4, r5, r6])
    o2 = product(F32, after(where, h3), a_mine, a_other, [r7])
    grad_gate, grad_up, part = own_half(where, gate_pre, up_pre, (o1, o2), ph_t)
    grad_gate, grad_up, feat = other_half(
        where, gate_pre, up_pre, h_in, ph_t, part, spread, grad_gate, grad_up
    )
    total = jnp.concatenate([sum_tensor(feat, c), down_feat], axis=1)
    features = total.reshape(4, RANK, 3, RANK).transpose(0, 2, 1, 3).reshape(4, 3, RANK * RANK)
    return grad_gate, grad_up, features


def solution(mesh):
    split = Mesh(mesh.devices.reshape(4, 4, 4, 2), AXES)
    dp, tensor = ("z", "x"), ("y", "c")
    return jax.shard_map(
        on_device,
        mesh=split,
        in_specs=(
            P(dp, tensor),
            P(dp, tensor),
            P(dp, tensor),
            P(dp, tensor),
            P((*tensor, *dp), None),
            P(),
            P(tensor, None),
            P(dp),
        ),
        out_specs=(P(dp, tensor), P(dp, tensor), P(dp, None, None)),
        check_vma=False,
    )
```

```python
import functools

import jax
import jax.numpy as jnp
from jax import lax
from jax.experimental import pallas as pl
from jax.experimental.pallas import tpu as pltpu
from jax.sharding import Mesh
from jax.sharding import PartitionSpec as P

AXES = ("z", "x", "y", "c")
F32, BF16 = jnp.float32, jnp.bfloat16
ROWS, FEAT, HID, HALF, RANK, DEPTH = 512, 640, 1792, 896, 64, 5120
SHARD = 112
TILE = 128
STEP = 2 * FEAT
NT = (((1,), (1,)), ((), ()))
LIGHT = pl.CostEstimate(flops=1 << 20, bytes_accessed=1 << 16, transcendentals=0)
ANY = pl.BlockSpec(memory_space=pl.ANY)


def send(value, target, name="send"):
    def line(z, x, y, c):
        return ((z % 4 * 4 + x % 4) * 4 + y % 4) * 2 + c

    pairs = [
        (line(z, x, y, c), line(*target(z, x, y, c)))
        for z in range(4)
        for x in range(4)
        for y in range(4)
        for c in range(2)
    ]
    with jax.named_scope(name):
        return lax.ppermute(value, AXES, pairs)


def up_y(v, name="up"):
    return send(v, lambda z, x, y, c: (z, x, y + 1, c), name)


def down_y(v, name="down"):
    return send(v, lambda z, x, y, c: (z, x, y - 1, c), name)


def along_y(v, way, name):
    return send(v, lambda z, x, y, c: (z, x, y + way * (1 - 2 * c), c), name)


def swap(v, name="swap"):
    return send(v, lambda z, x, y, c: (z, x, y, 1 - c), name)


def mate(v, name="mate"):
    return send(v, lambda z, x, y, c: (3 - z, x, y, c), name)


def after(value, *others):
    return lax.optimization_barrier((value, *others))[0]


def pick(c, a, b):
    return jnp.where(c == 0, a, b)


def route(v, zero, one, name):
    hop = {
        "p": lambda z, x, y, c: (z ^ 1, x, y, c),
        "+": lambda z, x, y, c: (z, x + 1, y, c),
        "-": lambda z, x, y, c: (z, x - 1, y, c),
    }
    return send(v, lambda z, x, y, c: hop[zero if c == 0 else one](z, x, y, c), name)


def slots(z, x, c):
    zl, first = z % 2, c == 0

    def at(dz, dx):
        return (zl + dz) % 2 * 4 + (x + dx) % 4

    held = jnp.stack(
        [
            at(0, 0),
            jnp.where(first, at(1, 0), at(0, 3)),
            jnp.where(first, at(0, 3), at(0, 1)),
            jnp.where(first, at(0, 1), at(1, 0)),
            at(1, 3),
            at(1, 1),
            at(0, 2),
            at(1, 2),
        ]
    )
    shard = jnp.arange(8)
    return jnp.sum(jnp.where(held[None, :] == shard[:, None], shard[None, :], 0), axis=1)


def product_kernel(shards, where_ref, *refs):
    mine, other, weights = refs[:4], refs[4:8], refs[8 : 8 + shards]
    out_ref, *acc = refs[8 + shards :]
    acc = acc[0] if acc else out_ref
    y, c = where_ref[16], where_ref[17]
    for step, shift in enumerate((0, 3 - 2 * c, 1 + 2 * c, 2)):
        first = lax.rem(y + shift, 4) * STEP
        near, far = (pl.multiple_of(first + core * FEAT, 128) for core in (c, 1 - c))
        left = jnp.concatenate([mine[step][...], other[step][...]], axis=1)
        rows = []
        for k, w in enumerate(weights):
            rows.append(
                jnp.concatenate([w[:, pl.ds(near, FEAT)], w[:, pl.ds(far, FEAT)]], axis=1)
            )
            if shards > 1:
                rows.append(jnp.zeros((128 - SHARD, STEP), BF16))
        right = jnp.concatenate(rows, axis=0) if shards > 1 else rows[0]
        part = lax.dot_general(left, right, NT, preferred_element_type=F32)
        if step == 0:
            acc[:, : part.shape[1]] = part
        elif step < 3:
            acc[:, : part.shape[1]] += part
        else:
            out_ref[:, : part.shape[1]] = (acc[:, : part.shape[1]] + part).astype(out_ref.dtype)


def product(dtype, where, mine, other, weights):
    shards = len(weights)
    width = shards * 128
    vmem = pl.BlockSpec(memory_space=pltpu.VMEM)
    return pl.pallas_call(
        functools.partial(product_kernel, shards),
        out_shape=jax.ShapeDtypeStruct((ROWS, width), dtype),
        in_specs=[pl.BlockSpec(memory_space=pltpu.SMEM)] + [vmem] * (8 + shards),
        out_specs=vmem,
        scratch_shapes=[] if dtype == F32 else [pltpu.VMEM((ROWS, width), F32)],
        compiler_params=pltpu.CompilerParams(
            vmem_limit_bytes=(4 << 20) + width * (4 * STEP + 14 * ROWS)
        ),
        cost_estimate=LIGHT,
        name="product",
    )(where, *mine, *other, *weights)


def early_kernel(where_ref, act_ref, grad_ref, pm_ref, gate_ref, up_ref, ph_ref, out_ref):
    gate, up = gate_ref[...].astype(F32), up_ref[...].astype(F32)
    hidden = (gate * jax.nn.sigmoid(gate) * up).astype(BF16)
    pm = pm_ref[...]
    out_ref[:, 0:64] = lax.dot_general(act_ref[...], pm, NT, preferred_element_type=F32)
    out_ref[:, 64:128] = lax.dot_general(hidden, ph_ref[...], NT, preferred_element_type=F32)
    out_ref[:, 128:192] = lax.dot_general(grad_ref[...], pm, NT, preferred_element_type=F32)


def early(where, activations, out_grad, pm_t, gate, up, ph_t):
    narrow = pl.BlockSpec((128, FEAT), lambda i, w: (i, 0))
    wide = pl.BlockSpec((128, HID), lambda i, w: (i, 0))
    return pl.pallas_call(
        early_kernel,
        out_shape=jax.ShapeDtypeStruct((ROWS, 3 * RANK), F32),
        grid_spec=pltpu.PrefetchScalarGridSpec(
            num_scalar_prefetch=1,
            grid=(4,),
            in_specs=[
                narrow,
                narrow,
                pl.BlockSpec((RANK, FEAT), lambda i, w: (0, 2 * w[16] + w[17])),
                wide,
                wide,
                pl.BlockSpec((RANK, HID), lambda i, w: (0, 0)),
            ],
            out_specs=pl.BlockSpec((128, 3 * RANK), lambda i, w: (i, 0)),
        ),
        compiler_params=pltpu.CompilerParams(vmem_limit_bytes=12 << 20),
        cost_estimate=LIGHT,
        name="early",
    )(where, activations, out_grad, pm_t, gate, up, ph_t)


def grads(where_ref, base, h_refs, held, gate_ref, up_ref, ph_ref, gg_ref, gu_ref):
    at = 0
    for h_ref in h_refs:
        width = h_ref.shape[1]
        held[:, at : at + width] = h_ref[...].astype(F32)
        at += width
    hidden_grad = jnp.concatenate(
        [
            held[:, pl.ds(pl.multiple_of(where_ref[base + i] * 128, 128), 128)][:, :SHARD]
            for i in range(8)
        ],
        axis=1,
    )
    row = pl.program_id(0) * TILE + lax.broadcasted_iota(jnp.int32, hidden_grad.shape, 0)
    hidden_grad = jnp.where(row < where_ref[19], hidden_grad, 0.0)
    gate, up = gate_ref[...].astype(F32), up_ref[...].astype(F32)
    sig = jax.nn.sigmoid(gate)
    grad_up = (hidden_grad * (gate * sig)).astype(BF16)
    grad_gate = (hidden_grad * up * sig * (1.0 + gate * (1.0 - sig))).astype(BF16)
    gg_ref[...] = grad_gate
    gu_ref[...] = grad_up
    both = jnp.concatenate([grad_gate, grad_up], axis=0)
    part = lax.dot_general(both, ph_ref[...], NT, preferred_element_type=F32)
    return jnp.concatenate([part[:TILE], part[TILE:]], axis=1)


def own_kernel(n, where_ref, gate_ref, up_ref, ph_ref, *refs):
    gg_ref, gu_ref, part_ref, held = refs[n:]
    part_ref[...] = grads(
        where_ref, 0, refs[:n], held, gate_ref, up_ref, ph_ref, gg_ref, gu_ref
    )


def row_tiles(half):
    tile = pl.BlockSpec((TILE, HALF), lambda i, w: (i, half(w)))
    return tile, pl.BlockSpec((RANK, HALF), lambda i, w: (0, half(w)))


def pieces_of(h):
    return [pl.BlockSpec((TILE, p.shape[1]), lambda i, w: (i, 0)) for p in h]


BIG = jax.ShapeDtypeStruct((ROWS, HID), BF16)


def own_half(where, gate, up, h, ph_t):
    tile, ranks = row_tiles(lambda w: w[18])
    return pl.pallas_call(
        functools.partial(own_kernel, len(h)),
        out_shape=(BIG, BIG, jax.ShapeDtypeStruct((ROWS, 2 * RANK), F32)),
        grid_spec=pltpu.PrefetchScalarGridSpec(
            num_scalar_prefetch=1,
            grid=(ROWS // TILE,),
            in_specs=[tile, tile, ranks] + pieces_of(h),
            out_specs=(tile, tile, pl.BlockSpec((TILE, 2 * RANK), lambda i, w: (i, 0))),
            scratch_shapes=[pltpu.VMEM((TILE, 1024), F32)],
        ),
        compiler_params=pltpu.CompilerParams(vmem_limit_bytes=14 << 20),
        cost_estimate=LIGHT,
        name="own_half",
    )(where, gate, up, ph_t, *h)


def other_kernel(n, where_ref, gate_ref, up_ref, ph_ref, part_ref, hi_ref, lo_ref,
                 gg_in, gu_in, *refs):
    gg_ref, gu_ref, feat_ref, held, acc = refs[n:]
    i = pl.program_id(0)
    part = grads(where_ref, 8, refs[:n], held, gate_ref, up_ref, ph_ref, gg_ref, gu_ref)
    acc[pl.ds(pl.multiple_of(i * TILE, TILE), TILE), :] = part_ref[...] + part

    @pl.when(i == ROWS // TILE - 1)
    def _():
        feat_ref[...] = twice(hi_ref[...], lo_ref[...], acc[...])


def parted(value):
    hi = value.astype(BF16)
    return hi, (value - hi.astype(F32)).astype(BF16)


def twice(hi, lo, right):
    right_hi, right_lo = parted(right)
    total = jnp.dot(lo, right_hi, preferred_element_type=F32)
    total += jnp.dot(hi, right_lo, preferred_element_type=F32)
    return total + jnp.dot(hi, right_hi, preferred_element_type=F32)


def other_half(where, gate, up, h, ph_t, part, spread, gg, gu):
    tile, ranks = row_tiles(lambda w: 1 - w[18])
    feat = pl.BlockSpec((4 * RANK, 2 * RANK), lambda i, w: (0, 0))
    spreads = pl.BlockSpec((4 * RANK, ROWS), lambda i, w: (0, 0))
    return pl.pallas_call(
        functools.partial(other_kernel, len(h)),
        out_shape=(BIG, BIG, jax.ShapeDtypeStruct((4 * RANK, 2 * RANK), F32)),
        grid_spec=pltpu.PrefetchScalarGridSpec(
            num_scalar_prefetch=1,
            grid=(ROWS // TILE,),
            in_specs=[
                tile,
                tile,
                ranks,
                pl.BlockSpec((TILE, 2 * RANK), lambda i, w: (i, 0)),
                spreads,
                spreads,
                ANY,
                ANY,
            ]
            + pieces_of(h),
            out_specs=(tile, tile, feat),
            scratch_shapes=[pltpu.VMEM((TILE, 1024), F32), pltpu.VMEM((ROWS, 2 * RANK), F32)],
        ),
        input_output_aliases={7: 0, 8: 1},
        compiler_params=pltpu.CompilerParams(vmem_limit_bytes=14 << 20),
        cost_estimate=LIGHT,
        name="other_half",
    )(where, gate, up, ph_t, part, *spread, gg, gu, *h)


def spread_kernel(where_ref, sums_ref, hi_ref, lo_ref, feat_ref):
    sums = sums_ref[...]
    left = sums[:, : 2 * RANK].T
    right = sums[:, 2 * RANK :]
    row = lax.broadcasted_iota(jnp.int32, (1, ROWS), 1)
    start = jnp.int32(0)
    for s in range(4):
        length = where_ref[20 + s]
        member = jnp.logical_and(row >= start, row < start + length).astype(F32)
        weight = member / jnp.sqrt(jnp.broadcast_to(length, (1, ROWS)).astype(F32))
        hi, lo = parted(left[:RANK] * weight)
        at = pl.ds(s * RANK, RANK)
        hi_ref[at, :] = hi
        lo_ref[at, :] = lo
        feat_ref[at, :] = twice(*parted(left[RANK:] * weight), right)
        start += length


def spread_features(where, sums):
    vmem = pl.BlockSpec(memory_space=pltpu.VMEM)
    side = jax.ShapeDtypeStruct((4 * RANK, ROWS), BF16)
    return pl.pallas_call(
        spread_kernel,
        out_shape=(side, side, jax.ShapeDtypeStruct((4 * RANK, RANK), F32)),
        in_specs=[pl.BlockSpec(memory_space=pltpu.SMEM), vmem],
        out_specs=(vmem, vmem, vmem),
        compiler_params=pltpu.CompilerParams(vmem_limit_bytes=8 << 20),
        name="spread",
    )(where, sums)


def sum_tensor(value, c):
    half = value.shape[0] // 2
    top, low = value[:half], value[half:]
    mine = jnp.where(c == 0, top, low) + swap(jnp.where(c == 0, low, top))
    across = send(mine, lambda z, x, y, c: (z, x, y + 2, c))
    mine = (mine + across) + (up_y(mine) + down_y(mine))
    theirs = swap(mine)
    return jnp.concatenate(
        [jnp.where(c == 0, mine, theirs), jnp.where(c == 0, theirs, mine)], axis=0
    )


def on_device(
    activations, out_grad, gate_pre, up_pre, down_weight, proj_model, proj_hidden, lengths
):
    z, x, y, c = (lax.axis_index(a) for a in AXES)
    where = jnp.concatenate(
        [
            slots(z, x, c),
            slots(3 - z, x, c),
            jnp.stack([y, c, z // 2, jnp.sum(lengths)]),
            lengths,
        ]
    ).astype(jnp.int32)
    own_w = down_weight
    r1 = route(own_w, "p", "+", "r1")
    r2 = route(own_w, "+", "-", "r2")
    r3 = route(own_w, "-", "p", "r3")
    theirs = mate(out_grad, "mate_rows")
    a1 = along_y(out_grad, 1, "a1")
    a2 = along_y(after(out_grad, a1), -1, "a2")
    b1 = along_y(theirs, 1, "b1")
    r1, r2, r3, a2, b1 = lax.optimization_barrier((r1, r2, r3, a2, b1))
    r4 = route(r1, "+", "p", "r4")
    r5 = route(pick(c, r1, r2), "-", "p", "r5")
    r6 = route(r2, "+", "-", "r6")
    b2 = along_y(after(theirs, a2), -1, "b2")
    b_far = along_y(b1, 1, "b_far")
    b_other = [swap(after(v, b2), "b_swap") for v in (theirs, b2)]
    b_other += [swap(after(v, *b_other), "b_swap") for v in (b1, b_far)]
    b_mine = [theirs, b1, b2, b_far]
    h1 = product(BF16, where, b_mine, b_other, [own_w, r1, r2, r3])
    r7 = route(after(pick(c, r4, r6), r5, h1), "+", "p", "r7")
    a_far = along_y(after(a1, *b_other), 1, "a_far")
    a_mine = [out_grad, a1, a2, a_far]
    a_other = [swap(after(v, *b_other), "a_swap") for v in (out_grad, a2, a1, a_far)]

    h2 = product(BF16, after(where, h1), b_mine, b_other, [r4, r5, r6])
    pm_t, ph_t = proj_model.T, proj_hidden.T
    parts = early(after(where, h1), activations, out_grad, pm_t, gate_pre, up_pre, ph_t)
    sums = sum_tensor(after(parts, h2), c)
    *spread, down_feat = spread_features(where, sums)

    h1_in = mate(h1, "mate_grad1")
    own1 = product(F32, after(where, h2), a_mine, a_other, [own_w, r1, r2, r3, r4, r5, r6])
    h3 = product(BF16, after(where, own1, h1_in), b_mine, b_other, [r7])
    h2_in = mate(h2, "mate_grad2")
    own2 = product(F32, after(where, h3, h2_in), a_mine, a_other, [r7])
    h_in = [h1_in, h2_in, mate(h3, "mate_grad3")]
    grad_gate, grad_up, part = own_half(where, gate_pre, up_pre, (own1, own2), ph_t)
    grad_gate, grad_up, feat = other_half(
        where, gate_pre, up_pre, h_in, ph_t, part, spread, grad_gate, grad_up
    )
    total = jnp.concatenate([sum_tensor(feat, c), down_feat], axis=1)
    features = total.reshape(4, RANK, 3, RANK).transpose(0, 2, 1, 3).reshape(4, 3, RANK * RANK)
    return grad_gate, grad_up, features


def solution(mesh):
    split = Mesh(mesh.devices.reshape(4, 4, 4, 2), AXES)
    dp, tensor = ("z", "x"), ("y", "c")
    return jax.shard_map(
        on_device,
        mesh=split,
        in_specs=(
            P(dp, tensor),
            P(dp, tensor),
            P(dp, tensor),
            P(dp, tensor),
            P((*tensor, *dp), None),
            P(),
            P(tensor, None),
            P(dp),
        ),
        out_specs=(P(dp, tensor), P(dp, tensor), P(dp, None, None)),
        check_vma=False,
    )
```

```python
import functools

import jax
import jax.numpy as jnp
from jax import lax
from jax.experimental import pallas as pl
from jax.experimental.pallas import tpu as pltpu
from jax.sharding import Mesh
from jax.sharding import PartitionSpec as P

AXES = ("z", "x", "y", "c")
F32, BF16 = jnp.float32, jnp.bfloat16
ROWS, FEAT, HID, HALF, RANK, DEPTH = 512, 640, 1792, 896, 64, 5120
SHARD = 112
TILE = 128
STEP = 2 * FEAT
NT = (((1,), (1,)), ((), ()))
LIGHT = pl.CostEstimate(flops=1 << 20, bytes_accessed=1 << 16, transcendentals=0)
ANY = pl.BlockSpec(memory_space=pl.ANY)


def send(value, target, name="send"):
    def line(z, x, y, c):
        return ((z % 4 * 4 + x % 4) * 4 + y % 4) * 2 + c

    pairs = [
        (line(z, x, y, c), line(*target(z, x, y, c)))
        for z in range(4)
        for x in range(4)
        for y in range(4)
        for c in range(2)
    ]
    with jax.named_scope(name):
        return lax.ppermute(value, AXES, pairs)


def up_y(v, name="up"):
    return send(v, lambda z, x, y, c: (z, x, y + 1, c), name)


def down_y(v, name="down"):
    return send(v, lambda z, x, y, c: (z, x, y - 1, c), name)


def along_y(v, way, name):
    return send(v, lambda z, x, y, c: (z, x, y + way * (1 - 2 * c), c), name)


def swap(v, name="swap"):
    return send(v, lambda z, x, y, c: (z, x, y, 1 - c), name)


def mate(v, name="mate"):
    return send(v, lambda z, x, y, c: (3 - z, x, y, c), name)


def after(value, *others):
    return lax.optimization_barrier((value, *others))[0]


def route(v, zero, one, name):
    hop = {
        "p": lambda z, x, y, c: (z ^ 1, x, y, c),
        "+": lambda z, x, y, c: (z, x + 1, y, c),
        "-": lambda z, x, y, c: (z, x - 1, y, c),
    }
    return send(v, lambda z, x, y, c: hop[zero if c == 0 else one](z, x, y, c), name)


def slots(z, x, c):
    zl, first = z % 2, c == 0

    def at(dz, dx):
        return (zl + dz) % 2 * 4 + (x + dx) % 4

    held = jnp.stack(
        [
            at(0, 0),
            at(0, 3),
            jnp.where(first, at(1, 0), at(0, 1)),
            jnp.where(first, at(0, 1), at(1, 0)),
            jnp.where(first, at(1, 3), at(1, 1)),
            jnp.where(first, at(0, 2), at(1, 3)),
            jnp.where(first, at(1, 1), at(0, 2)),
            at(1, 2),
        ]
    )
    shard = jnp.arange(8)
    return jnp.sum(jnp.where(held[None, :] == shard[:, None], shard[None, :], 0), axis=1)


def product_kernel(shards, where_ref, *refs):
    mine, other, weights = refs[:4], refs[4:8], refs[8 : 8 + shards]
    out_ref, *acc = refs[8 + shards :]
    acc = acc[0] if acc else out_ref
    y, c = where_ref[16], where_ref[17]
    for step, shift in enumerate((0, 3 - 2 * c, 1 + 2 * c, 2)):
        first = lax.rem(y + shift, 4) * STEP
        near, far = (pl.multiple_of(first + core * FEAT, 128) for core in (c, 1 - c))
        left = jnp.concatenate([mine[step][...], other[step][...]], axis=1)
        rows = []
        for k, w in enumerate(weights):
            rows.append(
                jnp.concatenate([w[:, pl.ds(near, FEAT)], w[:, pl.ds(far, FEAT)]], axis=1)
            )
            if shards > 1:
                rows.append(jnp.zeros((128 - SHARD, STEP), BF16))
        right = jnp.concatenate(rows, axis=0) if shards > 1 else rows[0]
        part = lax.dot_general(left, right, NT, preferred_element_type=F32)
        if step == 0:
            acc[:, : part.shape[1]] = part
        elif step < 3:
            acc[:, : part.shape[1]] += part
        else:
            out_ref[:, : part.shape[1]] = (acc[:, : part.shape[1]] + part).astype(out_ref.dtype)


def product(dtype, where, mine, other, weights):
    shards = len(weights)
    width = shards * 128
    vmem = pl.BlockSpec(memory_space=pltpu.VMEM)
    return pl.pallas_call(
        functools.partial(product_kernel, shards),
        out_shape=jax.ShapeDtypeStruct((ROWS, width), dtype),
        in_specs=[pl.BlockSpec(memory_space=pltpu.SMEM)] + [vmem] * (8 + shards),
        out_specs=vmem,
        scratch_shapes=[] if dtype == F32 else [pltpu.VMEM((ROWS, width), F32)],
        compiler_params=pltpu.CompilerParams(
            vmem_limit_bytes=(6 << 20) + width * (4 * STEP + 14 * ROWS)
        ),
        cost_estimate=LIGHT,
        name="product",
    )(where, *mine, *other, *weights)


def early_kernel(where_ref, act_ref, grad_ref, pm_ref, gate_ref, up_ref, ph_ref, out_ref):
    gate, up = gate_ref[...].astype(F32), up_ref[...].astype(F32)
    hidden = (gate * jax.nn.sigmoid(gate) * up).astype(BF16)
    pm = pm_ref[...]
    out_ref[:, 0:64] = lax.dot_general(act_ref[...], pm, NT, preferred_element_type=F32)
    out_ref[:, 64:128] = lax.dot_general(hidden, ph_ref[...], NT, preferred_element_type=F32)
    out_ref[:, 128:192] = lax.dot_general(grad_ref[...], pm, NT, preferred_element_type=F32)


def early(where, activations, out_grad, pm_t, gate, up, ph_t):
    narrow = pl.BlockSpec((128, FEAT), lambda i, w: (i, 0))
    wide = pl.BlockSpec((128, HID), lambda i, w: (i, 0))
    return pl.pallas_call(
        early_kernel,
        out_shape=jax.ShapeDtypeStruct((ROWS, 3 * RANK), F32),
        grid_spec=pltpu.PrefetchScalarGridSpec(
            num_scalar_prefetch=1,
            grid=(4,),
            in_specs=[
                narrow,
                narrow,
                pl.BlockSpec((RANK, FEAT), lambda i, w: (0, 2 * w[16] + w[17])),
                wide,
                wide,
                pl.BlockSpec((RANK, HID), lambda i, w: (0, 0)),
            ],
            out_specs=pl.BlockSpec((128, 3 * RANK), lambda i, w: (i, 0)),
        ),
        compiler_params=pltpu.CompilerParams(vmem_limit_bytes=12 << 20),
        cost_estimate=LIGHT,
        name="early",
    )(where, activations, out_grad, pm_t, gate, up, ph_t)


def grads(where_ref, base, h_refs, held, gate_ref, up_ref, ph_ref, gg_ref, gu_ref):
    at = 0
    for h_ref in h_refs:
        width = h_ref.shape[1]
        held[:, at : at + width] = h_ref[...].astype(F32)
        at += width
    hidden_grad = jnp.concatenate(
        [
            held[:, pl.ds(pl.multiple_of(where_ref[base + i] * 128, 128), 128)][:, :SHARD]
            for i in range(8)
        ],
        axis=1,
    )
    row = pl.program_id(0) * TILE + lax.broadcasted_iota(jnp.int32, hidden_grad.shape, 0)
    hidden_grad = jnp.where(row < where_ref[19], hidden_grad, 0.0)
    gate, up = gate_ref[...].astype(F32), up_ref[...].astype(F32)
    sig = jax.nn.sigmoid(gate)
    grad_up = (hidden_grad * (gate * sig)).astype(BF16)
    grad_gate = (hidden_grad * up * sig * (1.0 + gate * (1.0 - sig))).astype(BF16)
    gg_ref[...] = grad_gate
    gu_ref[...] = grad_up
    both = jnp.concatenate([grad_gate, grad_up], axis=0)
    part = lax.dot_general(both, ph_ref[...], NT, preferred_element_type=F32)
    return jnp.concatenate([part[:TILE], part[TILE:]], axis=1)


def own_kernel(n, where_ref, gate_ref, up_ref, ph_ref, *refs):
    gg_ref, gu_ref, part_ref, held = refs[n:]
    part_ref[...] = grads(
        where_ref, 0, refs[:n], held, gate_ref, up_ref, ph_ref, gg_ref, gu_ref
    )


def row_tiles(half):
    tile = pl.BlockSpec((TILE, HALF), lambda i, w: (i, half(w)))
    return tile, pl.BlockSpec((RANK, HALF), lambda i, w: (0, half(w)))


def pieces_of(h):
    return [pl.BlockSpec((TILE, p.shape[1]), lambda i, w: (i, 0)) for p in h]


BIG = jax.ShapeDtypeStruct((ROWS, HID), BF16)


def own_half(where, gate, up, h, ph_t):
    tile, ranks = row_tiles(lambda w: w[18])
    return pl.pallas_call(
        functools.partial(own_kernel, len(h)),
        out_shape=(BIG, BIG, jax.ShapeDtypeStruct((ROWS, 2 * RANK), F32)),
        grid_spec=pltpu.PrefetchScalarGridSpec(
            num_scalar_prefetch=1,
            grid=(ROWS // TILE,),
            in_specs=[tile, tile, ranks] + pieces_of(h),
            out_specs=(tile, tile, pl.BlockSpec((TILE, 2 * RANK), lambda i, w: (i, 0))),
            scratch_shapes=[pltpu.VMEM((TILE, 1024), F32)],
        ),
        compiler_params=pltpu.CompilerParams(vmem_limit_bytes=14 << 20),
        cost_estimate=LIGHT,
        name="own_half",
    )(where, gate, up, ph_t, *h)


def other_kernel(n, where_ref, gate_ref, up_ref, ph_ref, part_ref, hi_ref, lo_ref,
                 gg_in, gu_in, *refs):
    gg_ref, gu_ref, feat_ref, held, acc = refs[n:]
    i = pl.program_id(0)
    part = grads(where_ref, 8, refs[:n], held, gate_ref, up_ref, ph_ref, gg_ref, gu_ref)
    acc[pl.ds(pl.multiple_of(i * TILE, TILE), TILE), :] = part_ref[...] + part

    @pl.when(i == ROWS // TILE - 1)
    def _():
        feat_ref[...] = twice(hi_ref[...], lo_ref[...], acc[...])


def parted(value):
    hi = value.astype(BF16)
    return hi, (value - hi.astype(F32)).astype(BF16)


def twice(hi, lo, right):
    right_hi, right_lo = parted(right)
    total = jnp.dot(lo, right_hi, preferred_element_type=F32)
    total += jnp.dot(hi, right_lo, preferred_element_type=F32)
    return total + jnp.dot(hi, right_hi, preferred_element_type=F32)


def other_half(where, gate, up, h, ph_t, part, spread, gg, gu):
    tile, ranks = row_tiles(lambda w: 1 - w[18])
    feat = pl.BlockSpec((4 * RANK, 2 * RANK), lambda i, w: (0, 0))
    spreads = pl.BlockSpec((4 * RANK, ROWS), lambda i, w: (0, 0))
    return pl.pallas_call(
        functools.partial(other_kernel, len(h)),
        out_shape=(BIG, BIG, jax.ShapeDtypeStruct((4 * RANK, 2 * RANK), F32)),
        grid_spec=pltpu.PrefetchScalarGridSpec(
            num_scalar_prefetch=1,
            grid=(ROWS // TILE,),
            in_specs=[
                tile,
                tile,
                ranks,
                pl.BlockSpec((TILE, 2 * RANK), lambda i, w: (i, 0)),
                spreads,
                spreads,
                ANY,
                ANY,
            ]
            + pieces_of(h),
            out_specs=(tile, tile, feat),
            scratch_shapes=[pltpu.VMEM((TILE, 1024), F32), pltpu.VMEM((ROWS, 2 * RANK), F32)],
        ),
        input_output_aliases={7: 0, 8: 1},
        compiler_params=pltpu.CompilerParams(vmem_limit_bytes=14 << 20),
        cost_estimate=LIGHT,
        name="other_half",
    )(where, gate, up, ph_t, part, *spread, gg, gu, *h)


def spread_kernel(where_ref, sums_ref, hi_ref, lo_ref, feat_ref):
    sums = sums_ref[...]
    left = sums[:, : 2 * RANK].T
    right = sums[:, 2 * RANK :]
    row = lax.broadcasted_iota(jnp.int32, (1, ROWS), 1)
    start = jnp.int32(0)
    for s in range(4):
        length = where_ref[20 + s]
        member = jnp.logical_and(row >= start, row < start + length).astype(F32)
        weight = member / jnp.sqrt(jnp.broadcast_to(length, (1, ROWS)).astype(F32))
        hi, lo = parted(left[:RANK] * weight)
        at = pl.ds(s * RANK, RANK)
        hi_ref[at, :] = hi
        lo_ref[at, :] = lo
        feat_ref[at, :] = twice(*parted(left[RANK:] * weight), right)
        start += length


def spread_features(where, sums):
    vmem = pl.BlockSpec(memory_space=pltpu.VMEM)
    side = jax.ShapeDtypeStruct((4 * RANK, ROWS), BF16)
    return pl.pallas_call(
        spread_kernel,
        out_shape=(side, side, jax.ShapeDtypeStruct((4 * RANK, RANK), F32)),
        in_specs=[pl.BlockSpec(memory_space=pltpu.SMEM), vmem],
        out_specs=(vmem, vmem, vmem),
        compiler_params=pltpu.CompilerParams(vmem_limit_bytes=8 << 20),
        name="spread",
    )(where, sums)


def sum_tensor(value, c):
    half = value.shape[0] // 2
    top, low = value[:half], value[half:]
    mine = jnp.where(c == 0, top, low) + swap(jnp.where(c == 0, low, top))
    across = send(mine, lambda z, x, y, c: (z, x, y + 2, c))
    mine = (mine + across) + (up_y(mine) + down_y(mine))
    theirs = swap(mine)
    return jnp.concatenate(
        [jnp.where(c == 0, mine, theirs), jnp.where(c == 0, theirs, mine)], axis=0
    )


def on_device(
    activations, out_grad, gate_pre, up_pre, down_weight, proj_model, proj_hidden, lengths
):
    z, x, y, c = (lax.axis_index(a) for a in AXES)
    where = jnp.concatenate(
        [
            slots(z, x, c),
            slots(3 - z, x, c),
            jnp.stack([y, c, z // 2, jnp.sum(lengths)]),
            lengths,
        ]
    ).astype(jnp.int32)
    own_w = down_weight
    theirs = mate(out_grad, "mate_rows")
    a1, a2 = along_y(out_grad, 1, "a1"), along_y(out_grad, -1, "a2")
    r1 = route(own_w, "+", "+", "r1")
    r2 = route(own_w, "p", "-", "r2")
    theirs, a1, a2, again = lax.optimization_barrier((theirs, a1, a2, own_w))
    r3 = route(again, "-", "p", "r3")
    b1, b2 = along_y(theirs, 1, "b1"), along_y(theirs, -1, "b2")
    r1, r2, r3, b1, b2 = lax.optimization_barrier((r1, r2, r3, b1, b2))
    r6 = route(r2, "-", "-", "r6")
    r4 = route(r2, "+", "p", "r4")
    r5 = route(r1, "+", "p", "r5")
    b_far = along_y(b1, 1, "b_far")
    b_other = [swap(v, "b_swap") for v in (after(theirs, b1), b2, b1, b_far)]
    b_mine = [theirs, b1, b2, b_far]
    r7 = route(r6, "-", "p", "r7")
    h1 = product(BF16, after(where, r4, r5, r6), b_mine, b_other, [own_w, r1, r2, r3])
    h1_in = mate(h1, "mate_grad1")
    a_far = along_y(after(a1, h1), 1, "a_far")
    h2 = product(BF16, after(where, h1), b_mine, b_other, [r4, r5, r6])
    h2_in = mate(h2, "mate_grad2")
    a_mine = [out_grad, a1, a2, a_far]
    a_other = [swap(v, "a_swap") for v in (after(out_grad, h1), after(a2, h1), after(a1, h1), a_far)]

    pm_t, ph_t = proj_model.T, proj_hidden.T
    own1 = product(
        F32, after(where, h2), a_mine, a_other, [own_w, r1, r2, r3, r4, r5, r6]
    )
    parts = early(after(where, h2), activations, out_grad, pm_t, gate_pre, up_pre, ph_t)
    sums = sum_tensor(after(parts, r7, h1_in, own1), c)
    *spread, down_feat = spread_features(where, sums)

    h3 = product(BF16, after(where, h2, h1_in, own1), b_mine, b_other, [r7])
    own2 = product(F32, after(where, h3, h2_in), a_mine, a_other, [r7])
    h_in = [h1_in, h2_in, mate(h3, "mate_grad3")]
    grad_gate, grad_up, part = own_half(where, gate_pre, up_pre, (own1, own2), ph_t)
    grad_gate, grad_up, feat = other_half(
        where, gate_pre, up_pre, h_in, ph_t, part, spread, grad_gate, grad_up
    )
    total = jnp.concatenate([sum_tensor(feat, c), down_feat], axis=1)
    features = total.reshape(4, RANK, 3, RANK).transpose(0, 2, 1, 3).reshape(4, 3, RANK * RANK)
    return grad_gate, grad_up, features


def solution(mesh):
    split = Mesh(mesh.devices.reshape(4, 4, 4, 2), AXES)
    dp, tensor = ("z", "x"), ("y", "c")
    return jax.shard_map(
        on_device,
        mesh=split,
        in_specs=(
            P(dp, tensor),
            P(dp, tensor),
            P(dp, tensor),
            P(dp, tensor),
            P((*tensor, *dp), None),
            P(),
            P(tensor, None),
            P(dp),
        ),
        out_specs=(P(dp, tensor), P(dp, tensor), P(dp, None, None)),
        check_vma=False,
    )
```

```python
import functools

import jax
import jax.numpy as jnp
from jax import lax
from jax.experimental import pallas as pl
from jax.experimental.pallas import tpu as pltpu
from jax.sharding import Mesh
from jax.sharding import PartitionSpec as P

AXES = ("z", "x", "y", "c")
F32, BF16 = jnp.float32, jnp.bfloat16
ROWS, FEAT, HID, HALF, RANK, DEPTH = 512, 640, 1792, 896, 64, 5120
SHARD = 112
TILE = 128
STEP = 2 * FEAT
NT = (((1,), (1,)), ((), ()))
LIGHT = pl.CostEstimate(flops=1 << 20, bytes_accessed=1 << 16, transcendentals=0)
ANY = pl.BlockSpec(memory_space=pl.ANY)


def send(value, target, name="send"):
    def line(z, x, y, c):
        return ((z % 4 * 4 + x % 4) * 4 + y % 4) * 2 + c

    pairs = [
        (line(z, x, y, c), line(*target(z, x, y, c)))
        for z in range(4)
        for x in range(4)
        for y in range(4)
        for c in range(2)
    ]
    with jax.named_scope(name):
        return lax.ppermute(value, AXES, pairs)


def up_y(v, name="up"):
    return send(v, lambda z, x, y, c: (z, x, y + 1, c), name)


def down_y(v, name="down"):
    return send(v, lambda z, x, y, c: (z, x, y - 1, c), name)


def along_y(v, way, name):
    return send(v, lambda z, x, y, c: (z, x, y + way * (1 - 2 * c), c), name)


def swap(v, name="swap"):
    return send(v, lambda z, x, y, c: (z, x, y, 1 - c), name)


def mate(v, name="mate"):
    return send(v, lambda z, x, y, c: (3 - z, x, y, c), name)


def after(value, *others):
    return lax.optimization_barrier((value, *others))[0]


def route(v, zero, one, name):
    hop = {
        "p": lambda z, x, y, c: (z ^ 1, x, y, c),
        "+": lambda z, x, y, c: (z, x + 1, y, c),
        "-": lambda z, x, y, c: (z, x - 1, y, c),
    }
    return send(v, lambda z, x, y, c: hop[zero if c == 0 else one](z, x, y, c), name)


def slots(z, x, c):
    zl, first = z % 2, c == 0

    def at(dz, dx):
        return (zl + dz) % 2 * 4 + (x + dx) % 4

    held = jnp.stack(
        [
            at(0, 0),
            at(0, 3),
            jnp.where(first, at(1, 0), at(0, 1)),
            jnp.where(first, at(0, 1), at(1, 0)),
            jnp.where(first, at(1, 3), at(1, 1)),
            jnp.where(first, at(0, 2), at(1, 3)),
            jnp.where(first, at(1, 1), at(0, 2)),
            at(1, 2),
        ]
    )
    shard = jnp.arange(8)
    return jnp.sum(jnp.where(held[None, :] == shard[:, None], shard[None, :], 0), axis=1)


def product_kernel(shards, where_ref, *refs):
    mine, near, far, weights = refs[:4], refs[4], refs[5], refs[6 : 6 + shards]
    out_ref, *acc = refs[6 + shards :]
    acc = acc[0] if acc else out_ref
    y, c = where_ref[16], where_ref[17]
    for step, shift in enumerate((0, 3 - 2 * c, 1 + 2 * c, 2)):
        first = lax.rem(y + shift, 4) * STEP
        lane, swapped = (pl.multiple_of(first + core * FEAT, 128) for core in (c, 1 - c))
        other = near[step * ROWS : step * ROWS + ROWS, :] if step < 3 else far[...]
        left = jnp.concatenate([mine[step][...], other], axis=1)
        rows = []
        for k, w in enumerate(weights):
            rows.append(
                jnp.concatenate([w[:, pl.ds(lane, FEAT)], w[:, pl.ds(swapped, FEAT)]], axis=1)
            )
            if shards > 1:
                rows.append(jnp.zeros((128 - SHARD, STEP), BF16))
        right = jnp.concatenate(rows, axis=0) if shards > 1 else rows[0]
        part = lax.dot_general(left, right, NT, preferred_element_type=F32)
        if step == 0:
            acc[:, : part.shape[1]] = part
        elif step < 3:
            acc[:, : part.shape[1]] += part
        else:
            out_ref[:, : part.shape[1]] = (acc[:, : part.shape[1]] + part).astype(out_ref.dtype)


def product(dtype, where, mine, other, weights):
    shards = len(weights)
    width = shards * 128
    vmem = pl.BlockSpec(memory_space=pltpu.VMEM)
    return pl.pallas_call(
        functools.partial(product_kernel, shards),
        out_shape=jax.ShapeDtypeStruct((ROWS, width), dtype),
        in_specs=[pl.BlockSpec(memory_space=pltpu.SMEM)] + [vmem] * (6 + shards),
        out_specs=vmem,
        scratch_shapes=[] if dtype == F32 else [pltpu.VMEM((ROWS, width), F32)],
        compiler_params=pltpu.CompilerParams(
            vmem_limit_bytes=(6 << 20) + width * (4 * STEP + 14 * ROWS)
        ),
        cost_estimate=LIGHT,
        name="product",
    )(where, *mine, *other, *weights)


def early_kernel(where_ref, act_ref, grad_ref, pm_ref, gate_ref, up_ref, ph_ref, out_ref):
    gate, up = gate_ref[...].astype(F32), up_ref[...].astype(F32)
    hidden = (gate * jax.nn.sigmoid(gate) * up).astype(BF16)
    pm = pm_ref[...]
    out_ref[:, 0:64] = lax.dot_general(act_ref[...], pm, NT, preferred_element_type=F32)
    out_ref[:, 64:128] = lax.dot_general(hidden, ph_ref[...], NT, preferred_element_type=F32)
    out_ref[:, 128:192] = lax.dot_general(grad_ref[...], pm, NT, preferred_element_type=F32)


def early(where, activations, out_grad, pm_t, gate, up, ph_t):
    narrow = pl.BlockSpec((128, FEAT), lambda i, w: (i, 0))
    wide = pl.BlockSpec((128, HID), lambda i, w: (i, 0))
    return pl.pallas_call(
        early_kernel,
        out_shape=jax.ShapeDtypeStruct((ROWS, 3 * RANK), F32),
        grid_spec=pltpu.PrefetchScalarGridSpec(
            num_scalar_prefetch=1,
            grid=(4,),
            in_specs=[
                narrow,
                narrow,
                pl.BlockSpec((RANK, FEAT), lambda i, w: (0, 2 * w[16] + w[17])),
                wide,
                wide,
                pl.BlockSpec((RANK, HID), lambda i, w: (0, 0)),
            ],
            out_specs=pl.BlockSpec((128, 3 * RANK), lambda i, w: (i, 0)),
        ),
        compiler_params=pltpu.CompilerParams(vmem_limit_bytes=12 << 20),
        cost_estimate=LIGHT,
        name="early",
    )(where, activations, out_grad, pm_t, gate, up, ph_t)


def grads(where_ref, base, h_refs, held, gate_ref, up_ref, ph_ref, gg_ref, gu_ref):
    at = 0
    for h_ref in h_refs:
        width = h_ref.shape[1]
        held[:, at : at + width] = h_ref[...].astype(F32)
        at += width
    hidden_grad = jnp.concatenate(
        [
            held[:, pl.ds(pl.multiple_of(where_ref[base + i] * 128, 128), 128)][:, :SHARD]
            for i in range(8)
        ],
        axis=1,
    )
    row = pl.program_id(0) * TILE + lax.broadcasted_iota(jnp.int32, hidden_grad.shape, 0)
    hidden_grad = jnp.where(row < where_ref[19], hidden_grad, 0.0)
    gate, up = gate_ref[...].astype(F32), up_ref[...].astype(F32)
    sig = jax.nn.sigmoid(gate)
    grad_up = (hidden_grad * (gate * sig)).astype(BF16)
    grad_gate = (hidden_grad * up * sig * (1.0 + gate * (1.0 - sig))).astype(BF16)
    gg_ref[...] = grad_gate
    gu_ref[...] = grad_up
    both = jnp.concatenate([grad_gate, grad_up], axis=0)
    part = lax.dot_general(both, ph_ref[...], NT, preferred_element_type=F32)
    return jnp.concatenate([part[:TILE], part[TILE:]], axis=1)


def own_kernel(n, where_ref, gate_ref, up_ref, ph_ref, *refs):
    gg_ref, gu_ref, part_ref, held = refs[n:]
    part_ref[...] = grads(
        where_ref, 0, refs[:n], held, gate_ref, up_ref, ph_ref, gg_ref, gu_ref
    )


def row_tiles(half):
    tile = pl.BlockSpec((TILE, HALF), lambda i, w: (i, half(w)))
    return tile, pl.BlockSpec((RANK, HALF), lambda i, w: (0, half(w)))


def pieces_of(h):
    return [pl.BlockSpec((TILE, p.shape[1]), lambda i, w: (i, 0)) for p in h]


BIG = jax.ShapeDtypeStruct((ROWS, HID), BF16)


def own_half(where, gate, up, h, ph_t):
    tile, ranks = row_tiles(lambda w: w[18])
    return pl.pallas_call(
        functools.partial(own_kernel, len(h)),
        out_shape=(BIG, BIG, jax.ShapeDtypeStruct((ROWS, 2 * RANK), F32)),
        grid_spec=pltpu.PrefetchScalarGridSpec(
            num_scalar_prefetch=1,
            grid=(ROWS // TILE,),
            in_specs=[tile, tile, ranks] + pieces_of(h),
            out_specs=(tile, tile, pl.BlockSpec((TILE, 2 * RANK), lambda i, w: (i, 0))),
            scratch_shapes=[pltpu.VMEM((TILE, 1024), F32)],
        ),
        compiler_params=pltpu.CompilerParams(vmem_limit_bytes=14 << 20),
        cost_estimate=LIGHT,
        name="own_half",
    )(where, gate, up, ph_t, *h)


def other_kernel(n, where_ref, gate_ref, up_ref, ph_ref, part_ref, hi_ref, lo_ref,
                 gg_in, gu_in, *refs):
    gg_ref, gu_ref, feat_ref, held, acc = refs[n:]
    i = pl.program_id(0)
    part = grads(where_ref, 8, refs[:n], held, gate_ref, up_ref, ph_ref, gg_ref, gu_ref)
    acc[pl.ds(pl.multiple_of(i * TILE, TILE), TILE), :] = part_ref[...] + part

    @pl.when(i == ROWS // TILE - 1)
    def _():
        feat_ref[...] = twice(hi_ref[...], lo_ref[...], acc[...])


def parted(value):
    hi = value.astype(BF16)
    return hi, (value - hi.astype(F32)).astype(BF16)


def twice(hi, lo, right):
    right_hi, right_lo = parted(right)
    total = jnp.dot(lo, right_hi, preferred_element_type=F32)
    total += jnp.dot(hi, right_lo, preferred_element_type=F32)
    return total + jnp.dot(hi, right_hi, preferred_element_type=F32)


def other_half(where, gate, up, h, ph_t, part, spread, gg, gu):
    tile, ranks = row_tiles(lambda w: 1 - w[18])
    feat = pl.BlockSpec((4 * RANK, 2 * RANK), lambda i, w: (0, 0))
    spreads = pl.BlockSpec((4 * RANK, ROWS), lambda i, w: (0, 0))
    return pl.pallas_call(
        functools.partial(other_kernel, len(h)),
        out_shape=(BIG, BIG, jax.ShapeDtypeStruct((4 * RANK, 2 * RANK), F32)),
        grid_spec=pltpu.PrefetchScalarGridSpec(
            num_scalar_prefetch=1,
            grid=(ROWS // TILE,),
            in_specs=[
                tile,
                tile,
                ranks,
                pl.BlockSpec((TILE, 2 * RANK), lambda i, w: (i, 0)),
                spreads,
                spreads,
                ANY,
                ANY,
            ]
            + pieces_of(h),
            out_specs=(tile, tile, feat),
            scratch_shapes=[pltpu.VMEM((TILE, 1024), F32), pltpu.VMEM((ROWS, 2 * RANK), F32)],
        ),
        input_output_aliases={7: 0, 8: 1},
        compiler_params=pltpu.CompilerParams(vmem_limit_bytes=14 << 20),
        cost_estimate=LIGHT,
        name="other_half",
    )(where, gate, up, ph_t, part, *spread, gg, gu, *h)


def spread_kernel(where_ref, sums_ref, hi_ref, lo_ref, feat_ref):
    sums = sums_ref[...]
    left = sums[:, : 2 * RANK].T
    right = sums[:, 2 * RANK :]
    row = lax.broadcasted_iota(jnp.int32, (1, ROWS), 1)
    start = jnp.int32(0)
    for s in range(4):
        length = where_ref[20 + s]
        member = jnp.logical_and(row >= start, row < start + length).astype(F32)
        weight = member / jnp.sqrt(jnp.broadcast_to(length, (1, ROWS)).astype(F32))
        hi, lo = parted(left[:RANK] * weight)
        at = pl.ds(s * RANK, RANK)
        hi_ref[at, :] = hi
        lo_ref[at, :] = lo
        feat_ref[at, :] = twice(*parted(left[RANK:] * weight), right)
        start += length


def spread_features(where, sums):
    vmem = pl.BlockSpec(memory_space=pltpu.VMEM)
    side = jax.ShapeDtypeStruct((4 * RANK, ROWS), BF16)
    return pl.pallas_call(
        spread_kernel,
        out_shape=(side, side, jax.ShapeDtypeStruct((4 * RANK, RANK), F32)),
        in_specs=[pl.BlockSpec(memory_space=pltpu.SMEM), vmem],
        out_specs=(vmem, vmem, vmem),
        compiler_params=pltpu.CompilerParams(vmem_limit_bytes=8 << 20),
        name="spread",
    )(where, sums)


def sum_tensor(value, c):
    half = value.shape[0] // 2
    top, low = value[:half], value[half:]
    mine = jnp.where(c == 0, top, low) + swap(jnp.where(c == 0, low, top))
    across = send(mine, lambda z, x, y, c: (z, x, y + 2, c))
    mine = (mine + across) + (up_y(mine) + down_y(mine))
    theirs = swap(mine)
    return jnp.concatenate(
        [jnp.where(c == 0, mine, theirs), jnp.where(c == 0, theirs, mine)], axis=0
    )


def on_device(
    activations, out_grad, gate_pre, up_pre, down_weight, proj_model, proj_hidden, lengths
):
    z, x, y, c = (lax.axis_index(a) for a in AXES)
    where = jnp.concatenate(
        [
            slots(z, x, c),
            slots(3 - z, x, c),
            jnp.stack([y, c, z // 2, jnp.sum(lengths)]),
            lengths,
        ]
    ).astype(jnp.int32)
    pm_t, ph_t = proj_model.T, proj_hidden.T
    own_w = down_weight
    theirs = mate(out_grad, "mate_rows")
    a1, a2 = along_y(out_grad, 1, "a1"), along_y(out_grad, -1, "a2")
    r1 = route(own_w, "+", "+", "r1")
    r2 = route(own_w, "p", "-", "r2")
    parts = early(where, activations, out_grad, pm_t, gate_pre, up_pre, ph_t)
    theirs, a1, a2, again, parts, where = lax.optimization_barrier(
        (theirs, a1, a2, own_w, parts, where)
    )
    r3 = route(again, "-", "p", "r3")
    b1, b2 = along_y(theirs, 1, "b1"), along_y(theirs, -1, "b2")
    r1, r2, r3, b1, b2 = lax.optimization_barrier((r1, r2, r3, b1, b2))
    r6 = route(r2, "-", "-", "r6")
    r4 = route(r2, "+", "p", "r4")
    r5 = route(r1, "+", "p", "r5")
    b_far = along_y(b1, 1, "b_far")
    b_other = [swap(jnp.concatenate([theirs, b2, b1]), "b_swap"), swap(b_far, "b_swap")]
    a_far = along_y(after(a1, b_far), 1, "a_far")
    b_mine = [theirs, b1, b2, b_far]
    h1 = product(BF16, after(where, r4, r5, r6, a_far), b_mine, b_other, [own_w, r1, r2, r3])
    r7 = route(r6, "-", "p", "r7")
    h1_in = mate(h1, "mate_grad1")
    h2 = product(BF16, after(where, h1), b_mine, b_other, [r4, r5, r6])
    h2_in = mate(h2, "mate_grad2")
    a_mine = [out_grad, a1, a2, a_far]
    near = jnp.concatenate([out_grad, a2, a1])
    a_other = [swap(after(near, h1), "a_swap"), swap(a_far, "a_swap")]
    own1 = product(F32, after(where, h2, h1_in), a_mine, a_other, [own_w, r1, r2, r3, r4, r5, r6])
    sums = sum_tensor(after(parts, own1), c)
    h3 = product(BF16, after(where, h2, own1), b_mine, b_other, [r7])
    own2 = product(F32, after(where, h3, h2_in), a_mine, a_other, [r7])
    h_in = [h1_in, h2_in, mate(h3, "mate_grad3")]
    grad_gate, grad_up, part = own_half(where, gate_pre, up_pre, (own1, own2), ph_t)
    *spread, down_feat = spread_features(after(where, part), sums)
    grad_gate, grad_up, feat = other_half(
        where, gate_pre, up_pre, h_in, ph_t, part, spread, grad_gate, grad_up
    )
    total = jnp.concatenate([sum_tensor(feat, c), down_feat], axis=1)
    features = total.reshape(4, RANK, 3, RANK).transpose(0, 2, 1, 3).reshape(4, 3, RANK * RANK)
    return grad_gate, grad_up, features


def solution(mesh):
    split = Mesh(mesh.devices.reshape(4, 4, 4, 2), AXES)
    dp, tensor = ("z", "x"), ("y", "c")
    return jax.shard_map(
        on_device,
        mesh=split,
        in_specs=(
            P(dp, tensor),
            P(dp, tensor),
            P(dp, tensor),
            P(dp, tensor),
            P((*tensor, *dp), None),
            P(),
            P(tensor, None),
            P(dp),
        ),
        out_specs=(P(dp, tensor), P(dp, tensor), P(dp, None, None)),
        check_vma=False,
    )
```

```python
import functools

import jax
import jax.numpy as jnp
from jax import lax
from jax.experimental import pallas as pl
from jax.experimental.pallas import tpu as pltpu
from jax.sharding import Mesh
from jax.sharding import PartitionSpec as P

AXES = ("z", "x", "y", "c")
F32, BF16 = jnp.float32, jnp.bfloat16
ROWS, FEAT, HID, HALF, RANK, DEPTH = 512, 640, 1792, 896, 64, 5120
SHARD = 112
TILE = 128
STEP = 2 * FEAT
NT = (((1,), (1,)), ((), ()))
LIGHT = pl.CostEstimate(flops=1 << 20, bytes_accessed=1 << 16, transcendentals=0)
ANY = pl.BlockSpec(memory_space=pl.ANY)


def send(value, target, name="send"):
    def line(z, x, y, c):
        return ((z % 4 * 4 + x % 4) * 4 + y % 4) * 2 + c

    pairs = [
        (line(z, x, y, c), line(*target(z, x, y, c)))
        for z in range(4)
        for x in range(4)
        for y in range(4)
        for c in range(2)
    ]
    with jax.named_scope(name):
        return lax.ppermute(value, AXES, pairs)


def up_y(v, name="up"):
    return send(v, lambda z, x, y, c: (z, x, y + 1, c), name)


def down_y(v, name="down"):
    return send(v, lambda z, x, y, c: (z, x, y - 1, c), name)


def along_y(v, way, name):
    return send(v, lambda z, x, y, c: (z, x, y + way * (1 - 2 * c), c), name)


def swap(v, name="swap"):
    return send(v, lambda z, x, y, c: (z, x, y, 1 - c), name)


def mate(v, name="mate"):
    return send(v, lambda z, x, y, c: (3 - z, x, y, c), name)


def after(value, *others):
    return lax.optimization_barrier((value, *others))[0]


def route(v, zero, one, name):
    hop = {
        "p": lambda z, x, y, c: (z ^ 1, x, y, c),
        "+": lambda z, x, y, c: (z, x + 1, y, c),
        "-": lambda z, x, y, c: (z, x - 1, y, c),
    }
    return send(v, lambda z, x, y, c: hop[zero if c == 0 else one](z, x, y, c), name)


def slots(z, x, c):
    zl, first = z % 2, c == 0

    def at(dz, dx):
        return (zl + dz) % 2 * 4 + (x + dx) % 4

    held = jnp.stack(
        [
            at(0, 0),
            at(0, 3),
            jnp.where(first, at(1, 0), at(0, 1)),
            jnp.where(first, at(0, 1), at(1, 0)),
            jnp.where(first, at(1, 3), at(1, 1)),
            jnp.where(first, at(0, 2), at(1, 3)),
            jnp.where(first, at(1, 1), at(0, 2)),
            at(1, 2),
        ]
    )
    shard = jnp.arange(8)
    return jnp.sum(jnp.where(held[None, :] == shard[:, None], shard[None, :], 0), axis=1)


def product_kernel(shards, where_ref, *refs):
    mine, near, far, weights = refs[:4], refs[4], refs[5], refs[6 : 6 + shards]
    out_ref, *acc = refs[6 + shards :]
    acc = acc[0] if acc else out_ref
    y, c = where_ref[16], where_ref[17]
    for step, shift in enumerate((0, 3 - 2 * c, 1 + 2 * c, 2)):
        first = lax.rem(y + shift, 4) * STEP
        lane, swapped = (pl.multiple_of(first + core * FEAT, 128) for core in (c, 1 - c))
        other = near[step * ROWS : step * ROWS + ROWS, :] if step < 3 else far[...]
        left = jnp.concatenate([mine[step][...], other], axis=1)
        rows = []
        for k, w in enumerate(weights):
            rows.append(
                jnp.concatenate([w[:, pl.ds(lane, FEAT)], w[:, pl.ds(swapped, FEAT)]], axis=1)
            )
            if shards > 1:
                rows.append(jnp.zeros((128 - SHARD, STEP), BF16))
        right = jnp.concatenate(rows, axis=0) if shards > 1 else rows[0]
        part = lax.dot_general(left, right, NT, preferred_element_type=F32)
        if step == 0:
            acc[:, : part.shape[1]] = part
        elif step < 3:
            acc[:, : part.shape[1]] += part
        else:
            out_ref[:, : part.shape[1]] = (acc[:, : part.shape[1]] + part).astype(out_ref.dtype)


def product(dtype, where, mine, other, weights):
    shards = len(weights)
    width = shards * 128
    vmem = pl.BlockSpec(memory_space=pltpu.VMEM)
    return pl.pallas_call(
        functools.partial(product_kernel, shards),
        out_shape=jax.ShapeDtypeStruct((ROWS, width), dtype),
        in_specs=[pl.BlockSpec(memory_space=pltpu.SMEM)] + [vmem] * (6 + shards),
        out_specs=vmem,
        scratch_shapes=[] if dtype == F32 else [pltpu.VMEM((ROWS, width), F32)],
        compiler_params=pltpu.CompilerParams(
            vmem_limit_bytes=(6 << 20) + width * (4 * STEP + 14 * ROWS)
        ),
        cost_estimate=LIGHT,
        name="product",
    )(where, *mine, *other, *weights)


def early_kernel(where_ref, act_ref, grad_ref, pm_ref, gate_ref, up_ref, ph_ref, out_ref):
    gate, up = gate_ref[...].astype(F32), up_ref[...].astype(F32)
    hidden = (gate * jax.nn.sigmoid(gate) * up).astype(BF16)
    pm = pm_ref[...]
    out_ref[:, 0:64] = lax.dot_general(act_ref[...], pm, NT, preferred_element_type=F32)
    out_ref[:, 64:128] = lax.dot_general(hidden, ph_ref[...], NT, preferred_element_type=F32)
    out_ref[:, 128:192] = lax.dot_general(grad_ref[...], pm, NT, preferred_element_type=F32)


def early(where, activations, out_grad, pm_t, gate, up, ph_t):
    narrow = pl.BlockSpec((128, FEAT), lambda i, w: (i, 0))
    wide = pl.BlockSpec((128, HID), lambda i, w: (i, 0))
    return pl.pallas_call(
        early_kernel,
        out_shape=jax.ShapeDtypeStruct((ROWS, 3 * RANK), F32),
        grid_spec=pltpu.PrefetchScalarGridSpec(
            num_scalar_prefetch=1,
            grid=(4,),
            in_specs=[
                narrow,
                narrow,
                pl.BlockSpec((RANK, FEAT), lambda i, w: (0, 2 * w[16] + w[17])),
                wide,
                wide,
                pl.BlockSpec((RANK, HID), lambda i, w: (0, 0)),
            ],
            out_specs=pl.BlockSpec((128, 3 * RANK), lambda i, w: (i, 0)),
        ),
        compiler_params=pltpu.CompilerParams(vmem_limit_bytes=12 << 20),
        cost_estimate=LIGHT,
        name="early",
    )(where, activations, out_grad, pm_t, gate, up, ph_t)


def grads(where_ref, base, h_refs, held, gate_ref, up_ref, ph_ref, gg_ref, gu_ref):
    at = 0
    for h_ref in h_refs:
        width = h_ref.shape[1]
        held[:, at : at + width] = h_ref[...].astype(F32)
        at += width
    hidden_grad = jnp.concatenate(
        [
            held[:, pl.ds(pl.multiple_of(where_ref[base + i] * 128, 128), 128)][:, :SHARD]
            for i in range(8)
        ],
        axis=1,
    )
    row = pl.program_id(0) * TILE + lax.broadcasted_iota(jnp.int32, hidden_grad.shape, 0)
    hidden_grad = jnp.where(row < where_ref[19], hidden_grad, 0.0)
    gate, up = gate_ref[...].astype(F32), up_ref[...].astype(F32)
    sig = jax.nn.sigmoid(gate)
    grad_up = (hidden_grad * (gate * sig)).astype(BF16)
    grad_gate = (hidden_grad * up * sig * (1.0 + gate * (1.0 - sig))).astype(BF16)
    gg_ref[...] = grad_gate
    gu_ref[...] = grad_up
    both = jnp.concatenate([grad_gate, grad_up], axis=0)
    part = lax.dot_general(both, ph_ref[...], NT, preferred_element_type=F32)
    return jnp.concatenate([part[:TILE], part[TILE:]], axis=1)


def own_kernel(n, where_ref, gate_ref, up_ref, ph_ref, *refs):
    gg_ref, gu_ref, part_ref, held = refs[n:]
    part_ref[...] = grads(
        where_ref, 0, refs[:n], held, gate_ref, up_ref, ph_ref, gg_ref, gu_ref
    )


def row_tiles(half):
    tile = pl.BlockSpec((TILE, HALF), lambda i, w: (i, half(w)))
    return tile, pl.BlockSpec((RANK, HALF), lambda i, w: (0, half(w)))


def pieces_of(h):
    return [pl.BlockSpec((TILE, p.shape[1]), lambda i, w: (i, 0)) for p in h]


BIG = jax.ShapeDtypeStruct((ROWS, HID), BF16)


def own_half(where, gate, up, h, ph_t):
    tile, ranks = row_tiles(lambda w: w[18])
    return pl.pallas_call(
        functools.partial(own_kernel, len(h)),
        out_shape=(BIG, BIG, jax.ShapeDtypeStruct((ROWS, 2 * RANK), F32)),
        grid_spec=pltpu.PrefetchScalarGridSpec(
            num_scalar_prefetch=1,
            grid=(ROWS // TILE,),
            in_specs=[tile, tile, ranks] + pieces_of(h),
            out_specs=(tile, tile, pl.BlockSpec((TILE, 2 * RANK), lambda i, w: (i, 0))),
            scratch_shapes=[pltpu.VMEM((TILE, 1024), F32)],
        ),
        compiler_params=pltpu.CompilerParams(vmem_limit_bytes=14 << 20),
        cost_estimate=LIGHT,
        name="own_half",
    )(where, gate, up, ph_t, *h)


def other_kernel(n, where_ref, gate_ref, up_ref, ph_ref, part_ref, hi_ref, lo_ref,
                 gg_in, gu_in, *refs):
    gg_ref, gu_ref, feat_ref, held, acc = refs[n:]
    i = pl.program_id(0)
    part = grads(where_ref, 8, refs[:n], held, gate_ref, up_ref, ph_ref, gg_ref, gu_ref)
    acc[pl.ds(pl.multiple_of(i * TILE, TILE), TILE), :] = part_ref[...] + part

    @pl.when(i == ROWS // TILE - 1)
    def _():
        feat_ref[...] = twice(hi_ref[...], lo_ref[...], acc[...])


def parted(value):
    hi = value.astype(BF16)
    return hi, (value - hi.astype(F32)).astype(BF16)


def twice(hi, lo, right):
    right_hi, right_lo = parted(right)
    total = jnp.dot(lo, right_hi, preferred_element_type=F32)
    total += jnp.dot(hi, right_lo, preferred_element_type=F32)
    return total + jnp.dot(hi, right_hi, preferred_element_type=F32)


def other_half(where, gate, up, h, ph_t, part, spread, gg, gu):
    tile, ranks = row_tiles(lambda w: 1 - w[18])
    feat = pl.BlockSpec((4 * RANK, 2 * RANK), lambda i, w: (0, 0))
    spreads = pl.BlockSpec((4 * RANK, ROWS), lambda i, w: (0, 0))
    return pl.pallas_call(
        functools.partial(other_kernel, len(h)),
        out_shape=(BIG, BIG, jax.ShapeDtypeStruct((4 * RANK, 2 * RANK), F32)),
        grid_spec=pltpu.PrefetchScalarGridSpec(
            num_scalar_prefetch=1,
            grid=(ROWS // TILE,),
            in_specs=[
                tile,
                tile,
                ranks,
                pl.BlockSpec((TILE, 2 * RANK), lambda i, w: (i, 0)),
                spreads,
                spreads,
                ANY,
                ANY,
            ]
            + pieces_of(h),
            out_specs=(tile, tile, feat),
            scratch_shapes=[pltpu.VMEM((TILE, 1024), F32), pltpu.VMEM((ROWS, 2 * RANK), F32)],
        ),
        input_output_aliases={7: 0, 8: 1},
        compiler_params=pltpu.CompilerParams(vmem_limit_bytes=14 << 20),
        cost_estimate=LIGHT,
        name="other_half",
    )(where, gate, up, ph_t, part, *spread, gg, gu, *h)


def spread_kernel(where_ref, sums_ref, hi_ref, lo_ref, feat_ref):
    sums = sums_ref[...]
    left = sums[:, : 2 * RANK].T
    right = sums[:, 2 * RANK :]
    row = lax.broadcasted_iota(jnp.int32, (1, ROWS), 1)
    start = jnp.int32(0)
    for s in range(4):
        length = where_ref[20 + s]
        member = jnp.logical_and(row >= start, row < start + length).astype(F32)
        weight = member / jnp.sqrt(jnp.broadcast_to(length, (1, ROWS)).astype(F32))
        hi, lo = parted(left[:RANK] * weight)
        at = pl.ds(s * RANK, RANK)
        hi_ref[at, :] = hi
        lo_ref[at, :] = lo
        feat_ref[at, :] = twice(*parted(left[RANK:] * weight), right)
        start += length


def spread_features(where, sums):
    vmem = pl.BlockSpec(memory_space=pltpu.VMEM)
    side = jax.ShapeDtypeStruct((4 * RANK, ROWS), BF16)
    return pl.pallas_call(
        spread_kernel,
        out_shape=(side, side, jax.ShapeDtypeStruct((4 * RANK, RANK), F32)),
        in_specs=[pl.BlockSpec(memory_space=pltpu.SMEM), vmem],
        out_specs=(vmem, vmem, vmem),
        compiler_params=pltpu.CompilerParams(vmem_limit_bytes=8 << 20),
        name="spread",
    )(where, sums)


def sum_tensor(value, c):
    half = value.shape[0] // 2
    top, low = value[:half], value[half:]
    mine = jnp.where(c == 0, top, low) + swap(jnp.where(c == 0, low, top))
    across = send(mine, lambda z, x, y, c: (z, x, y + 2, c))
    mine = (mine + across) + (up_y(mine) + down_y(mine))
    theirs = swap(mine)
    return jnp.concatenate(
        [jnp.where(c == 0, mine, theirs), jnp.where(c == 0, theirs, mine)], axis=0
    )


def on_device(
    activations, out_grad, gate_pre, up_pre, down_weight, proj_model, proj_hidden, lengths
):
    z, x, y, c = (lax.axis_index(a) for a in AXES)
    where = jnp.concatenate(
        [
            slots(z, x, c),
            slots(3 - z, x, c),
            jnp.stack([y, c, z // 2, jnp.sum(lengths)]),
            lengths,
        ]
    ).astype(jnp.int32)
    pm_t, ph_t = proj_model.T, proj_hidden.T
    own_w = down_weight
    theirs = mate(out_grad, "mate_rows")
    a1, a2 = along_y(out_grad, 1, "a1"), along_y(out_grad, -1, "a2")
    r1 = route(own_w, "+", "+", "r1")
    r2 = route(own_w, "p", "-", "r2")
    parts = early(where, activations, out_grad, pm_t, gate_pre, up_pre, ph_t)
    theirs, a1, a2, again, parts, where = lax.optimization_barrier(
        (theirs, a1, a2, own_w, parts, where)
    )
    r3 = route(again, "-", "p", "r3")
    b1, b2 = along_y(theirs, 1, "b1"), along_y(theirs, -1, "b2")
    r1, r2, r3, b1, b2 = lax.optimization_barrier((r1, r2, r3, b1, b2))
    r6 = route(r2, "-", "-", "r6")
    r4 = route(r2, "+", "p", "r4")
    r5 = route(r1, "+", "p", "r5")
    b_far = along_y(b1, 1, "b_far")
    b_other = [swap(jnp.concatenate([theirs, b2, b1]), "b_swap"), swap(b_far, "b_swap")]
    a_far = along_y(after(a1, b_far), 1, "a_far")
    b_mine = [theirs, b1, b2, b_far]
    h1 = product(BF16, after(where, r4, r5, r6, a_far), b_mine, b_other, [own_w, r1, r2, r3])
    r7 = route(r6, "-", "p", "r7")
    h1_in = mate(h1, "mate_grad1")
    h2 = product(BF16, after(where, h1), b_mine, b_other, [r4, r5, r6])
    h2_in = mate(h2, "mate_grad2")
    a_mine = [out_grad, a1, a2, a_far]
    near = jnp.concatenate([out_grad, a2, a1])
    a_other = [swap(after(near, h1), "a_swap"), swap(a_far, "a_swap")]
    top, low = parts[:256], parts[256:]
    half = jnp.where(c == 0, top, low) + swap(after(jnp.where(c == 0, low, top), h1), "s_core")
    near_y = send(half, lambda z, x, y, c: (z, x, y ^ 1, c), "s_near")
    half += after(near_y, h2)
    far_y = send(half, lambda z, x, y, c: (z, x, y ^ 2, c), "s_far")
    own1 = product(F32, after(where, h2), a_mine, a_other, [own_w, r1, r2, r3, r4, r5, r6])
    half += after(far_y, own1)
    rest = swap(half, "s_core")
    h3 = product(BF16, after(where, h1_in, own1), b_mine, b_other, [r7])
    own2 = product(F32, after(where, h3, h2_in), a_mine, a_other, [r7])
    rest = after(rest, own2)
    sums = jnp.concatenate(
        [jnp.where(c == 0, half, rest), jnp.where(c == 0, rest, half)], axis=0
    )
    h_in = [h1_in, h2_in, mate(h3, "mate_grad3")]
    grad_gate, grad_up, part = own_half(where, gate_pre, up_pre, (own1, own2), ph_t)
    *spread, down_feat = spread_features(after(where, part), sums)
    grad_gate, grad_up, feat = other_half(
        where, gate_pre, up_pre, h_in, ph_t, part, spread, grad_gate, grad_up
    )
    total = jnp.concatenate([sum_tensor(feat, c), down_feat], axis=1)
    features = total.reshape(4, RANK, 3, RANK).transpose(0, 2, 1, 3).reshape(4, 3, RANK * RANK)
    return grad_gate, grad_up, features


def solution(mesh):
    split = Mesh(mesh.devices.reshape(4, 4, 4, 2), AXES)
    dp, tensor = ("z", "x"), ("y", "c")
    return jax.shard_map(
        on_device,
        mesh=split,
        in_specs=(
            P(dp, tensor),
            P(dp, tensor),
            P(dp, tensor),
            P(dp, tensor),
            P((*tensor, *dp), None),
            P(),
            P(tensor, None),
            P(dp),
        ),
        out_specs=(P(dp, tensor), P(dp, tensor), P(dp, None, None)),
        check_vma=False,
    )
```

```python
import functools

import jax
import jax.numpy as jnp
from jax import lax
from jax.experimental import pallas as pl
from jax.experimental.pallas import tpu as pltpu
from jax.sharding import Mesh
from jax.sharding import PartitionSpec as P

AXES = ("z", "x", "y", "c")
F32, BF16 = jnp.float32, jnp.bfloat16
ROWS, FEAT, HID, HALF, RANK, DEPTH = 512, 640, 1792, 896, 64, 5120
SHARD = 112
TILE = 128
STEP = 2 * FEAT
NT = (((1,), (1,)), ((), ()))
LIGHT = pl.CostEstimate(flops=1 << 20, bytes_accessed=1 << 16, transcendentals=0)
ANY = pl.BlockSpec(memory_space=pl.ANY)


def send(value, target, name="send"):
    def line(z, x, y, c):
        return ((z % 4 * 4 + x % 4) * 4 + y % 4) * 2 + c

    pairs = [
        (line(z, x, y, c), line(*target(z, x, y, c)))
        for z in range(4)
        for x in range(4)
        for y in range(4)
        for c in range(2)
    ]
    with jax.named_scope(name):
        return lax.ppermute(value, AXES, pairs)


def up_y(v, name="up"):
    return send(v, lambda z, x, y, c: (z, x, y + 1, c), name)


def down_y(v, name="down"):
    return send(v, lambda z, x, y, c: (z, x, y - 1, c), name)


def along_y(v, way, name):
    return send(v, lambda z, x, y, c: (z, x, y + way * (1 - 2 * c), c), name)


def swap(v, name="swap"):
    return send(v, lambda z, x, y, c: (z, x, y, 1 - c), name)


def mate(v, name="mate"):
    return send(v, lambda z, x, y, c: (3 - z, x, y, c), name)


def after(value, *others):
    return lax.optimization_barrier((value, *others))[0]


def route(v, zero, one, name):
    hop = {
        "p": lambda z, x, y, c: (z ^ 1, x, y, c),
        "+": lambda z, x, y, c: (z, x + 1, y, c),
        "-": lambda z, x, y, c: (z, x - 1, y, c),
    }
    return send(v, lambda z, x, y, c: hop[zero if c == 0 else one](z, x, y, c), name)


def slots(z, x, c):
    zl, first = z % 2, c == 0

    def at(dz, dx):
        return (zl + dz) % 2 * 4 + (x + dx) % 4

    held = jnp.stack(
        [
            at(0, 0),
            at(0, 3),
            jnp.where(first, at(1, 0), at(0, 1)),
            jnp.where(first, at(0, 1), at(1, 0)),
            jnp.where(first, at(1, 3), at(1, 1)),
            jnp.where(first, at(0, 2), at(1, 3)),
            jnp.where(first, at(1, 1), at(0, 2)),
            at(1, 2),
        ]
    )
    shard = jnp.arange(8)
    return jnp.sum(jnp.where(held[None, :] == shard[:, None], shard[None, :], 0), axis=1)


def product_kernel(shards, where_ref, *refs):
    mine, near, far, weights = refs[:4], refs[4], refs[5], refs[6 : 6 + shards]
    out_ref, *acc = refs[6 + shards :]
    acc = acc[0] if acc else out_ref
    y, c = where_ref[16], where_ref[17]
    for step, shift in enumerate((0, 3 - 2 * c, 1 + 2 * c, 2)):
        first = lax.rem(y + shift, 4) * STEP
        lane, swapped = (pl.multiple_of(first + core * FEAT, 128) for core in (c, 1 - c))
        other = near[step * ROWS : step * ROWS + ROWS, :] if step < 3 else far[...]
        left = jnp.concatenate([mine[step][...], other], axis=1)
        rows = []
        for k, w in enumerate(weights):
            rows.append(
                jnp.concatenate([w[:, pl.ds(lane, FEAT)], w[:, pl.ds(swapped, FEAT)]], axis=1)
            )
            if shards > 1:
                rows.append(jnp.zeros((128 - SHARD, STEP), BF16))
        right = jnp.concatenate(rows, axis=0) if shards > 1 else rows[0]
        part = lax.dot_general(left, right, NT, preferred_element_type=F32)
        if step == 0:
            acc[:, : part.shape[1]] = part
        elif step < 3:
            acc[:, : part.shape[1]] += part
        else:
            out_ref[:, : part.shape[1]] = (acc[:, : part.shape[1]] + part).astype(out_ref.dtype)


def product(dtype, where, mine, other, weights):
    shards = len(weights)
    width = shards * 128
    vmem = pl.BlockSpec(memory_space=pltpu.VMEM)
    return pl.pallas_call(
        functools.partial(product_kernel, shards),
        out_shape=jax.ShapeDtypeStruct((ROWS, width), dtype),
        in_specs=[pl.BlockSpec(memory_space=pltpu.SMEM)] + [vmem] * (6 + shards),
        out_specs=vmem,
        scratch_shapes=[] if dtype == F32 else [pltpu.VMEM((ROWS, width), F32)],
        compiler_params=pltpu.CompilerParams(
            vmem_limit_bytes=(6 << 20) + width * (4 * STEP + 14 * ROWS)
        ),
        cost_estimate=LIGHT,
        name="product",
    )(where, *mine, *other, *weights)


def early_kernel(where_ref, act_ref, grad_ref, pm_ref, gate_ref, up_ref, ph_ref, out_ref):
    gate, up = gate_ref[...].astype(F32), up_ref[...].astype(F32)
    hidden = (gate * jax.nn.sigmoid(gate) * up).astype(BF16)
    pm = pm_ref[...]
    out_ref[:, 0:64] = lax.dot_general(act_ref[...], pm, NT, preferred_element_type=F32)
    out_ref[:, 64:128] = lax.dot_general(hidden, ph_ref[...], NT, preferred_element_type=F32)
    out_ref[:, 128:192] = lax.dot_general(grad_ref[...], pm, NT, preferred_element_type=F32)


def early(where, activations, out_grad, pm_t, gate, up, ph_t):
    narrow = pl.BlockSpec((128, FEAT), lambda i, w: (i, 0))
    wide = pl.BlockSpec((128, HID), lambda i, w: (i, 0))
    return pl.pallas_call(
        early_kernel,
        out_shape=jax.ShapeDtypeStruct((ROWS, 3 * RANK), F32),
        grid_spec=pltpu.PrefetchScalarGridSpec(
            num_scalar_prefetch=1,
            grid=(4,),
            in_specs=[
                narrow,
                narrow,
                pl.BlockSpec((RANK, FEAT), lambda i, w: (0, 2 * w[16] + w[17])),
                wide,
                wide,
                pl.BlockSpec((RANK, HID), lambda i, w: (0, 0)),
            ],
            out_specs=pl.BlockSpec((128, 3 * RANK), lambda i, w: (i, 0)),
        ),
        compiler_params=pltpu.CompilerParams(vmem_limit_bytes=12 << 20),
        cost_estimate=LIGHT,
        name="early",
    )(where, activations, out_grad, pm_t, gate, up, ph_t)


def grads(where_ref, base, h_refs, held, gate_ref, up_ref, ph_ref, gg_ref, gu_ref):
    at = 0
    for h_ref in h_refs:
        width = h_ref.shape[1]
        held[:, at : at + width] = h_ref[...].astype(F32)
        at += width
    hidden_grad = jnp.concatenate(
        [
            held[:, pl.ds(pl.multiple_of(where_ref[base + i] * 128, 128), 128)][:, :SHARD]
            for i in range(8)
        ],
        axis=1,
    )
    row = pl.program_id(0) * TILE + lax.broadcasted_iota(jnp.int32, hidden_grad.shape, 0)
    hidden_grad = jnp.where(row < where_ref[19], hidden_grad, 0.0)
    gate, up = gate_ref[...].astype(F32), up_ref[...].astype(F32)
    sig = jax.nn.sigmoid(gate)
    grad_up = (hidden_grad * (gate * sig)).astype(BF16)
    grad_gate = (hidden_grad * up * sig * (1.0 + gate * (1.0 - sig))).astype(BF16)
    gg_ref[...] = grad_gate
    gu_ref[...] = grad_up
    both = jnp.concatenate([grad_gate, grad_up], axis=0)
    part = lax.dot_general(both, ph_ref[...], NT, preferred_element_type=F32)
    return jnp.concatenate([part[:TILE], part[TILE:]], axis=1)


def own_kernel(n, where_ref, gate_ref, up_ref, ph_ref, *refs):
    gg_ref, gu_ref, part_ref, held = refs[n:]
    part_ref[...] = grads(
        where_ref, 0, refs[:n], held, gate_ref, up_ref, ph_ref, gg_ref, gu_ref
    )


def row_tiles(half):
    tile = pl.BlockSpec((TILE, HALF), lambda i, w: (i, half(w)))
    return tile, pl.BlockSpec((RANK, HALF), lambda i, w: (0, half(w)))


def pieces_of(h):
    return [pl.BlockSpec((TILE, p.shape[1]), lambda i, w: (i, 0)) for p in h]


BIG = jax.ShapeDtypeStruct((ROWS, HID), BF16)


def own_half(where, gate, up, h, ph_t):
    tile, ranks = row_tiles(lambda w: w[18])
    return pl.pallas_call(
        functools.partial(own_kernel, len(h)),
        out_shape=(BIG, BIG, jax.ShapeDtypeStruct((ROWS, 2 * RANK), F32)),
        grid_spec=pltpu.PrefetchScalarGridSpec(
            num_scalar_prefetch=1,
            grid=(ROWS // TILE,),
            in_specs=[tile, tile, ranks] + pieces_of(h),
            out_specs=(tile, tile, pl.BlockSpec((TILE, 2 * RANK), lambda i, w: (i, 0))),
            scratch_shapes=[pltpu.VMEM((TILE, 1024), F32)],
        ),
        compiler_params=pltpu.CompilerParams(vmem_limit_bytes=14 << 20),
        cost_estimate=LIGHT,
        name="own_half",
    )(where, gate, up, ph_t, *h)


def other_kernel(n, where_ref, gate_ref, up_ref, ph_ref, part_ref, hi_ref, lo_ref,
                 gg_in, gu_in, *refs):
    gg_ref, gu_ref, feat_ref, held, acc = refs[n:]
    i = pl.program_id(0)
    part = grads(where_ref, 8, refs[:n], held, gate_ref, up_ref, ph_ref, gg_ref, gu_ref)
    acc[pl.ds(pl.multiple_of(i * TILE, TILE), TILE), :] = part_ref[...] + part

    @pl.when(i == ROWS // TILE - 1)
    def _():
        feat_ref[...] = twice(hi_ref[...], lo_ref[...], acc[...])


def parted(value):
    hi = value.astype(BF16)
    return hi, (value - hi.astype(F32)).astype(BF16)


def twice(hi, lo, right):
    right_hi, right_lo = parted(right)
    total = jnp.dot(lo, right_hi, preferred_element_type=F32)
    total += jnp.dot(hi, right_lo, preferred_element_type=F32)
    return total + jnp.dot(hi, right_hi, preferred_element_type=F32)


def other_half(where, gate, up, h, ph_t, part, spread, gg, gu):
    tile, ranks = row_tiles(lambda w: 1 - w[18])
    feat = pl.BlockSpec((4 * RANK, 2 * RANK), lambda i, w: (0, 0))
    spreads = pl.BlockSpec((4 * RANK, ROWS), lambda i, w: (0, 0))
    return pl.pallas_call(
        functools.partial(other_kernel, len(h)),
        out_shape=(BIG, BIG, jax.ShapeDtypeStruct((4 * RANK, 2 * RANK), F32)),
        grid_spec=pltpu.PrefetchScalarGridSpec(
            num_scalar_prefetch=1,
            grid=(ROWS // TILE,),
            in_specs=[
                tile,
                tile,
                ranks,
                pl.BlockSpec((TILE, 2 * RANK), lambda i, w: (i, 0)),
                spreads,
                spreads,
                ANY,
                ANY,
            ]
            + pieces_of(h),
            out_specs=(tile, tile, feat),
            scratch_shapes=[pltpu.VMEM((TILE, 1024), F32), pltpu.VMEM((ROWS, 2 * RANK), F32)],
        ),
        input_output_aliases={7: 0, 8: 1},
        compiler_params=pltpu.CompilerParams(vmem_limit_bytes=14 << 20),
        cost_estimate=LIGHT,
        name="other_half",
    )(where, gate, up, ph_t, part, *spread, gg, gu, *h)


def spread_kernel(where_ref, sums_ref, hi_ref, lo_ref, feat_ref):
    sums = sums_ref[...]
    left = sums[:, : 2 * RANK].T
    right = sums[:, 2 * RANK :]
    row = lax.broadcasted_iota(jnp.int32, (1, ROWS), 1)
    start = jnp.int32(0)
    for s in range(4):
        length = where_ref[20 + s]
        member = jnp.logical_and(row >= start, row < start + length).astype(F32)
        weight = member / jnp.sqrt(jnp.broadcast_to(length, (1, ROWS)).astype(F32))
        hi, lo = parted(left[:RANK] * weight)
        at = pl.ds(s * RANK, RANK)
        hi_ref[at, :] = hi
        lo_ref[at, :] = lo
        feat_ref[at, :] = twice(*parted(left[RANK:] * weight), right)
        start += length


def spread_features(where, sums):
    vmem = pl.BlockSpec(memory_space=pltpu.VMEM)
    side = jax.ShapeDtypeStruct((4 * RANK, ROWS), BF16)
    return pl.pallas_call(
        spread_kernel,
        out_shape=(side, side, jax.ShapeDtypeStruct((4 * RANK, RANK), F32)),
        in_specs=[pl.BlockSpec(memory_space=pltpu.SMEM), vmem],
        out_specs=(vmem, vmem, vmem),
        compiler_params=pltpu.CompilerParams(vmem_limit_bytes=8 << 20),
        name="spread",
    )(where, sums)


def sum_tensor(value, c):
    half = value.shape[0] // 2
    top, low = value[:half], value[half:]
    mine = jnp.where(c == 0, top, low) + swap(jnp.where(c == 0, low, top))
    across = send(mine, lambda z, x, y, c: (z, x, y + 2, c))
    mine = (mine + across) + (up_y(mine) + down_y(mine))
    theirs = swap(mine)
    return jnp.concatenate(
        [jnp.where(c == 0, mine, theirs), jnp.where(c == 0, theirs, mine)], axis=0
    )


def on_device(
    activations, out_grad, gate_pre, up_pre, down_weight, proj_model, proj_hidden, lengths
):
    z, x, y, c = (lax.axis_index(a) for a in AXES)
    where = jnp.concatenate(
        [
            slots(z, x, c),
            slots(3 - z, x, c),
            jnp.stack([y, c, z // 2, jnp.sum(lengths)]),
            lengths,
        ]
    ).astype(jnp.int32)
    pm_t, ph_t = proj_model.T, proj_hidden.T
    own_w = down_weight
    theirs = mate(out_grad, "mate_rows")
    a1, a2 = along_y(out_grad, 1, "a1"), along_y(out_grad, -1, "a2")
    r1 = route(own_w, "+", "+", "r1")
    r2 = route(own_w, "p", "-", "r2")
    theirs, a1, a2, again, where = lax.optimization_barrier((theirs, a1, a2, own_w, where))
    r3 = route(again, "-", "p", "r3")
    b1, b2 = along_y(theirs, 1, "b1"), along_y(theirs, -1, "b2")
    r1, r2, r3, b1, b2 = lax.optimization_barrier((r1, r2, r3, b1, b2))
    r6 = route(r2, "-", "-", "r6")
    r4 = route(r2, "+", "p", "r4")
    r5 = route(r1, "+", "p", "r5")
    b_far = along_y(b1, 1, "b_far")
    b_near = swap(jnp.concatenate([theirs, b2, b1]), "b_swap")
    b_other = [b_near, swap(after(b_far, b_near), "b_swap")]
    a_far = along_y(after(a1, b_far), 1, "a_far")
    parts = early(after(where, b_far), activations, out_grad, pm_t, gate_pre, up_pre, ph_t)
    top, low = parts[:256], parts[256:]
    core_sum = swap(after(jnp.where(c == 0, low, top), b_other[1]), "s_core")
    b_mine = [theirs, b1, b2, b_far]
    h1 = product(BF16, after(where, r4, r5, r6, a_far, parts), b_mine, b_other, [own_w, r1, r2, r3])
    r7 = route(r6, "-", "p", "r7")
    h1_in = mate(h1, "mate_grad1")
    h2 = product(BF16, after(where, h1), b_mine, b_other, [r4, r5, r6])
    h2_in = mate(h2, "mate_grad2")
    a_mine = [out_grad, a1, a2, a_far]
    near = jnp.concatenate([out_grad, a2, a1])
    a_other = [swap(after(near, h1), "a_swap"), swap(a_far, "a_swap")]
    half = jnp.where(c == 0, top, low) + after(core_sum, h2)
    near_y = send(half, lambda z, x, y, c: (z, x, y ^ 1, c), "s_near")
    own1 = product(F32, after(where, h2), a_mine, a_other, [own_w, r1, r2, r3, r4, r5, r6])
    half += after(near_y, own1)
    far_y = send(half, lambda z, x, y, c: (z, x, y ^ 2, c), "s_far")
    h3 = product(BF16, after(where, h1_in, own1), b_mine, b_other, [r7])
    own2 = product(F32, after(where, h3), a_mine, a_other, [r7])
    half += after(far_y, own2)
    rest = swap(half, "s_core")
    sums = jnp.concatenate(
        [jnp.where(c == 0, half, rest), jnp.where(c == 0, rest, half)], axis=0
    )
    h_in = [h1_in, h2_in, mate(h3, "mate_grad3")]
    grad_gate, grad_up, part = own_half(after(where, h2_in), gate_pre, up_pre, (own1, own2), ph_t)
    *spread, down_feat = spread_features(after(where, part, h_in[2]), sums)
    grad_gate, grad_up, feat = other_half(
        where, gate_pre, up_pre, h_in, ph_t, part, spread, grad_gate, grad_up
    )
    total = jnp.concatenate([sum_tensor(feat, c), down_feat], axis=1)
    features = total.reshape(4, RANK, 3, RANK).transpose(0, 2, 1, 3).reshape(4, 3, RANK * RANK)
    return grad_gate, grad_up, features


def solution(mesh):
    split = Mesh(mesh.devices.reshape(4, 4, 4, 2), AXES)
    dp, tensor = ("z", "x"), ("y", "c")
    return jax.shard_map(
        on_device,
        mesh=split,
        in_specs=(
            P(dp, tensor),
            P(dp, tensor),
            P(dp, tensor),
            P(dp, tensor),
            P((*tensor, *dp), None),
            P(),
            P(tensor, None),
            P(dp),
        ),
        out_specs=(P(dp, tensor), P(dp, tensor), P(dp, None, None)),
        check_vma=False,
    )
```

```python
import functools

import jax
import jax.numpy as jnp
from jax import lax
from jax.experimental import pallas as pl
from jax.experimental.pallas import tpu as pltpu
from jax.sharding import Mesh
from jax.sharding import PartitionSpec as P

AXES = ("z", "x", "y", "c")
F32, BF16 = jnp.float32, jnp.bfloat16
ROWS, FEAT, HID, HALF, RANK, DEPTH = 512, 640, 1792, 896, 64, 5120
SHARD = 112
TILE = 128
STEP = 2 * FEAT
NT = (((1,), (1,)), ((), ()))
LIGHT = pl.CostEstimate(flops=1 << 20, bytes_accessed=1 << 16, transcendentals=0)
ANY = pl.BlockSpec(memory_space=pl.ANY)


def send(value, target, name="send"):
    def line(z, x, y, c):
        return ((z % 4 * 4 + x % 4) * 4 + y % 4) * 2 + c

    pairs = [
        (line(z, x, y, c), line(*target(z, x, y, c)))
        for z in range(4)
        for x in range(4)
        for y in range(4)
        for c in range(2)
    ]
    with jax.named_scope(name):
        return lax.ppermute(value, AXES, pairs)


def up_y(v, name="up"):
    return send(v, lambda z, x, y, c: (z, x, y + 1, c), name)


def down_y(v, name="down"):
    return send(v, lambda z, x, y, c: (z, x, y - 1, c), name)


def along_y(v, way, name):
    return send(v, lambda z, x, y, c: (z, x, y + way * (1 - 2 * c), c), name)


def swap(v, name="swap"):
    return send(v, lambda z, x, y, c: (z, x, y, 1 - c), name)


def mate(v, name="mate"):
    return send(v, lambda z, x, y, c: (3 - z, x, y, c), name)


def after(value, *others):
    return lax.optimization_barrier((value, *others))[0]


def route(v, zero, one, name):
    hop = {
        "p": lambda z, x, y, c: (z ^ 1, x, y, c),
        "+": lambda z, x, y, c: (z, x + 1, y, c),
        "-": lambda z, x, y, c: (z, x - 1, y, c),
    }
    return send(v, lambda z, x, y, c: hop[zero if c == 0 else one](z, x, y, c), name)


def slots(z, x, c):
    zl, first = z % 2, c == 0

    def at(dz, dx):
        return (zl + dz) % 2 * 4 + (x + dx) % 4

    held = jnp.stack(
        [
            at(0, 0),
            at(0, 3),
            jnp.where(first, at(1, 0), at(0, 1)),
            jnp.where(first, at(0, 1), at(1, 0)),
            jnp.where(first, at(1, 3), at(1, 1)),
            jnp.where(first, at(0, 2), at(1, 3)),
            jnp.where(first, at(1, 1), at(0, 2)),
            at(1, 2),
        ]
    )
    shard = jnp.arange(8)
    return jnp.sum(jnp.where(held[None, :] == shard[:, None], shard[None, :], 0), axis=1)


def product_kernel(shards, where_ref, *refs):
    mine, near, far, weights = refs[:4], refs[4], refs[5], refs[6 : 6 + shards]
    out_ref, *acc = refs[6 + shards :]
    acc = acc[0] if acc else out_ref
    y, c = where_ref[16], where_ref[17]
    for step, shift in enumerate((0, 3 - 2 * c, 1 + 2 * c, 2)):
        first = lax.rem(y + shift, 4) * STEP
        lane, swapped = (pl.multiple_of(first + core * FEAT, 128) for core in (c, 1 - c))
        other = near[step * ROWS : step * ROWS + ROWS, :] if step < 3 else far[...]
        left = jnp.concatenate([mine[step][...], other], axis=1)
        rows = []
        for k, w in enumerate(weights):
            rows.append(
                jnp.concatenate([w[:, pl.ds(lane, FEAT)], w[:, pl.ds(swapped, FEAT)]], axis=1)
            )
            if shards > 1:
                rows.append(jnp.zeros((128 - SHARD, STEP), BF16))
        right = jnp.concatenate(rows, axis=0) if shards > 1 else rows[0]
        part = lax.dot_general(left, right, NT, preferred_element_type=F32)
        if step == 0:
            acc[:, : part.shape[1]] = part
        elif step < 3:
            acc[:, : part.shape[1]] += part
        else:
            out_ref[:, : part.shape[1]] = (acc[:, : part.shape[1]] + part).astype(out_ref.dtype)


def product(dtype, where, mine, other, weights):
    shards = len(weights)
    width = shards * 128
    vmem = pl.BlockSpec(memory_space=pltpu.VMEM)
    return pl.pallas_call(
        functools.partial(product_kernel, shards),
        out_shape=jax.ShapeDtypeStruct((ROWS, width), dtype),
        in_specs=[pl.BlockSpec(memory_space=pltpu.SMEM)] + [vmem] * (6 + shards),
        out_specs=vmem,
        scratch_shapes=[] if dtype == F32 else [pltpu.VMEM((ROWS, width), F32)],
        compiler_params=pltpu.CompilerParams(
            vmem_limit_bytes=(6 << 20) + width * (4 * STEP + 14 * ROWS)
        ),
        cost_estimate=LIGHT,
        name="product",
    )(where, *mine, *other, *weights)


def early_kernel(where_ref, act_ref, grad_ref, pm_ref, gate_ref, up_ref, ph_ref, out_ref):
    gate, up = gate_ref[...].astype(F32), up_ref[...].astype(F32)
    hidden = (gate * jax.nn.sigmoid(gate) * up).astype(BF16)
    pm = pm_ref[...]
    out_ref[:, 0:64] = lax.dot_general(act_ref[...], pm, NT, preferred_element_type=F32)
    out_ref[:, 64:128] = lax.dot_general(hidden, ph_ref[...], NT, preferred_element_type=F32)
    out_ref[:, 128:192] = lax.dot_general(grad_ref[...], pm, NT, preferred_element_type=F32)


def early(where, activations, out_grad, pm_t, gate, up, ph_t):
    narrow = pl.BlockSpec((128, FEAT), lambda i, w: (i, 0))
    wide = pl.BlockSpec((128, HID), lambda i, w: (i, 0))
    return pl.pallas_call(
        early_kernel,
        out_shape=jax.ShapeDtypeStruct((ROWS, 3 * RANK), F32),
        grid_spec=pltpu.PrefetchScalarGridSpec(
            num_scalar_prefetch=1,
            grid=(4,),
            in_specs=[
                narrow,
                narrow,
                pl.BlockSpec((RANK, FEAT), lambda i, w: (0, 2 * w[16] + w[17])),
                wide,
                wide,
                pl.BlockSpec((RANK, HID), lambda i, w: (0, 0)),
            ],
            out_specs=pl.BlockSpec((128, 3 * RANK), lambda i, w: (i, 0)),
        ),
        compiler_params=pltpu.CompilerParams(vmem_limit_bytes=12 << 20),
        cost_estimate=LIGHT,
        name="early",
    )(where, activations, out_grad, pm_t, gate, up, ph_t)


def grads(where_ref, base, h_refs, held, gate_ref, up_ref, ph_ref, gg_ref, gu_ref):
    at = 0
    for h_ref in h_refs:
        width = h_ref.shape[1]
        held[:, at : at + width] = h_ref[...].astype(F32)
        at += width
    hidden_grad = jnp.concatenate(
        [
            held[:, pl.ds(pl.multiple_of(where_ref[base + i] * 128, 128), 128)][:, :SHARD]
            for i in range(8)
        ],
        axis=1,
    )
    row = pl.program_id(0) * TILE + lax.broadcasted_iota(jnp.int32, hidden_grad.shape, 0)
    hidden_grad = jnp.where(row < where_ref[19], hidden_grad, 0.0)
    gate, up = gate_ref[...].astype(F32), up_ref[...].astype(F32)
    sig = jax.nn.sigmoid(gate)
    grad_up = (hidden_grad * (gate * sig)).astype(BF16)
    grad_gate = (hidden_grad * up * sig * (1.0 + gate * (1.0 - sig))).astype(BF16)
    gg_ref[...] = grad_gate
    gu_ref[...] = grad_up
    both = jnp.concatenate([grad_gate, grad_up], axis=0)
    part = lax.dot_general(both, ph_ref[...], NT, preferred_element_type=F32)
    return jnp.concatenate([part[:TILE], part[TILE:]], axis=1)


def own_kernel(n, where_ref, gate_ref, up_ref, ph_ref, *refs):
    gg_ref, gu_ref, part_ref, held = refs[n:]
    part_ref[...] = grads(
        where_ref, 0, refs[:n], held, gate_ref, up_ref, ph_ref, gg_ref, gu_ref
    )


def row_tiles(half):
    tile = pl.BlockSpec((TILE, HALF), lambda i, w: (i, half(w)))
    return tile, pl.BlockSpec((RANK, HALF), lambda i, w: (0, half(w)))


def pieces_of(h):
    return [pl.BlockSpec((TILE, p.shape[1]), lambda i, w: (i, 0)) for p in h]


BIG = jax.ShapeDtypeStruct((ROWS, HID), BF16)


def own_half(where, gate, up, h, ph_t):
    tile, ranks = row_tiles(lambda w: w[18])
    return pl.pallas_call(
        functools.partial(own_kernel, len(h)),
        out_shape=(BIG, BIG, jax.ShapeDtypeStruct((ROWS, 2 * RANK), F32)),
        grid_spec=pltpu.PrefetchScalarGridSpec(
            num_scalar_prefetch=1,
            grid=(ROWS // TILE,),
            in_specs=[tile, tile, ranks] + pieces_of(h),
            out_specs=(tile, tile, pl.BlockSpec((TILE, 2 * RANK), lambda i, w: (i, 0))),
            scratch_shapes=[pltpu.VMEM((TILE, 1024), F32)],
        ),
        compiler_params=pltpu.CompilerParams(vmem_limit_bytes=14 << 20),
        cost_estimate=LIGHT,
        name="own_half",
    )(where, gate, up, ph_t, *h)


def other_kernel(n, where_ref, gate_ref, up_ref, ph_ref, part_ref, hi_ref, lo_ref,
                 gg_in, gu_in, *refs):
    gg_ref, gu_ref, feat_ref, held, acc = refs[n:]
    i = pl.program_id(0)
    part = grads(where_ref, 8, refs[:n], held, gate_ref, up_ref, ph_ref, gg_ref, gu_ref)
    acc[pl.ds(pl.multiple_of(i * TILE, TILE), TILE), :] = part_ref[...] + part

    @pl.when(i == ROWS // TILE - 1)
    def _():
        feat_ref[...] = twice(hi_ref[...], lo_ref[...], acc[...])


def parted(value):
    hi = value.astype(BF16)
    return hi, (value - hi.astype(F32)).astype(BF16)


def twice(hi, lo, right):
    right_hi, right_lo = parted(right)
    total = jnp.dot(lo, right_hi, preferred_element_type=F32)
    total += jnp.dot(hi, right_lo, preferred_element_type=F32)
    return total + jnp.dot(hi, right_hi, preferred_element_type=F32)


def other_half(where, gate, up, h, ph_t, part, spread, gg, gu):
    tile, ranks = row_tiles(lambda w: 1 - w[18])
    feat = pl.BlockSpec((4 * RANK, 2 * RANK), lambda i, w: (0, 0))
    spreads = pl.BlockSpec((4 * RANK, ROWS), lambda i, w: (0, 0))
    return pl.pallas_call(
        functools.partial(other_kernel, len(h)),
        out_shape=(BIG, BIG, jax.ShapeDtypeStruct((4 * RANK, 2 * RANK), F32)),
        grid_spec=pltpu.PrefetchScalarGridSpec(
            num_scalar_prefetch=1,
            grid=(ROWS // TILE,),
            in_specs=[
                tile,
                tile,
                ranks,
                pl.BlockSpec((TILE, 2 * RANK), lambda i, w: (i, 0)),
                spreads,
                spreads,
                ANY,
                ANY,
            ]
            + pieces_of(h),
            out_specs=(tile, tile, feat),
            scratch_shapes=[pltpu.VMEM((TILE, 1024), F32), pltpu.VMEM((ROWS, 2 * RANK), F32)],
        ),
        input_output_aliases={7: 0, 8: 1},
        compiler_params=pltpu.CompilerParams(vmem_limit_bytes=14 << 20),
        cost_estimate=LIGHT,
        name="other_half",
    )(where, gate, up, ph_t, part, *spread, gg, gu, *h)


def spread_kernel(where_ref, sums_ref, hi_ref, lo_ref, feat_ref):
    sums = sums_ref[...]
    left = sums[:, : 2 * RANK].T
    right = sums[:, 2 * RANK :]
    row = lax.broadcasted_iota(jnp.int32, (1, ROWS), 1)
    start = jnp.int32(0)
    for s in range(4):
        length = where_ref[20 + s]
        member = jnp.logical_and(row >= start, row < start + length).astype(F32)
        weight = member / jnp.sqrt(jnp.broadcast_to(length, (1, ROWS)).astype(F32))
        hi, lo = parted(left[:RANK] * weight)
        at = pl.ds(s * RANK, RANK)
        hi_ref[at, :] = hi
        lo_ref[at, :] = lo
        feat_ref[at, :] = twice(*parted(left[RANK:] * weight), right)
        start += length


def spread_features(where, sums):
    vmem = pl.BlockSpec(memory_space=pltpu.VMEM)
    side = jax.ShapeDtypeStruct((4 * RANK, ROWS), BF16)
    return pl.pallas_call(
        spread_kernel,
        out_shape=(side, side, jax.ShapeDtypeStruct((4 * RANK, RANK), F32)),
        in_specs=[pl.BlockSpec(memory_space=pltpu.SMEM), vmem],
        out_specs=(vmem, vmem, vmem),
        compiler_params=pltpu.CompilerParams(vmem_limit_bytes=8 << 20),
        name="spread",
    )(where, sums)


def sum_tensor(value, c):
    half = value.shape[0] // 2
    top, low = value[:half], value[half:]
    mine = jnp.where(c == 0, top, low) + swap(jnp.where(c == 0, low, top))
    across = send(mine, lambda z, x, y, c: (z, x, y + 2, c))
    mine = (mine + across) + (up_y(mine) + down_y(mine))
    theirs = swap(mine)
    return jnp.concatenate(
        [jnp.where(c == 0, mine, theirs), jnp.where(c == 0, theirs, mine)], axis=0
    )


def on_device(
    activations, out_grad, gate_pre, up_pre, down_weight, proj_model, proj_hidden, lengths
):
    z, x, y, c = (lax.axis_index(a) for a in AXES)
    where = jnp.concatenate(
        [
            slots(z, x, c),
            slots(3 - z, x, c),
            jnp.stack([y, c, z // 2, jnp.sum(lengths)]),
            lengths,
        ]
    ).astype(jnp.int32)
    pm_t, ph_t = proj_model.T, proj_hidden.T
    own_w = down_weight
    theirs = mate(out_grad, "mate_rows")
    a1, a2 = along_y(out_grad, 1, "a1"), along_y(out_grad, -1, "a2")
    r1 = route(own_w, "+", "+", "r1")
    r2 = route(own_w, "p", "-", "r2")
    r3 = route(own_w, "-", "p", "r3")
    b1, b2 = along_y(theirs, 1, "b1"), along_y(theirs, -1, "b2")
    r1, r2, r3, b1, b2, a1, a2, where = lax.optimization_barrier(
        (r1, r2, r3, b1, b2, a1, a2, where)
    )
    r6 = route(r2, "-", "-", "r6")
    r4 = route(r2, "+", "p", "r4")
    r5 = route(r1, "+", "p", "r5")
    b_far = along_y(b1, 1, "b_far")
    b_near = swap(jnp.concatenate([theirs, b2, b1]), "b_swap")
    b_other = [b_near, swap(after(b_far, b_near), "b_swap")]
    a_far = along_y(after(a1, b_far), 1, "a_far")
    parts = early(after(where, b_far), activations, out_grad, pm_t, gate_pre, up_pre, ph_t)
    top, low = parts[:256], parts[256:]
    core_sum = swap(after(jnp.where(c == 0, low, top), b_other[1]), "s_core")
    b_mine = [theirs, b1, b2, b_far]
    h1 = product(BF16, after(where, r4, r5, r6, a_far, parts), b_mine, b_other, [own_w, r1, r2, r3])
    r7 = route(r6, "-", "p", "r7")
    h1_in = mate(h1, "mate_grad1")
    h2 = product(BF16, after(where, h1), b_mine, b_other, [r4, r5, r6])
    h2_in = mate(h2, "mate_grad2")
    a_mine = [out_grad, a1, a2, a_far]
    near = jnp.concatenate([out_grad, a2, a1])
    a_other = [swap(after(near, h1), "a_swap"), swap(a_far, "a_swap")]
    half = jnp.where(c == 0, top, low) + after(core_sum, h2)
    near_y = send(half, lambda z, x, y, c: (z, x, y ^ 1, c), "s_near")
    own1 = product(F32, after(where, h2), a_mine, a_other, [own_w, r1, r2, r3, r4, r5, r6])
    half += after(near_y, own1)
    far_y = send(half, lambda z, x, y, c: (z, x, y ^ 2, c), "s_far")
    h3 = product(BF16, after(where, h1_in, own1), b_mine, b_other, [r7])
    own2 = product(F32, after(where, h3), a_mine, a_other, [r7])
    half += after(far_y, own2)
    rest = swap(half, "s_core")
    sums = jnp.concatenate(
        [jnp.where(c == 0, half, rest), jnp.where(c == 0, rest, half)], axis=0
    )
    h_in = [h1_in, h2_in, mate(h3, "mate_grad3")]
    grad_gate, grad_up, part = own_half(after(where, h2_in), gate_pre, up_pre, (own1, own2), ph_t)
    *spread, down_feat = spread_features(after(where, part, h_in[2]), sums)
    grad_gate, grad_up, feat = other_half(
        where, gate_pre, up_pre, h_in, ph_t, part, spread, grad_gate, grad_up
    )
    total = jnp.concatenate([sum_tensor(feat, c), down_feat], axis=1)
    features = total.reshape(4, RANK, 3, RANK).transpose(0, 2, 1, 3).reshape(4, 3, RANK * RANK)
    return grad_gate, grad_up, features


def solution(mesh):
    split = Mesh(mesh.devices.reshape(4, 4, 4, 2), AXES)
    dp, tensor = ("z", "x"), ("y", "c")
    return jax.shard_map(
        on_device,
        mesh=split,
        in_specs=(
            P(dp, tensor),
            P(dp, tensor),
            P(dp, tensor),
            P(dp, tensor),
            P((*tensor, *dp), None),
            P(),
            P(tensor, None),
            P(dp),
        ),
        out_specs=(P(dp, tensor), P(dp, tensor), P(dp, None, None)),
        check_vma=False,
    )
```

```python
import functools

import jax
import jax.numpy as jnp
from jax import lax
from jax.experimental import pallas as pl
from jax.experimental.pallas import tpu as pltpu
from jax.sharding import Mesh
from jax.sharding import PartitionSpec as P

AXES = ("z", "x", "y", "c")
F32, BF16 = jnp.float32, jnp.bfloat16
ROWS, FEAT, HID, HALF, RANK, DEPTH = 512, 640, 1792, 896, 64, 5120
SHARD = 112
TILE = 128
STEP = 2 * FEAT
NT = (((1,), (1,)), ((), ()))
LIGHT = pl.CostEstimate(flops=1 << 20, bytes_accessed=1 << 16, transcendentals=0)
ANY = pl.BlockSpec(memory_space=pl.ANY)


def send(value, target, name="send"):
    def line(z, x, y, c):
        return ((z % 4 * 4 + x % 4) * 4 + y % 4) * 2 + c

    pairs = [
        (line(z, x, y, c), line(*target(z, x, y, c)))
        for z in range(4)
        for x in range(4)
        for y in range(4)
        for c in range(2)
    ]
    with jax.named_scope(name):
        return lax.ppermute(value, AXES, pairs)


def up_y(v, name="up"):
    return send(v, lambda z, x, y, c: (z, x, y + 1, c), name)


def down_y(v, name="down"):
    return send(v, lambda z, x, y, c: (z, x, y - 1, c), name)


def along_y(v, way, name):
    return send(v, lambda z, x, y, c: (z, x, y + way * (1 - 2 * c), c), name)


def swap(v, name="swap"):
    return send(v, lambda z, x, y, c: (z, x, y, 1 - c), name)


def mate(v, name="mate"):
    return send(v, lambda z, x, y, c: (3 - z, x, y, c), name)


def after(value, *others):
    return lax.optimization_barrier((value, *others))[0]


def route(v, zero, one, name):
    hop = {
        "p": lambda z, x, y, c: (z ^ 1, x, y, c),
        "+": lambda z, x, y, c: (z, x + 1, y, c),
        "-": lambda z, x, y, c: (z, x - 1, y, c),
    }
    return send(v, lambda z, x, y, c: hop[zero if c == 0 else one](z, x, y, c), name)


def slots(z, x, c):
    zl, first = z % 2, c == 0

    def at(dz, dx):
        return (zl + dz) % 2 * 4 + (x + dx) % 4

    held = jnp.stack(
        [
            at(0, 0),
            at(0, 3),
            jnp.where(first, at(1, 0), at(0, 1)),
            jnp.where(first, at(0, 1), at(1, 0)),
            jnp.where(first, at(1, 3), at(1, 1)),
            jnp.where(first, at(0, 2), at(1, 3)),
            jnp.where(first, at(1, 1), at(0, 2)),
            at(1, 2),
        ]
    )
    shard = jnp.arange(8)
    return jnp.sum(jnp.where(held[None, :] == shard[:, None], shard[None, :], 0), axis=1)


def product_kernel(shards, where_ref, *refs):
    mine, near, far, weights = refs[:4], refs[4], refs[5], refs[6 : 6 + shards]
    out_ref, *acc = refs[6 + shards :]
    acc = acc[0] if acc else out_ref
    y, c = where_ref[16], where_ref[17]
    for step, shift in enumerate((0, 3 - 2 * c, 1 + 2 * c, 2)):
        first = lax.rem(y + shift, 4) * STEP
        lane, swapped = (pl.multiple_of(first + core * FEAT, 128) for core in (c, 1 - c))
        other = near[step * ROWS : step * ROWS + ROWS, :] if step < 3 else far[...]
        left = jnp.concatenate([mine[step][...], other], axis=1)
        rows = []
        for k, w in enumerate(weights):
            rows.append(
                jnp.concatenate([w[:, pl.ds(lane, FEAT)], w[:, pl.ds(swapped, FEAT)]], axis=1)
            )
            if shards > 1:
                rows.append(jnp.zeros((128 - SHARD, STEP), BF16))
        right = jnp.concatenate(rows, axis=0) if shards > 1 else rows[0]
        part = lax.dot_general(left, right, NT, preferred_element_type=F32)
        if step == 0:
            acc[:, : part.shape[1]] = part
        elif step < 3:
            acc[:, : part.shape[1]] += part
        else:
            out_ref[:, : part.shape[1]] = (acc[:, : part.shape[1]] + part).astype(out_ref.dtype)


def product(dtype, where, mine, other, weights):
    shards = len(weights)
    width = shards * 128
    vmem = pl.BlockSpec(memory_space=pltpu.VMEM)
    return pl.pallas_call(
        functools.partial(product_kernel, shards),
        out_shape=jax.ShapeDtypeStruct((ROWS, width), dtype),
        in_specs=[pl.BlockSpec(memory_space=pltpu.SMEM)] + [vmem] * (6 + shards),
        out_specs=vmem,
        scratch_shapes=[] if dtype == F32 else [pltpu.VMEM((ROWS, width), F32)],
        compiler_params=pltpu.CompilerParams(
            vmem_limit_bytes=(6 << 20) + width * (4 * STEP + 14 * ROWS)
        ),
        cost_estimate=LIGHT,
        name="product",
    )(where, *mine, *other, *weights)


def early_kernel(where_ref, act_ref, grad_ref, pm_ref, gate_ref, up_ref, ph_ref, out_ref):
    gate, up = gate_ref[...].astype(F32), up_ref[...].astype(F32)
    hidden = (gate * jax.nn.sigmoid(gate) * up).astype(BF16)
    pm = pm_ref[...]
    out_ref[:, 0:64] = lax.dot_general(act_ref[...], pm, NT, preferred_element_type=F32)
    out_ref[:, 64:128] = lax.dot_general(hidden, ph_ref[...], NT, preferred_element_type=F32)
    out_ref[:, 128:192] = lax.dot_general(grad_ref[...], pm, NT, preferred_element_type=F32)


def early(where, activations, out_grad, pm_t, gate, up, ph_t):
    narrow = pl.BlockSpec((128, FEAT), lambda i, w: (i, 0))
    wide = pl.BlockSpec((128, HID), lambda i, w: (i, 0))
    return pl.pallas_call(
        early_kernel,
        out_shape=jax.ShapeDtypeStruct((ROWS, 3 * RANK), F32),
        grid_spec=pltpu.PrefetchScalarGridSpec(
            num_scalar_prefetch=1,
            grid=(4,),
            in_specs=[
                narrow,
                narrow,
                pl.BlockSpec((RANK, FEAT), lambda i, w: (0, 2 * w[16] + w[17])),
                wide,
                wide,
                pl.BlockSpec((RANK, HID), lambda i, w: (0, 0)),
            ],
            out_specs=pl.BlockSpec((128, 3 * RANK), lambda i, w: (i, 0)),
        ),
        compiler_params=pltpu.CompilerParams(vmem_limit_bytes=12 << 20),
        cost_estimate=LIGHT,
        name="early",
    )(where, activations, out_grad, pm_t, gate, up, ph_t)


def grads(where_ref, base, h_refs, held, gate_ref, up_ref, ph_ref, gg_ref, gu_ref):
    at = 0
    for h_ref in h_refs:
        width = h_ref.shape[1]
        held[:, at : at + width] = h_ref[...].astype(F32)
        at += width
    hidden_grad = jnp.concatenate(
        [
            held[:, pl.ds(pl.multiple_of(where_ref[base + i] * 128, 128), 128)][:, :SHARD]
            for i in range(8)
        ],
        axis=1,
    )
    row = pl.program_id(0) * TILE + lax.broadcasted_iota(jnp.int32, hidden_grad.shape, 0)
    hidden_grad = jnp.where(row < where_ref[19], hidden_grad, 0.0)
    gate, up = gate_ref[...].astype(F32), up_ref[...].astype(F32)
    sig = jax.nn.sigmoid(gate)
    grad_up = (hidden_grad * (gate * sig)).astype(BF16)
    grad_gate = (hidden_grad * up * sig * (1.0 + gate * (1.0 - sig))).astype(BF16)
    gg_ref[...] = grad_gate
    gu_ref[...] = grad_up
    both = jnp.concatenate([grad_gate, grad_up], axis=0)
    part = lax.dot_general(both, ph_ref[...], NT, preferred_element_type=F32)
    return jnp.concatenate([part[:TILE], part[TILE:]], axis=1)


def own_kernel(n, where_ref, gate_ref, up_ref, ph_ref, *refs):
    gg_ref, gu_ref, part_ref, held = refs[n:]
    part_ref[...] = grads(
        where_ref, 0, refs[:n], held, gate_ref, up_ref, ph_ref, gg_ref, gu_ref
    )


def row_tiles(half):
    tile = pl.BlockSpec((TILE, HALF), lambda i, w: (i, half(w)))
    return tile, pl.BlockSpec((RANK, HALF), lambda i, w: (0, half(w)))


def pieces_of(h):
    return [pl.BlockSpec((TILE, p.shape[1]), lambda i, w: (i, 0)) for p in h]


BIG = jax.ShapeDtypeStruct((ROWS, HID), BF16)


def own_half(where, gate, up, h, ph_t):
    tile, ranks = row_tiles(lambda w: w[18])
    return pl.pallas_call(
        functools.partial(own_kernel, len(h)),
        out_shape=(BIG, BIG, jax.ShapeDtypeStruct((ROWS, 2 * RANK), F32)),
        grid_spec=pltpu.PrefetchScalarGridSpec(
            num_scalar_prefetch=1,
            grid=(ROWS // TILE,),
            in_specs=[tile, tile, ranks] + pieces_of(h),
            out_specs=(tile, tile, pl.BlockSpec((TILE, 2 * RANK), lambda i, w: (i, 0))),
            scratch_shapes=[pltpu.VMEM((TILE, 1024), F32)],
        ),
        compiler_params=pltpu.CompilerParams(vmem_limit_bytes=14 << 20),
        cost_estimate=LIGHT,
        name="own_half",
    )(where, gate, up, ph_t, *h)


def other_kernel(n, where_ref, gate_ref, up_ref, ph_ref, part_ref, gg_in, gu_in, *refs):
    gg_ref, gu_ref, sum_ref, held = refs[n:]
    sum_ref[...] = part_ref[...] + grads(
        where_ref, 8, refs[:n], held, gate_ref, up_ref, ph_ref, gg_ref, gu_ref
    )


def parted(value):
    hi = value.astype(BF16)
    return hi, (value - hi.astype(F32)).astype(BF16)


def twice(hi, lo, right):
    right_hi, right_lo = parted(right)
    total = jnp.dot(lo, right_hi, preferred_element_type=F32)
    total += jnp.dot(hi, right_lo, preferred_element_type=F32)
    return total + jnp.dot(hi, right_hi, preferred_element_type=F32)


def other_half(where, gate, up, h, ph_t, part, gg, gu):
    tile, ranks = row_tiles(lambda w: 1 - w[18])
    narrow = pl.BlockSpec((TILE, 2 * RANK), lambda i, w: (i, 0))
    return pl.pallas_call(
        functools.partial(other_kernel, len(h)),
        out_shape=(BIG, BIG, jax.ShapeDtypeStruct((ROWS, 2 * RANK), F32)),
        grid_spec=pltpu.PrefetchScalarGridSpec(
            num_scalar_prefetch=1,
            grid=(ROWS // TILE,),
            in_specs=[tile, tile, ranks, narrow, ANY, ANY] + pieces_of(h),
            out_specs=(tile, tile, narrow),
            scratch_shapes=[pltpu.VMEM((TILE, 1024), F32)],
        ),
        input_output_aliases={5: 0, 6: 1},
        compiler_params=pltpu.CompilerParams(vmem_limit_bytes=14 << 20),
        cost_estimate=LIGHT,
        name="other_half",
    )(where, gate, up, ph_t, part, gg, gu, *h)


def feature_kernel(hi_ref, lo_ref, right_ref, out_ref):
    out_ref[...] = twice(hi_ref[...], lo_ref[...], right_ref[...])


def features_of(spread, right):
    vmem = pl.BlockSpec(memory_space=pltpu.VMEM)
    return pl.pallas_call(
        feature_kernel,
        out_shape=jax.ShapeDtypeStruct((4 * RANK, 2 * RANK), F32),
        in_specs=[vmem] * 3,
        out_specs=vmem,
        compiler_params=pltpu.CompilerParams(vmem_limit_bytes=4 << 20),
        cost_estimate=LIGHT,
        name="features",
    )(*spread, right)


def spread_kernel(where_ref, sums_ref, hi_ref, lo_ref, feat_ref):
    sums = sums_ref[...]
    left = sums[:, : 2 * RANK].T
    right = sums[:, 2 * RANK :]
    row = lax.broadcasted_iota(jnp.int32, (1, ROWS), 1)
    start = jnp.int32(0)
    for s in range(4):
        length = where_ref[20 + s]
        member = jnp.logical_and(row >= start, row < start + length).astype(F32)
        weight = member / jnp.sqrt(jnp.broadcast_to(length, (1, ROWS)).astype(F32))
        hi, lo = parted(left[:RANK] * weight)
        at = pl.ds(s * RANK, RANK)
        hi_ref[at, :] = hi
        lo_ref[at, :] = lo
        feat_ref[at, :] = twice(*parted(left[RANK:] * weight), right)
        start += length


def spread_features(where, sums):
    vmem = pl.BlockSpec(memory_space=pltpu.VMEM)
    side = jax.ShapeDtypeStruct((4 * RANK, ROWS), BF16)
    return pl.pallas_call(
        spread_kernel,
        out_shape=(side, side, jax.ShapeDtypeStruct((4 * RANK, RANK), F32)),
        in_specs=[pl.BlockSpec(memory_space=pltpu.SMEM), vmem],
        out_specs=(vmem, vmem, vmem),
        compiler_params=pltpu.CompilerParams(vmem_limit_bytes=8 << 20),
        name="spread",
    )(where, sums)


def sum_tensor(value, c):
    half = value.shape[0] // 2
    top, low = value[:half], value[half:]
    mine = jnp.where(c == 0, top, low) + swap(jnp.where(c == 0, low, top))
    across = send(mine, lambda z, x, y, c: (z, x, y + 2, c))
    mine = (mine + across) + (up_y(mine) + down_y(mine))
    theirs = swap(mine)
    return jnp.concatenate(
        [jnp.where(c == 0, mine, theirs), jnp.where(c == 0, theirs, mine)], axis=0
    )


def on_device(
    activations, out_grad, gate_pre, up_pre, down_weight, proj_model, proj_hidden, lengths
):
    z, x, y, c = (lax.axis_index(a) for a in AXES)
    where = jnp.concatenate(
        [
            slots(z, x, c),
            slots(3 - z, x, c),
            jnp.stack([y, c, z // 2, jnp.sum(lengths)]),
            lengths,
        ]
    ).astype(jnp.int32)
    pm_t, ph_t = proj_model.T, proj_hidden.T
    own_w = down_weight
    theirs = mate(out_grad, "mate_rows")
    a1, a2 = along_y(out_grad, 1, "a1"), along_y(out_grad, -1, "a2")
    r1 = route(own_w, "+", "+", "r1")
    r2 = route(own_w, "p", "-", "r2")
    r3 = route(own_w, "-", "p", "r3")
    b1, b2 = along_y(theirs, 1, "b1"), along_y(theirs, -1, "b2")
    r1, r2, r3, b1, b2, a1, a2, where = lax.optimization_barrier(
        (r1, r2, r3, b1, b2, a1, a2, where)
    )
    r6 = route(r2, "-", "-", "r6")
    r4 = route(r2, "+", "p", "r4")
    r5 = route(r1, "+", "p", "r5")
    b_far = along_y(b1, 1, "b_far")
    b_near = swap(jnp.concatenate([theirs, b2, b1]), "b_swap")
    b_other = [b_near, swap(after(b_far, b_near), "b_swap")]
    a_far = along_y(after(a1, b_far), 1, "a_far")
    parts = early(after(where, b_far), activations, out_grad, pm_t, gate_pre, up_pre, ph_t)
    top, low = parts[:256], parts[256:]
    core_sum = swap(after(jnp.where(c == 0, low, top), b_other[1]), "s_core")
    b_mine = [theirs, b1, b2, b_far]
    h1 = product(BF16, after(where, r4, r5, r6, a_far, parts), b_mine, b_other, [own_w, r1, r2, r3])
    r7 = route(r6, "-", "p", "r7")
    h1_in = mate(h1, "mate_grad1")
    h2 = product(BF16, after(where, h1), b_mine, b_other, [r4, r5, r6])
    h2_in = mate(h2, "mate_grad2")
    a_mine = [out_grad, a1, a2, a_far]
    near = jnp.concatenate([out_grad, a2, a1])
    a_other = [swap(after(near, h1), "a_swap"), swap(a_far, "a_swap")]
    half = jnp.where(c == 0, top, low) + after(core_sum, h2)
    near_y = send(half, lambda z, x, y, c: (z, x, y ^ 1, c), "s_near")
    own1 = product(F32, after(where, h2), a_mine, a_other, [own_w, r1, r2, r3, r4, r5, r6])
    half += after(near_y, own1)
    far_y = send(half, lambda z, x, y, c: (z, x, y ^ 2, c), "s_far")
    h3 = product(BF16, after(where, h1_in, own1), b_mine, b_other, [r7])
    own2 = product(F32, after(where, h3), a_mine, a_other, [r7])
    h_in = [h1_in, h2_in, mate(h3, "mate_grad3")]
    grad_gate, grad_up, part = own_half(where, gate_pre, up_pre, (own1, own2), ph_t)
    half += after(far_y, part, h_in[1], h_in[2])
    rest = swap(half, "s_core")
    sums = jnp.concatenate(
        [jnp.where(c == 0, half, rest), jnp.where(c == 0, rest, half)], axis=0
    )
    *spread, down_feat = spread_features(where, sums)
    grad_gate, grad_up, part = other_half(
        where, gate_pre, up_pre, h_in, ph_t, part, grad_gate, grad_up
    )
    feat = features_of(spread, part)
    total = jnp.concatenate([sum_tensor(feat, c), down_feat], axis=1)
    features = total.reshape(4, RANK, 3, RANK).transpose(0, 2, 1, 3).reshape(4, 3, RANK * RANK)
    return grad_gate, grad_up, features


def solution(mesh):
    split = Mesh(mesh.devices.reshape(4, 4, 4, 2), AXES)
    dp, tensor = ("z", "x"), ("y", "c")
    return jax.shard_map(
        on_device,
        mesh=split,
        in_specs=(
            P(dp, tensor),
            P(dp, tensor),
            P(dp, tensor),
            P(dp, tensor),
            P((*tensor, *dp), None),
            P(),
            P(tensor, None),
            P(dp),
        ),
        out_specs=(P(dp, tensor), P(dp, tensor), P(dp, None, None)),
        check_vma=False,
    )
```

```python
import functools

import jax
import jax.numpy as jnp
from jax import lax
from jax.experimental import pallas as pl
from jax.experimental.pallas import tpu as pltpu
from jax.sharding import Mesh
from jax.sharding import PartitionSpec as P

AXES = ("z", "x", "y", "c")
F32, BF16 = jnp.float32, jnp.bfloat16
ROWS, FEAT, HID, HALF, RANK, DEPTH = 512, 640, 1792, 896, 64, 5120
SHARD = 112
TILE = 128
STEP = 2 * FEAT
NT = (((1,), (1,)), ((), ()))
LIGHT = pl.CostEstimate(flops=1 << 20, bytes_accessed=1 << 16, transcendentals=0)
ANY = pl.BlockSpec(memory_space=pl.ANY)


def send(value, target, name="send"):
    def line(z, x, y, c):
        return ((z % 4 * 4 + x % 4) * 4 + y % 4) * 2 + c

    pairs = [
        (line(z, x, y, c), line(*target(z, x, y, c)))
        for z in range(4)
        for x in range(4)
        for y in range(4)
        for c in range(2)
    ]
    with jax.named_scope(name):
        return lax.ppermute(value, AXES, pairs)


def up_y(v, name="up"):
    return send(v, lambda z, x, y, c: (z, x, y + 1, c), name)


def down_y(v, name="down"):
    return send(v, lambda z, x, y, c: (z, x, y - 1, c), name)


def along_y(v, way, name):
    return send(v, lambda z, x, y, c: (z, x, y + way * (1 - 2 * c), c), name)


def swap(v, name="swap"):
    return send(v, lambda z, x, y, c: (z, x, y, 1 - c), name)


def mate(v, name="mate"):
    return send(v, lambda z, x, y, c: (3 - z, x, y, c), name)


def after(value, *others):
    return lax.optimization_barrier((value, *others))[0]


def route(v, zero, one, name):
    hop = {
        "p": lambda z, x, y, c: (z ^ 1, x, y, c),
        "+": lambda z, x, y, c: (z, x + 1, y, c),
        "-": lambda z, x, y, c: (z, x - 1, y, c),
    }
    return send(v, lambda z, x, y, c: hop[zero if c == 0 else one](z, x, y, c), name)


def slots(z, x, c):
    zl, first = z % 2, c == 0

    def at(dz, dx):
        return (zl + dz) % 2 * 4 + (x + dx) % 4

    held = jnp.stack(
        [
            at(0, 0),
            at(0, 3),
            jnp.where(first, at(1, 0), at(0, 1)),
            jnp.where(first, at(0, 1), at(1, 0)),
            jnp.where(first, at(1, 3), at(1, 1)),
            jnp.where(first, at(0, 2), at(1, 3)),
            jnp.where(first, at(1, 1), at(0, 2)),
            at(1, 2),
        ]
    )
    shard = jnp.arange(8)
    return jnp.sum(jnp.where(held[None, :] == shard[:, None], shard[None, :], 0), axis=1)


def product_kernel(shards, where_ref, *refs):
    mine, near, far, weights = refs[:4], refs[4], refs[5], refs[6 : 6 + shards]
    out_ref, *acc = refs[6 + shards :]
    acc = acc[0] if acc else out_ref
    y, c = where_ref[16], where_ref[17]
    for step, shift in enumerate((0, 3 - 2 * c, 1 + 2 * c, 2)):
        first = lax.rem(y + shift, 4) * STEP
        lane, swapped = (pl.multiple_of(first + core * FEAT, 128) for core in (c, 1 - c))
        other = near[step * ROWS : step * ROWS + ROWS, :] if step < 3 else far[...]
        left = jnp.concatenate([mine[step][...], other], axis=1)
        rows = []
        for k, w in enumerate(weights):
            rows.append(
                jnp.concatenate([w[:, pl.ds(lane, FEAT)], w[:, pl.ds(swapped, FEAT)]], axis=1)
            )
            if shards > 1:
                rows.append(jnp.zeros((128 - SHARD, STEP), BF16))
        right = jnp.concatenate(rows, axis=0) if shards > 1 else rows[0]
        part = lax.dot_general(left, right, NT, preferred_element_type=F32)
        if step == 0:
            acc[:, : part.shape[1]] = part
        elif step < 3:
            acc[:, : part.shape[1]] += part
        else:
            out_ref[:, : part.shape[1]] = (acc[:, : part.shape[1]] + part).astype(out_ref.dtype)


def product(dtype, where, mine, other, weights):
    shards = len(weights)
    width = shards * 128
    vmem = pl.BlockSpec(memory_space=pltpu.VMEM)
    return pl.pallas_call(
        functools.partial(product_kernel, shards),
        out_shape=jax.ShapeDtypeStruct((ROWS, width), dtype),
        in_specs=[pl.BlockSpec(memory_space=pltpu.SMEM)] + [vmem] * (6 + shards),
        out_specs=vmem,
        scratch_shapes=[] if dtype == F32 else [pltpu.VMEM((ROWS, width), F32)],
        compiler_params=pltpu.CompilerParams(
            vmem_limit_bytes=(6 << 20) + width * (4 * STEP + 14 * ROWS)
        ),
        cost_estimate=LIGHT,
        name="product",
    )(where, *mine, *other, *weights)


def early_kernel(where_ref, act_ref, grad_ref, pm_ref, gate_ref, up_ref, ph_ref, out_ref):
    gate, up = gate_ref[...].astype(F32), up_ref[...].astype(F32)
    hidden = (gate * jax.nn.sigmoid(gate) * up).astype(BF16)
    pm = pm_ref[...]
    out_ref[:, 0:64] = lax.dot_general(act_ref[...], pm, NT, preferred_element_type=F32)
    out_ref[:, 64:128] = lax.dot_general(hidden, ph_ref[...], NT, preferred_element_type=F32)
    out_ref[:, 128:192] = lax.dot_general(grad_ref[...], pm, NT, preferred_element_type=F32)


def early(where, activations, out_grad, pm_t, gate, up, ph_t):
    narrow = pl.BlockSpec((128, FEAT), lambda i, w: (i, 0))
    wide = pl.BlockSpec((128, HID), lambda i, w: (i, 0))
    return pl.pallas_call(
        early_kernel,
        out_shape=jax.ShapeDtypeStruct((ROWS, 3 * RANK), F32),
        grid_spec=pltpu.PrefetchScalarGridSpec(
            num_scalar_prefetch=1,
            grid=(4,),
            in_specs=[
                narrow,
                narrow,
                pl.BlockSpec((RANK, FEAT), lambda i, w: (0, 2 * w[16] + w[17])),
                wide,
                wide,
                pl.BlockSpec((RANK, HID), lambda i, w: (0, 0)),
            ],
            out_specs=pl.BlockSpec((128, 3 * RANK), lambda i, w: (i, 0)),
        ),
        compiler_params=pltpu.CompilerParams(vmem_limit_bytes=12 << 20),
        cost_estimate=LIGHT,
        name="early",
    )(where, activations, out_grad, pm_t, gate, up, ph_t)


def grads(where_ref, base, h_refs, held, gate_ref, up_ref, ph_ref, gg_ref, gu_ref):
    at = 0
    for h_ref in h_refs:
        width = h_ref.shape[1]
        held[:, at : at + width] = h_ref[...].astype(F32)
        at += width
    hidden_grad = jnp.concatenate(
        [
            held[:, pl.ds(pl.multiple_of(where_ref[base + i] * 128, 128), 128)][:, :SHARD]
            for i in range(8)
        ],
        axis=1,
    )
    row = pl.program_id(0) * TILE + lax.broadcasted_iota(jnp.int32, hidden_grad.shape, 0)
    hidden_grad = jnp.where(row < where_ref[19], hidden_grad, 0.0)
    gate, up = gate_ref[...].astype(F32), up_ref[...].astype(F32)
    sig = jax.nn.sigmoid(gate)
    grad_up = (hidden_grad * (gate * sig)).astype(BF16)
    grad_gate = (hidden_grad * up * sig * (1.0 + gate * (1.0 - sig))).astype(BF16)
    gg_ref[...] = grad_gate
    gu_ref[...] = grad_up
    both = jnp.concatenate([grad_gate, grad_up], axis=0)
    part = lax.dot_general(both, ph_ref[...], NT, preferred_element_type=F32)
    return jnp.concatenate([part[:TILE], part[TILE:]], axis=1)


def own_kernel(n, where_ref, gate_ref, up_ref, ph_ref, *refs):
    gg_ref, gu_ref, part_ref, held = refs[n:]
    part_ref[...] = grads(
        where_ref, 0, refs[:n], held, gate_ref, up_ref, ph_ref, gg_ref, gu_ref
    )


def row_tiles(half):
    tile = pl.BlockSpec((TILE, HALF), lambda i, w: (i, half(w)))
    return tile, pl.BlockSpec((RANK, HALF), lambda i, w: (0, half(w)))


def pieces_of(h):
    return [pl.BlockSpec((TILE, p.shape[1]), lambda i, w: (i, 0)) for p in h]


BIG = jax.ShapeDtypeStruct((ROWS, HID), BF16)


def own_half(where, gate, up, h, ph_t):
    tile, ranks = row_tiles(lambda w: w[18])
    return pl.pallas_call(
        functools.partial(own_kernel, len(h)),
        out_shape=(BIG, BIG, jax.ShapeDtypeStruct((ROWS, 2 * RANK), F32)),
        grid_spec=pltpu.PrefetchScalarGridSpec(
            num_scalar_prefetch=1,
            grid=(ROWS // TILE,),
            in_specs=[tile, tile, ranks] + pieces_of(h),
            out_specs=(tile, tile, pl.BlockSpec((TILE, 2 * RANK), lambda i, w: (i, 0))),
            scratch_shapes=[pltpu.VMEM((TILE, 1024), F32)],
        ),
        compiler_params=pltpu.CompilerParams(vmem_limit_bytes=14 << 20),
        cost_estimate=LIGHT,
        name="own_half",
    )(where, gate, up, ph_t, *h)


def other_kernel(n, where_ref, gate_ref, up_ref, ph_ref, part_ref, gg_in, gu_in, *refs):
    gg_ref, gu_ref, sum_ref, held = refs[n:]
    sum_ref[...] = part_ref[...] + grads(
        where_ref, 8, refs[:n], held, gate_ref, up_ref, ph_ref, gg_ref, gu_ref
    )


def parted(value):
    hi = value.astype(BF16)
    return hi, (value - hi.astype(F32)).astype(BF16)


def twice(hi, lo, right):
    right_hi, right_lo = parted(right)
    total = jnp.dot(lo, right_hi, preferred_element_type=F32)
    total += jnp.dot(hi, right_lo, preferred_element_type=F32)
    return total + jnp.dot(hi, right_hi, preferred_element_type=F32)


def other_half(where, gate, up, h, ph_t, part, gg, gu):
    tile, ranks = row_tiles(lambda w: 1 - w[18])
    narrow = pl.BlockSpec((TILE, 2 * RANK), lambda i, w: (i, 0))
    return pl.pallas_call(
        functools.partial(other_kernel, len(h)),
        out_shape=(BIG, BIG, jax.ShapeDtypeStruct((ROWS, 2 * RANK), F32)),
        grid_spec=pltpu.PrefetchScalarGridSpec(
            num_scalar_prefetch=1,
            grid=(ROWS // TILE,),
            in_specs=[tile, tile, ranks, narrow, ANY, ANY] + pieces_of(h),
            out_specs=(tile, tile, narrow),
            scratch_shapes=[pltpu.VMEM((TILE, 1024), F32)],
        ),
        input_output_aliases={5: 0, 6: 1},
        compiler_params=pltpu.CompilerParams(vmem_limit_bytes=14 << 20),
        cost_estimate=LIGHT,
        name="other_half",
    )(where, gate, up, ph_t, part, gg, gu, *h)


def feature_kernel(hi_ref, lo_ref, right_ref, out_ref):
    out_ref[...] = twice(hi_ref[...], lo_ref[...], right_ref[...])


def features_of(spread, right):
    vmem = pl.BlockSpec(memory_space=pltpu.VMEM)
    return pl.pallas_call(
        feature_kernel,
        out_shape=jax.ShapeDtypeStruct((4 * RANK, 2 * RANK), F32),
        in_specs=[vmem] * 3,
        out_specs=vmem,
        compiler_params=pltpu.CompilerParams(vmem_limit_bytes=4 << 20),
        cost_estimate=LIGHT,
        name="features",
    )(*spread, right)


def spread_kernel(where_ref, sums_ref, hi_ref, lo_ref, feat_ref):
    sums = sums_ref[...]
    left = sums[:, : 2 * RANK].T
    right = sums[:, 2 * RANK :]
    row = lax.broadcasted_iota(jnp.int32, (1, ROWS), 1)
    start = jnp.int32(0)
    for s in range(4):
        length = where_ref[20 + s]
        member = jnp.logical_and(row >= start, row < start + length).astype(F32)
        weight = member / jnp.sqrt(jnp.broadcast_to(length, (1, ROWS)).astype(F32))
        hi, lo = parted(left[:RANK] * weight)
        at = pl.ds(s * RANK, RANK)
        hi_ref[at, :] = hi
        lo_ref[at, :] = lo
        feat_ref[at, :] = twice(*parted(left[RANK:] * weight), right)
        start += length


def spread_features(where, sums):
    vmem = pl.BlockSpec(memory_space=pltpu.VMEM)
    side = jax.ShapeDtypeStruct((4 * RANK, ROWS), BF16)
    return pl.pallas_call(
        spread_kernel,
        out_shape=(side, side, jax.ShapeDtypeStruct((4 * RANK, RANK), F32)),
        in_specs=[pl.BlockSpec(memory_space=pltpu.SMEM), vmem],
        out_specs=(vmem, vmem, vmem),
        compiler_params=pltpu.CompilerParams(vmem_limit_bytes=8 << 20),
        name="spread",
    )(where, sums)


def sum_tensor(value, c):
    half = value.shape[0] // 2
    top, low = value[:half], value[half:]
    mine = jnp.where(c == 0, top, low) + swap(jnp.where(c == 0, low, top))
    across = send(mine, lambda z, x, y, c: (z, x, y + 2, c))
    mine = (mine + across) + (up_y(mine) + down_y(mine))
    theirs = swap(mine)
    return jnp.concatenate(
        [jnp.where(c == 0, mine, theirs), jnp.where(c == 0, theirs, mine)], axis=0
    )


def on_device(
    activations, out_grad, gate_pre, up_pre, down_weight, proj_model, proj_hidden, lengths
):
    z, x, y, c = (lax.axis_index(a) for a in AXES)
    where = jnp.concatenate(
        [
            slots(z, x, c),
            slots(3 - z, x, c),
            jnp.stack([y, c, z // 2, jnp.sum(lengths)]),
            lengths,
        ]
    ).astype(jnp.int32)
    pm_t, ph_t = proj_model.T, proj_hidden.T
    own_w = down_weight
    theirs = mate(out_grad, "mate_rows")
    a1, a2 = along_y(out_grad, 1, "a1"), along_y(out_grad, -1, "a2")
    r1 = route(own_w, "+", "+", "r1")
    r2 = route(own_w, "p", "-", "r2")
    r3 = route(own_w, "-", "p", "r3")
    b1, b2 = along_y(theirs, 1, "b1"), along_y(theirs, -1, "b2")
    r1, r2, r3, b1, b2, a1, a2, where = lax.optimization_barrier(
        (r1, r2, r3, b1, b2, a1, a2, where)
    )
    r6 = route(r2, "-", "-", "r6")
    r4 = route(r2, "+", "p", "r4")
    r5 = route(r1, "+", "p", "r5")
    b_far = along_y(b1, 1, "b_far")
    b_near = swap(jnp.concatenate([theirs, b2, b1]), "b_swap")
    b_other = [b_near, swap(after(b_far, b_near), "b_swap")]
    a_far = along_y(after(a1, b_far), 1, "a_far")
    parts = early(after(where, b_far), activations, out_grad, pm_t, gate_pre, up_pre, ph_t)
    top, low = parts[:256], parts[256:]
    half = jnp.where(c == 0, top, low) + swap(jnp.where(c == 0, low, top), "s_core")
    b_mine = [theirs, b1, b2, b_far]
    h1 = product(BF16, after(where, r4, r5, r6, a_far, half), b_mine, b_other, [own_w, r1, r2, r3])
    r7 = route(r6, "-", "p", "r7")
    h1_in = mate(h1, "mate_grad1")
    h2 = product(BF16, after(where, h1), b_mine, b_other, [r4, r5, r6])
    h2_in = mate(h2, "mate_grad2")
    a_mine = [out_grad, a1, a2, a_far]
    near = jnp.concatenate([out_grad, a2, a1])
    a_other = [swap(after(near, h1), "a_swap"), swap(a_far, "a_swap")]
    near_y = send(half, lambda z, x, y, c: (z, x, y ^ 1, c), "s_near")
    own1 = product(F32, after(where, h2), a_mine, a_other, [own_w, r1, r2, r3, r4, r5, r6])
    half += after(near_y, own1)
    far_y = send(half, lambda z, x, y, c: (z, x, y ^ 2, c), "s_far")
    h3 = product(BF16, after(where, h1_in, own1), b_mine, b_other, [r7])
    own2 = product(F32, after(where, h3), a_mine, a_other, [r7])
    h_in = [h1_in, h2_in, mate(h3, "mate_grad3")]
    grad_gate, grad_up, part = own_half(where, gate_pre, up_pre, (own1, own2), ph_t)
    half += after(far_y, part, h_in[1], h_in[2])
    rest = swap(half, "s_core")
    sums = jnp.concatenate(
        [jnp.where(c == 0, half, rest), jnp.where(c == 0, rest, half)], axis=0
    )
    *spread, down_feat = spread_features(where, sums)
    grad_gate, grad_up, part = other_half(
        where, gate_pre, up_pre, h_in, ph_t, part, grad_gate, grad_up
    )
    feat = features_of(spread, part)
    total = jnp.concatenate([sum_tensor(feat, c), down_feat], axis=1)
    features = total.reshape(4, RANK, 3, RANK).transpose(0, 2, 1, 3).reshape(4, 3, RANK * RANK)
    return grad_gate, grad_up, features


def solution(mesh):
    split = Mesh(mesh.devices.reshape(4, 4, 4, 2), AXES)
    dp, tensor = ("z", "x"), ("y", "c")
    return jax.shard_map(
        on_device,
        mesh=split,
        in_specs=(
            P(dp, tensor),
            P(dp, tensor),
            P(dp, tensor),
            P(dp, tensor),
            P((*tensor, *dp), None),
            P(),
            P(tensor, None),
            P(dp),
        ),
        out_specs=(P(dp, tensor), P(dp, tensor), P(dp, None, None)),
        check_vma=False,
    )
```

```python
import functools

import jax
import jax.numpy as jnp
from jax import lax
from jax.experimental import pallas as pl
from jax.experimental.pallas import tpu as pltpu
from jax.sharding import Mesh
from jax.sharding import PartitionSpec as P

AXES = ("z", "x", "y", "c")
F32, BF16 = jnp.float32, jnp.bfloat16
ROWS, FEAT, HID, HALF, RANK, DEPTH = 512, 640, 1792, 896, 64, 5120
SHARD = 112
TILE = 128
STEP = 2 * FEAT
NT = (((1,), (1,)), ((), ()))
LIGHT = pl.CostEstimate(flops=1 << 20, bytes_accessed=1 << 16, transcendentals=0)
ANY = pl.BlockSpec(memory_space=pl.ANY)


def send(value, target, name="send"):
    def line(z, x, y, c):
        return ((z % 4 * 4 + x % 4) * 4 + y % 4) * 2 + c

    pairs = [
        (line(z, x, y, c), line(*target(z, x, y, c)))
        for z in range(4)
        for x in range(4)
        for y in range(4)
        for c in range(2)
    ]
    with jax.named_scope(name):
        return lax.ppermute(value, AXES, pairs)


def up_y(v, name="up"):
    return send(v, lambda z, x, y, c: (z, x, y + 1, c), name)


def down_y(v, name="down"):
    return send(v, lambda z, x, y, c: (z, x, y - 1, c), name)


def along_y(v, way, name):
    return send(v, lambda z, x, y, c: (z, x, y + way * (1 - 2 * c), c), name)


def swap(v, name="swap"):
    return send(v, lambda z, x, y, c: (z, x, y, 1 - c), name)


def mate(v, name="mate"):
    return send(v, lambda z, x, y, c: (3 - z, x, y, c), name)


def after(value, *others):
    return lax.optimization_barrier((value, *others))[0]


def route(v, zero, one, name):
    hop = {
        "p": lambda z, x, y, c: (z ^ 1, x, y, c),
        "+": lambda z, x, y, c: (z, x + 1, y, c),
        "-": lambda z, x, y, c: (z, x - 1, y, c),
    }
    return send(v, lambda z, x, y, c: hop[zero if c == 0 else one](z, x, y, c), name)


def slots(z, x, c):
    zl, first = z % 2, c == 0

    def at(dz, dx):
        return (zl + dz) % 2 * 4 + (x + dx) % 4

    held = jnp.stack(
        [
            at(0, 0),
            at(0, 3),
            jnp.where(first, at(1, 0), at(0, 1)),
            jnp.where(first, at(0, 1), at(1, 0)),
            jnp.where(first, at(1, 3), at(1, 1)),
            jnp.where(first, at(0, 2), at(1, 3)),
            jnp.where(first, at(1, 1), at(0, 2)),
            at(1, 2),
        ]
    )
    shard = jnp.arange(8)
    return jnp.sum(jnp.where(held[None, :] == shard[:, None], shard[None, :], 0), axis=1)


def product_kernel(shards, where_ref, *refs):
    mine, near, far, weights = refs[:4], refs[4], refs[5], refs[6 : 6 + shards]
    out_ref, *acc = refs[6 + shards :]
    acc = acc[0] if acc else out_ref
    y, c = where_ref[16], where_ref[17]
    for step, shift in enumerate((0, 3 - 2 * c, 1 + 2 * c, 2)):
        first = lax.rem(y + shift, 4) * STEP
        lane, swapped = (pl.multiple_of(first + core * FEAT, 128) for core in (c, 1 - c))
        other = near[step * ROWS : step * ROWS + ROWS, :] if step < 3 else far[...]
        left = jnp.concatenate([mine[step][...], other], axis=1)
        rows = []
        for k, w in enumerate(weights):
            rows.append(
                jnp.concatenate([w[:, pl.ds(lane, FEAT)], w[:, pl.ds(swapped, FEAT)]], axis=1)
            )
            if shards > 1:
                rows.append(jnp.zeros((128 - SHARD, STEP), BF16))
        right = jnp.concatenate(rows, axis=0) if shards > 1 else rows[0]
        part = lax.dot_general(left, right, NT, preferred_element_type=F32)
        if step == 0:
            acc[:, : part.shape[1]] = part
        elif step < 3:
            acc[:, : part.shape[1]] += part
        else:
            out_ref[:, : part.shape[1]] = (acc[:, : part.shape[1]] + part).astype(out_ref.dtype)


def product(dtype, where, mine, other, weights):
    shards = len(weights)
    width = shards * 128
    vmem = pl.BlockSpec(memory_space=pltpu.VMEM)
    return pl.pallas_call(
        functools.partial(product_kernel, shards),
        out_shape=jax.ShapeDtypeStruct((ROWS, width), dtype),
        in_specs=[pl.BlockSpec(memory_space=pltpu.SMEM)] + [vmem] * (6 + shards),
        out_specs=vmem,
        scratch_shapes=[] if dtype == F32 else [pltpu.VMEM((ROWS, width), F32)],
        compiler_params=pltpu.CompilerParams(
            vmem_limit_bytes=(6 << 20) + width * (4 * STEP + 14 * ROWS)
        ),
        cost_estimate=LIGHT,
        name="product",
    )(where, *mine, *other, *weights)


def early_kernel(where_ref, act_ref, grad_ref, pm_ref, gate_ref, up_ref, ph_ref, out_ref):
    gate, up = gate_ref[...].astype(F32), up_ref[...].astype(F32)
    hidden = (gate * jax.nn.sigmoid(gate) * up).astype(BF16)
    pm = pm_ref[...]
    out_ref[:, 0:64] = lax.dot_general(act_ref[...], pm, NT, preferred_element_type=F32)
    out_ref[:, 64:128] = lax.dot_general(hidden, ph_ref[...], NT, preferred_element_type=F32)
    out_ref[:, 128:192] = lax.dot_general(grad_ref[...], pm, NT, preferred_element_type=F32)


def early(where, activations, out_grad, pm_t, gate, up, ph_t):
    narrow = pl.BlockSpec((128, FEAT), lambda i, w: (i, 0))
    wide = pl.BlockSpec((128, HID), lambda i, w: (i, 0))
    return pl.pallas_call(
        early_kernel,
        out_shape=jax.ShapeDtypeStruct((ROWS, 3 * RANK), F32),
        grid_spec=pltpu.PrefetchScalarGridSpec(
            num_scalar_prefetch=1,
            grid=(4,),
            in_specs=[
                narrow,
                narrow,
                pl.BlockSpec((RANK, FEAT), lambda i, w: (0, 2 * w[16] + w[17])),
                wide,
                wide,
                pl.BlockSpec((RANK, HID), lambda i, w: (0, 0)),
            ],
            out_specs=pl.BlockSpec((128, 3 * RANK), lambda i, w: (i, 0)),
        ),
        compiler_params=pltpu.CompilerParams(vmem_limit_bytes=12 << 20),
        cost_estimate=LIGHT,
        name="early",
    )(where, activations, out_grad, pm_t, gate, up, ph_t)


def grads(where_ref, base, h_refs, held, gate_ref, up_ref, ph_ref, gg_ref, gu_ref):
    at = 0
    for h_ref in h_refs:
        width = h_ref.shape[1]
        held[:, at : at + width] = h_ref[...].astype(F32)
        at += width
    hidden_grad = jnp.concatenate(
        [
            held[:, pl.ds(pl.multiple_of(where_ref[base + i] * 128, 128), 128)][:, :SHARD]
            for i in range(8)
        ],
        axis=1,
    )
    row = pl.program_id(0) * TILE + lax.broadcasted_iota(jnp.int32, hidden_grad.shape, 0)
    hidden_grad = jnp.where(row < where_ref[19], hidden_grad, 0.0)
    gate, up = gate_ref[...].astype(F32), up_ref[...].astype(F32)
    sig = jax.nn.sigmoid(gate)
    grad_up = (hidden_grad * (gate * sig)).astype(BF16)
    grad_gate = (hidden_grad * up * sig * (1.0 + gate * (1.0 - sig))).astype(BF16)
    gg_ref[...] = grad_gate
    gu_ref[...] = grad_up
    both = jnp.concatenate([grad_gate, grad_up], axis=0)
    part = lax.dot_general(both, ph_ref[...], NT, preferred_element_type=F32)
    return jnp.concatenate([part[:TILE], part[TILE:]], axis=1)


def own_kernel(n, where_ref, gate_ref, up_ref, ph_ref, *refs):
    gg_ref, gu_ref, part_ref, held = refs[n:]
    part_ref[...] = grads(
        where_ref, 0, refs[:n], held, gate_ref, up_ref, ph_ref, gg_ref, gu_ref
    )


def row_tiles(half):
    tile = pl.BlockSpec((TILE, HALF), lambda i, w: (i, half(w)))
    return tile, pl.BlockSpec((RANK, HALF), lambda i, w: (0, half(w)))


def pieces_of(h):
    return [pl.BlockSpec((TILE, p.shape[1]), lambda i, w: (i, 0)) for p in h]


BIG = jax.ShapeDtypeStruct((ROWS, HID), BF16)


def own_half(where, gate, up, h, ph_t):
    tile, ranks = row_tiles(lambda w: w[18])
    return pl.pallas_call(
        functools.partial(own_kernel, len(h)),
        out_shape=(BIG, BIG, jax.ShapeDtypeStruct((ROWS, 2 * RANK), F32)),
        grid_spec=pltpu.PrefetchScalarGridSpec(
            num_scalar_prefetch=1,
            grid=(ROWS // TILE,),
            in_specs=[tile, tile, ranks] + pieces_of(h),
            out_specs=(tile, tile, pl.BlockSpec((TILE, 2 * RANK), lambda i, w: (i, 0))),
            scratch_shapes=[pltpu.VMEM((TILE, 1024), F32)],
        ),
        compiler_params=pltpu.CompilerParams(vmem_limit_bytes=14 << 20),
        cost_estimate=LIGHT,
        name="own_half",
    )(where, gate, up, ph_t, *h)


def other_kernel(n, where_ref, gate_ref, up_ref, ph_ref, part_ref, gg_in, gu_in, *refs):
    gg_ref, gu_ref, sum_ref, held = refs[n:]
    sum_ref[...] = part_ref[...] + grads(
        where_ref, 8, refs[:n], held, gate_ref, up_ref, ph_ref, gg_ref, gu_ref
    )


def parted(value):
    hi = value.astype(BF16)
    return hi, (value - hi.astype(F32)).astype(BF16)


def twice(hi, lo, right):
    right_hi, right_lo = parted(right)
    total = jnp.dot(lo, right_hi, preferred_element_type=F32)
    total += jnp.dot(hi, right_lo, preferred_element_type=F32)
    return total + jnp.dot(hi, right_hi, preferred_element_type=F32)


def other_half(where, gate, up, h, ph_t, part, gg, gu):
    tile, ranks = row_tiles(lambda w: 1 - w[18])
    narrow = pl.BlockSpec((TILE, 2 * RANK), lambda i, w: (i, 0))
    return pl.pallas_call(
        functools.partial(other_kernel, len(h)),
        out_shape=(BIG, BIG, jax.ShapeDtypeStruct((ROWS, 2 * RANK), F32)),
        grid_spec=pltpu.PrefetchScalarGridSpec(
            num_scalar_prefetch=1,
            grid=(ROWS // TILE,),
            in_specs=[tile, tile, ranks, narrow, ANY, ANY] + pieces_of(h),
            out_specs=(tile, tile, narrow),
            scratch_shapes=[pltpu.VMEM((TILE, 1024), F32)],
        ),
        input_output_aliases={5: 0, 6: 1},
        compiler_params=pltpu.CompilerParams(vmem_limit_bytes=14 << 20),
        cost_estimate=LIGHT,
        name="other_half",
    )(where, gate, up, ph_t, part, gg, gu, *h)


def feature_kernel(hi_ref, lo_ref, right_ref, out_ref):
    out_ref[...] = twice(hi_ref[...], lo_ref[...], right_ref[...])


def features_of(spread, right):
    vmem = pl.BlockSpec(memory_space=pltpu.VMEM)
    return pl.pallas_call(
        feature_kernel,
        out_shape=jax.ShapeDtypeStruct((4 * RANK, 2 * RANK), F32),
        in_specs=[vmem] * 3,
        out_specs=vmem,
        compiler_params=pltpu.CompilerParams(vmem_limit_bytes=4 << 20),
        cost_estimate=LIGHT,
        name="features",
    )(*spread, right)


def spread_kernel(where_ref, sums_ref, hi_ref, lo_ref, feat_ref):
    sums = sums_ref[...]
    left = sums[:, : 2 * RANK].T
    right = sums[:, 2 * RANK :]
    row = lax.broadcasted_iota(jnp.int32, (1, ROWS), 1)
    start = jnp.int32(0)
    for s in range(4):
        length = where_ref[20 + s]
        member = jnp.logical_and(row >= start, row < start + length).astype(F32)
        weight = member / jnp.sqrt(jnp.broadcast_to(length, (1, ROWS)).astype(F32))
        hi, lo = parted(left[:RANK] * weight)
        at = pl.ds(s * RANK, RANK)
        hi_ref[at, :] = hi
        lo_ref[at, :] = lo
        feat_ref[at, :] = twice(*parted(left[RANK:] * weight), right)
        start += length


def spread_features(where, sums):
    vmem = pl.BlockSpec(memory_space=pltpu.VMEM)
    side = jax.ShapeDtypeStruct((4 * RANK, ROWS), BF16)
    return pl.pallas_call(
        spread_kernel,
        out_shape=(side, side, jax.ShapeDtypeStruct((4 * RANK, RANK), F32)),
        in_specs=[pl.BlockSpec(memory_space=pltpu.SMEM), vmem],
        out_specs=(vmem, vmem, vmem),
        compiler_params=pltpu.CompilerParams(vmem_limit_bytes=8 << 20),
        name="spread",
    )(where, sums)


def sum_tensor(value, c):
    half = value.shape[0] // 2
    top, low = value[:half], value[half:]
    mine = jnp.where(c == 0, top, low) + swap(jnp.where(c == 0, low, top))
    across = send(mine, lambda z, x, y, c: (z, x, y + 2, c))
    mine = (mine + across) + (up_y(mine) + down_y(mine))
    theirs = swap(mine)
    return jnp.concatenate(
        [jnp.where(c == 0, mine, theirs), jnp.where(c == 0, theirs, mine)], axis=0
    )


def on_device(
    activations, out_grad, gate_pre, up_pre, down_weight, proj_model, proj_hidden, lengths
):
    z, x, y, c = (lax.axis_index(a) for a in AXES)
    where = jnp.concatenate(
        [
            slots(z, x, c),
            slots(3 - z, x, c),
            jnp.stack([y, c, z // 2, jnp.sum(lengths)]),
            lengths,
        ]
    ).astype(jnp.int32)
    pm_t, ph_t = proj_model.T, proj_hidden.T
    own_w = down_weight
    theirs = mate(out_grad, "mate_rows")
    a1, a2 = along_y(out_grad, 1, "a1"), along_y(out_grad, -1, "a2")
    r1 = route(own_w, "+", "+", "r1")
    r2 = route(own_w, "p", "-", "r2")
    r3 = route(own_w, "-", "p", "r3")
    b1, b2 = along_y(theirs, 1, "b1"), along_y(theirs, -1, "b2")
    r1, r2, r3, b1, b2, a1, a2, where = lax.optimization_barrier(
        (r1, r2, r3, b1, b2, a1, a2, where)
    )
    r6 = route(r2, "-", "-", "r6")
    r4 = route(r2, "+", "p", "r4")
    r5 = route(r1, "+", "p", "r5")
    b_far = along_y(b1, 1, "b_far")
    b_near = swap(jnp.concatenate([theirs, b2, b1]), "b_swap")
    b_other = [b_near, swap(after(b_far, b_near), "b_swap")]
    a_far = along_y(after(a1, b_far), 1, "a_far")
    parts = early(after(where, b_far), activations, out_grad, pm_t, gate_pre, up_pre, ph_t)
    top, low = parts[:256], parts[256:]
    half = jnp.where(c == 0, top, low) + swap(jnp.where(c == 0, low, top), "s_core")
    b_mine = [theirs, b1, b2, b_far]
    h1 = product(BF16, after(where, r4, r5, r6, a_far, half), b_mine, b_other, [own_w, r1, r2, r3])
    r7 = route(r6, "-", "p", "r7")
    h1_in = mate(h1, "mate_grad1")
    h2 = product(BF16, after(where, h1), b_mine, b_other, [r4, r5, r6])
    h2_in = mate(h2, "mate_grad2")
    a_mine = [out_grad, a1, a2, a_far]
    near = jnp.concatenate([out_grad, a2, a1])
    a_other = [swap(after(near, h1), "a_swap"), swap(a_far, "a_swap")]
    near_y = send(half, lambda z, x, y, c: (z, x, y ^ 1, c), "s_near")
    own1 = product(F32, after(where, h2), a_mine, a_other, [own_w, r1, r2, r3, r4, r5, r6])
    half += after(near_y, h2)
    far_y = send(half, lambda z, x, y, c: (z, x, y ^ 2, c), "s_far")
    h3 = product(BF16, after(where, h1_in, own1), b_mine, b_other, [r7])
    own2 = product(F32, after(where, h3), a_mine, a_other, [r7])
    h_in = [h1_in, h2_in, mate(h3, "mate_grad3")]
    grad_gate, grad_up, part = own_half(where, gate_pre, up_pre, (own1, own2), ph_t)
    half = after(half + after(far_y, own1), part, h_in[1], h_in[2])
    rest = swap(half, "s_core")
    sums = jnp.concatenate(
        [jnp.where(c == 0, half, rest), jnp.where(c == 0, rest, half)], axis=0
    )
    *spread, down_feat = spread_features(where, sums)
    grad_gate, grad_up, part = other_half(
        where, gate_pre, up_pre, h_in, ph_t, part, grad_gate, grad_up
    )
    feat = features_of(spread, part)
    total = jnp.concatenate([sum_tensor(feat, c), down_feat], axis=1)
    features = total.reshape(4, RANK, 3, RANK).transpose(0, 2, 1, 3).reshape(4, 3, RANK * RANK)
    return grad_gate, grad_up, features


def solution(mesh):
    split = Mesh(mesh.devices.reshape(4, 4, 4, 2), AXES)
    dp, tensor = ("z", "x"), ("y", "c")
    return jax.shard_map(
        on_device,
        mesh=split,
        in_specs=(
            P(dp, tensor),
            P(dp, tensor),
            P(dp, tensor),
            P(dp, tensor),
            P((*tensor, *dp), None),
            P(),
            P(tensor, None),
            P(dp),
        ),
        out_specs=(P(dp, tensor), P(dp, tensor), P(dp, None, None)),
        check_vma=False,
    )
```
